32 devices in a mesh: fac: 2 (over core), str: 16 (over z, y, x).
Axes of the slice: x: 2, y: 2, z: 4, core: 2. Of those that a mesh axis runs over, the one named last changes fastest.
Arguments:
- vector: bfloat16 [4096, 8192], P('str'), may hold values from -6 to 6
- alpha_tiles: bfloat16 [2, 4, 128, 128], P('fac'), may hold values from -0.25 to 0.25
- alpha_pattern: int32 [2, 32, 4], P('fac'), may hold values from 0 to 31
- beta_tiles: bfloat16 [2, 4, 128, 128], P('fac'), may hold values from -0.25 to 0.25
- beta_pattern: int32 [2, 64, 4], P('fac'), may hold values from 0 to 63
- alpha_sector: int32 [32], replicated, may hold values from 0 to 1
- beta_sector: int32 [64], replicated, may hold values from 0 to 1
- alpha_diag: float32 [4096], replicated, may hold values from 0.5 to 2
- beta_diag: float32 [8192], replicated, may hold values from 0.5 to 2
- energy: float32 [1], replicated, may hold values from -1 to 0
Outputs:
- first_update: bfloat16 [4096, 8192], P('fac', 'str')
- second_update: bfloat16 [4096, 8192], P('str', 'fac')
The draws below stay inside these ranges and needn't reach their ends.
All inputs are finite; a program needn't handle non-finite values.
Results may differ from the reference program's by a relative error of at most 0.0064.
Values may be sent and summed in bfloat16 or wider, within the bound.
A program may use at most 128 MiB of HBM per device.

```python
import jax
import jax.numpy as jnp
from jax import lax

NA = 4096
NB = 8192
BLK = 128
S = 4
K = 2
NAB = 32
NBB = 64


def plant(values, key, smallest, high):
    place = [jax.random.randint(jax.random.fold_in(key, axis), (), 0, length) for axis, length in enumerate(values.shape)]
    widest = values.shape.index(max(values.shape))
    beside = place[:widest] + [(place[widest] + 1) % values.shape[widest]] + place[widest + 1:]
    return values.at[tuple(place)].set(smallest).at[tuple(beside)].set(high)


def steps_of(stream_key, dims, split, smallest, high):
    loudness, own = 1.0, jax.random.fold_in(stream_key, 6)
    for dim, parts in split:
        heights = jnp.exp(jax.random.uniform(jax.random.fold_in(own, dim), (parts,), jnp.float32, smallest / len(split), high / len(split)))
        loudness = loudness * jnp.repeat(heights, dims[dim] // parts).reshape([-1 if axis == dim else 1 for axis in range(len(dims))])
    return loudness


def scatter_about(own_key, shape, width, bound, cuts=(), kind=jnp.bfloat16):
    values = width * jax.random.normal(own_key, shape, jnp.float32)
    if cuts:
        values = values * steps_of(own_key, shape, cuts, -0.22, 0.18)
    return jnp.clip(values, -bound, bound).astype(kind)


def setup_inputs(seed: int = 0) -> dict:
    seeds = jax.random.split(jax.random.key(seed), 11)
    return {
        "vector": scatter_about(seeds[0], (NA, NB), 1.0, 6.0, ((0, 16),)),
        "alpha_tiles": scatter_about(seeds[1], (K, S, BLK, BLK), (BLK * S) ** -0.5, 0.25, ((0, 2),)),
        "alpha_pattern": plant(jax.random.randint(seeds[2], (K, NAB, S), 0, NAB), jax.random.fold_in(seeds[2], 1), 0, NAB - 1).astype(jnp.int32),
        "beta_tiles": scatter_about(seeds[3], (K, S, BLK, BLK), (BLK * S) ** -0.5, 0.25, ((0, 2),)),
        "beta_pattern": plant(jax.random.randint(seeds[4], (K, NBB, S), 0, NBB), jax.random.fold_in(seeds[4], 1), 0, NBB - 1).astype(jnp.int32),
        "alpha_sector": plant(jax.random.randint(seeds[5], (NAB,), 0, 2), jax.random.fold_in(seeds[5], 1), 0, 1).astype(jnp.int32),
        "beta_sector": plant(jax.random.randint(seeds[6], (NBB,), 0, 2), jax.random.fold_in(seeds[6], 1), 0, 1).astype(jnp.int32),
        "alpha_diag": jnp.clip(jax.random.uniform(seeds[7], (NA,), jnp.float32, 0.5, 2.0), 0.5, 2.0),
        "beta_diag": jnp.clip(jax.random.uniform(seeds[8], (NB,), jnp.float32, 0.5, 2.0), 0.5, 2.0),
        "energy": jnp.clip(jax.random.uniform(seeds[9], (1,), jnp.float32, -1.0, 0.0), -1.0, 0.0),
    }


def beta_apply(matrix, tile_set, pattern):
    height = matrix.shape[0]
    blocks = matrix.reshape(height, NBB, BLK).astype(jnp.float32)
    picked = jnp.take(blocks, pattern.reshape(-1), axis=1).reshape(height, NBB, S * BLK)
    stacked = tile_set.astype(jnp.float32).reshape(S * BLK, BLK)
    result = jnp.einsum("rjk,kc->rjc", picked, stacked)
    return result.reshape(height, NBB * BLK)


def alpha_apply(matrix, tile_set, pattern):
    breadth = matrix.shape[1]
    blocks = matrix.reshape(NAB, BLK, breadth).astype(jnp.float32)
    picked = jnp.take(blocks, pattern.reshape(-1), axis=0).reshape(NAB, S * BLK, breadth)
    stacked = tile_set.astype(jnp.float32).transpose(1, 0, 2).reshape(BLK, S * BLK)
    result = jnp.einsum("ak,jkc->jac", stacked, picked)
    return result.reshape(NAB * BLK, breadth)


def reference(vector, alpha_tiles, alpha_pattern, beta_tiles, beta_pattern, alpha_sector, beta_sector, alpha_diag, beta_diag, energy):
    live_mask = (jnp.repeat(alpha_sector, BLK)[:, None] == jnp.repeat(beta_sector, BLK)[None, :]).astype(jnp.float32)
    denominator = alpha_diag[:, None] + beta_diag[None, :] - energy[0]

    def forward(running, inputs):
        image = beta_apply(vector, inputs[2], inputs[3]).astype(jnp.bfloat16)
        return running + alpha_apply(image, inputs[0], inputs[1]), None

    factors = (alpha_tiles, alpha_pattern, beta_tiles, beta_pattern)
    sigma_first, _ = lax.scan(forward, jnp.zeros((NA, NB), jnp.float32), factors)
    first_update = (live_mask * sigma_first / denominator).astype(jnp.bfloat16)

    def backward(running, inputs):
        image = alpha_apply(first_update, inputs[0], inputs[1]).astype(jnp.bfloat16)
        return running + beta_apply(image, inputs[2], inputs[3]), None

    sigma_second, _ = lax.scan(backward, jnp.zeros((NA, NB), jnp.float32), factors)
    second_update = (live_mask * sigma_second / denominator).astype(jnp.bfloat16)
    return first_update, second_update
```

```python
import functools

import jax
import jax.numpy as jnp
from jax import lax
from jax.experimental import pallas as pl
from jax.experimental.pallas import tpu as pltpu
from jax.sharding import PartitionSpec as P

MESH = pl.DeviceIdType.MESH


def beta_apply(matrix, tile_set, pattern):
    height, width = matrix.shape
    slot_count, block_size = tile_set.shape[:2]
    stacked = tile_set.reshape(slot_count * block_size, block_size)

    def one(j, result):
        picked = jnp.concatenate(
            [
                lax.dynamic_slice_in_dim(matrix, pattern[j, s] * block_size, block_size, 1)
                for s in range(slot_count)
            ],
            axis=1,
        )
        image = jnp.dot(picked, stacked, preferred_element_type=jnp.float32)
        return lax.dynamic_update_slice_in_dim(result, image, j * block_size, 1)

    return lax.fori_loop(
        0, width // block_size, one, jnp.zeros((height, width), jnp.float32)
    )


def alpha_apply(matrix, tile_set, pattern):
    height, width = matrix.shape
    slot_count, block_size = tile_set.shape[:2]
    stacked = tile_set.transpose(1, 0, 2).reshape(block_size, slot_count * block_size)

    def one(i, result):
        picked = jnp.concatenate(
            [
                lax.dynamic_slice_in_dim(matrix, pattern[i, s] * block_size, block_size, 0)
                for s in range(slot_count)
            ],
            axis=0,
        )
        image = jnp.dot(stacked, picked, preferred_element_type=jnp.float32)
        return lax.dynamic_update_slice_in_dim(result, image, i * block_size, 0)

    return lax.fori_loop(
        0, height // block_size, one, jnp.zeros((height, width), jnp.float32)
    )


def precondition(
    sigma_part,
    row_start,
    col_start,
    block_size,
    alpha_sector,
    beta_sector,
    alpha_diag,
    beta_diag,
    energy,
):
    row_count, col_count = sigma_part.shape
    row_blocks = row_count // block_size
    col_blocks = col_count // block_size
    alpha_labels = lax.dynamic_slice_in_dim(alpha_sector, row_start // block_size, row_blocks)
    beta_labels = lax.dynamic_slice_in_dim(beta_sector, col_start // block_size, col_blocks)
    live_mask = (alpha_labels[:, None, None, None] == beta_labels[None, None, :, None]).astype(
        jnp.float32
    )
    masked = (
        sigma_part.reshape(row_blocks, block_size, col_blocks, block_size) * live_mask
    ).reshape(row_count, col_count)
    alpha_part = lax.dynamic_slice_in_dim(alpha_diag, row_start, row_count)
    beta_part = lax.dynamic_slice_in_dim(beta_diag, col_start, col_count)
    denominator = alpha_part[:, None] + beta_part[None, :] - energy[0]
    return (masked / denominator).astype(jnp.bfloat16)


def body(
    vector,
    alpha_tiles,
    alpha_pattern,
    beta_tiles,
    beta_pattern,
    alpha_sector,
    beta_sector,
    alpha_diag,
    beta_diag,
    energy,
):
    string_index = lax.axis_index("str")
    group_index = lax.axis_index("fac")
    string_count = lax.axis_size("str")
    block_size = alpha_tiles.shape[2]
    row_count = vector.shape[0]
    col_count = vector.shape[1] // string_count
    factor = 0
    image = beta_apply(vector, beta_tiles[factor], beta_pattern[factor]).astype(jnp.bfloat16)
    moved_one = lax.all_to_all(image, "str", split_axis=1, concat_axis=0, tiled=True)
    partial_value = alpha_apply(moved_one, alpha_tiles[factor], alpha_pattern[factor])
    share_rows = lax.psum_scatter(partial_value, "fac", scatter_dimension=0, tiled=True)
    first_update = precondition(
        share_rows,
        group_index * share_rows.shape[0],
        string_index * col_count,
        block_size,
        alpha_sector,
        beta_sector,
        alpha_diag,
        beta_diag,
        energy,
    )
    whole_first = lax.all_gather(first_update, "fac", axis=0, tiled=True)
    factor = 0
    back_image = alpha_apply(whole_first, alpha_tiles[factor], alpha_pattern[factor]).astype(
        jnp.bfloat16
    )
    returned_one = lax.all_to_all(back_image, "str", split_axis=0, concat_axis=1, tiled=True)
    partial_back = beta_apply(returned_one, beta_tiles[factor], beta_pattern[factor])
    share_cols = lax.psum_scatter(partial_back, "fac", scatter_dimension=1, tiled=True)
    second_update = precondition(
        share_cols,
        string_index * row_count,
        group_index * share_cols.shape[1],
        block_size,
        alpha_sector,
        beta_sector,
        alpha_diag,
        beta_diag,
        energy,
    )
    return (first_update, second_update)


PLANES = 4
HALVES = 2


def exchange_kernel(
    sizes,
    energy,
    vec,
    ta_in,
    tb_in,
    ints_in,
    ad_in,
    bd_in,
    out1,
    out2,
    held,
    ta_all,
    tb_all,
    tiles_row,
    ints,
    adiag,
    bdiag,
    send1,
    recv1,
    first,
    send2,
    recv2,
    staged,
    held_sem,
    early_sem,
    late_sem,
    give_send,
    give_recv,
    send1_sem,
    recv1_sem,
    send2_sem,
    recv2_sem,
    o1_send,
    o1_recv,
    o2_send,
    o2_recv,
):
    n, nf, bs, sc, qc, nab, nbb, length = sizes
    me = lax.axis_index("str")
    c = lax.axis_index("fac")
    everyone = n * nf
    lanes = n // PLANES
    per = lanes * nf
    row_blocks = nab // n
    half_rows = nab // nf
    half_blocks = nbb // nf
    kb = sc * bs
    hb = bs // HALVES
    plane = me // lanes
    lane = lax.rem(me, lanes)

    def target(v):
        step = v // per
        u = lax.rem(v, per)
        high = lax.rem(plane // 2 + 1 - step // 2, 2)
        low = lax.rem(lax.rem(plane, 2) + step + step // 2, 2)
        d = (2 * high + low) * lanes + lax.rem(lane + u // nf, lanes)
        return d, lax.rem(c + lax.rem(u, nf), nf)

    own = 3 * per

    def partner(t):
        return t + t // own

    barrier = pltpu.get_barrier_semaphore()

    def greet(t, carry):
        d, f = target(partner(t))
        pl.semaphore_signal(
            barrier, inc=1, device_id={"fac": f, "str": d}, device_id_type=MESH
        )
        return carry

    lax.fori_loop(0, everyone - 1, greet, 0)

    def load(b, carry):
        columns = pl.ds(pl.multiple_of(b * bs, bs), bs)
        pltpu.make_async_copy(vec.at[:, columns], held.at[b], held_sem).start()
        return carry

    own_kb = pl.ds(pl.multiple_of(c * kb, kb), kb)
    own_ints = pl.ds(pl.multiple_of(c * length, length), length)
    early = [
        pltpu.make_async_copy(tb_in, tb_all.at[own_kb], early_sem.at[0]),
        pltpu.make_async_copy(ints_in, ints.at[own_ints], early_sem.at[1]),
    ]
    late = [
        pltpu.make_async_copy(ta_in, ta_all.at[own_kb], late_sem.at[0]),
        pltpu.make_async_copy(ad_in, adiag, late_sem.at[1]),
        pltpu.make_async_copy(bd_in, bdiag, late_sem.at[2]),
    ]
    for copy in early:
        copy.start()
    lax.fori_loop(0, nbb, load, 0)
    for copy in late:
        copy.start()

    def gives():
        for e in range(1, nf):
            f = lax.rem(c + e, nf)
            for x, (a, b) in enumerate(
                [
                    (tb_in, tb_all.at[own_kb]),
                    (ta_in, ta_all.at[own_kb]),
                    (ints_in, ints.at[own_ints]),
                ]
            ):
                yield pltpu.make_async_remote_copy(
                    src_ref=a,
                    dst_ref=b,
                    send_sem=give_send.at[e - 1, x],
                    recv_sem=give_recv.at[e - 1, x],
                    device_id={"fac": f, "str": me},
                    device_id_type=MESH,
                )

    def a_index(k, i, s):
        return ints[k * length + i * sc + s]

    def b_index(k, j, s):
        return ints[k * length + nab * sc + j * sc + s]

    def sector_a(i):
        return ints[(nab + nbb) * sc + i]

    def sector_b(j):
        return ints[(nab + nbb) * sc + nab + j]

    def column(ref, index):
        return jnp.transpose(jnp.broadcast_to(ref[pl.ds(index, 1), :], (bs, bs)))

    def alive(i, j):
        return jnp.where(sector_a(i) == sector_b(j), 1.0, 0.0).astype(jnp.float32)

    def beta_image(q, v, dst):
        d, f = target(v)
        j = (d * nf + f) * qc + q
        picked = jnp.concatenate([held[b_index(c, j, s)] for s in range(sc)], axis=1)
        image = jnp.dot(picked, tb_all[own_kb, :], preferred_element_type=jnp.float32)
        for x in range(row_blocks):
            dst[x] = image[x * bs : (x + 1) * bs].astype(jnp.bfloat16)

    def first_copy(q, t):
        v = partner(t)
        d, f = target(v)
        return pltpu.make_async_remote_copy(
            src_ref=send1[q].at[v],
            dst_ref=recv1[q].at[pl.ds(c * nab + me * row_blocks, row_blocks)],
            send_sem=send1_sem.at[q],
            recv_sem=recv1_sem.at[q],
            device_id={"fac": f, "str": d},
            device_id_type=MESH,
        )

    pltpu.make_async_copy(held, held, held_sem).wait()
    for copy in early:
        copy.wait()
    beta_image(0, 0, send1[0].at[0])
    pl.semaphore_wait(barrier, everyone - 1)
    for copy in gives():
        copy.start()

    for q in range(qc):
        if q > 0:
            beta_image(q, 0, send1[q].at[0])

        def step_one(t, carry, q=q):
            v = partner(t)
            beta_image(q, v, send1[q].at[v])
            first_copy(q, t - 1).start()
            return carry

        lax.fori_loop(1, everyone - 1, step_one, 0)
        first_copy(q, everyone - 2).start()
        beta_image(q, own, recv1[q].at[pl.ds(c * nab + me * row_blocks, row_blocks)])

    for copy in late:
        copy.wait()
    for copy in gives():
        copy.wait()
    for x in range(nf * sc):
        tiles_row[:, x * bs : (x + 1) * bs] = ta_all[x * bs : (x + 1) * bs, :]

    def second_copy(q, h, t):
        v = partner(t)
        d, f = target(v)
        return pltpu.make_async_remote_copy(
            src_ref=send2[q].at[h, v],
            dst_ref=recv2[h].at[(me * nf + c) * qc + q],
            send_sem=send2_sem.at[q, h],
            recv_sem=recv2_sem.at[h],
            device_id={"fac": f, "str": d},
            device_id_type=MESH,
        )

    def share_copy(q, e):
        f = lax.rem(c + e, nf)
        src = first[q].at[pl.ds(f * half_rows, half_rows)]
        dst = out1.at[:, :, pl.ds(pl.multiple_of((c * qc + q) * bs, bs), bs)]
        if e == 0:
            return pltpu.make_async_copy(src, dst, o1_send.at[q, e])
        return pltpu.make_async_remote_copy(
            src_ref=src,
            dst_ref=dst,
            send_sem=o1_send.at[q, e],
            recv_sem=o1_recv.at[q, e],
            device_id={"fac": f, "str": me},
            device_id_type=MESH,
        )

    for q in range(qc):
        landed = recv1[q].at[pl.ds(0, (everyone - 1) * row_blocks)]
        pltpu.make_async_copy(landed, landed, recv1_sem.at[q]).wait()
        j = (me * nf + c) * qc + q

        def sigma_one(i, carry, q=q, j=j):
            parts = [
                recv1[q][k * nab + a_index(k, i, s)] for k in range(nf) for s in range(sc)
            ]
            sigma = jnp.dot(
                tiles_row[...], jnp.concatenate(parts, axis=0), preferred_element_type=jnp.float32
            )
            denominator = column(adiag, i) + bdiag[pl.ds(j, 1), :] - energy[0]
            first[q][i] = (sigma * alive(i, j) / denominator).astype(jnp.bfloat16)
            return carry

        lax.fori_loop(0, nab, sigma_one, 0)

        def alpha_image(v, store, q=q):
            d, f = target(v)
            i = d * nf + f
            for k in range(nf):
                picked = jnp.concatenate(
                    [first[q][a_index(k, i, s)] for s in range(sc)], axis=0
                )
                image = jnp.dot(
                    tiles_row[:, k * kb : (k + 1) * kb],
                    picked,
                    preferred_element_type=jnp.float32,
                ).astype(jnp.bfloat16)
                for h in range(HALVES):
                    store(h, k, image[h * hb : (h + 1) * hb])

        def step_two(t, carry, q=q, alpha_image=alpha_image):
            v = partner(t)

            def store(h, k, value):
                send2[q][h, v, k] = value

            alpha_image(v, store)

            @pl.when(t > 0)
            def _():
                second_copy(q, 0, t - 1).start()

            return carry

        lax.fori_loop(0, everyone - 1, step_two, 0)
        second_copy(q, 0, everyone - 2).start()

        def keep(h, k, value, j=j):
            recv2[h][j, k] = value

        alpha_image(own, keep)
        for e in range(nf):
            share_copy(q, e).start()

    for h in range(1, HALVES):
        for q in range(qc):

            def rest(t, carry, q=q, h=h):
                second_copy(q, h, t).start()
                return carry

            lax.fori_loop(0, everyone - 1, rest, 0)

    mine = me * nf + c
    group = max(g for g in (1, 2, 4, 8) if half_blocks % g == 0)
    pieces = half_blocks // group

    def sigma_two(h, first_block):
        rows = []
        for g in range(group):
            parts = [
                recv2[h][b_index(k, first_block + g, s), k]
                for k in range(nf)
                for s in range(sc)
            ]
            rows.append(jnp.concatenate(parts, axis=1))
        sigma = jnp.dot(
            jnp.concatenate(rows, axis=0), tb_all[...], preferred_element_type=jnp.float32
        )
        alpha_part = column(adiag, mine)[h * hb : (h + 1) * hb]
        for g in range(group):
            j = first_block + g
            denominator = alpha_part + bdiag[pl.ds(j, 1), :] - energy[0]
            value = sigma[g * hb : (g + 1) * hb] * alive(mine, j) / denominator
            staged[h * hb : (h + 1) * hb, pl.ds(pl.multiple_of(j * bs, bs), bs)] = value.astype(
                jnp.bfloat16
            )

    def piece_copy(h, e, x):
        f = lax.rem(c + e, nf)
        src_start = pl.multiple_of((f * half_blocks + x * group) * bs, bs)
        dst_start = pl.multiple_of(x * group * bs, bs)
        src = staged.at[pl.ds(h * hb, hb), pl.ds(src_start, group * bs)]
        dst = out2.at[
            pl.ds(pl.multiple_of(c * bs + h * hb, hb), hb), pl.ds(dst_start, group * bs)
        ]
        if e == 0:
            return pltpu.make_async_copy(src, dst, o2_send.at[e])
        return pltpu.make_async_remote_copy(
            src_ref=src,
            dst_ref=dst,
            send_sem=o2_send.at[e],
            recv_sem=o2_recv.at[e],
            device_id={"fac": f, "str": me},
            device_id_type=MESH,
        )

    for h in range(HALVES):
        landed = recv2[h].at[pl.ds(0, (everyone - 1) * qc)]
        pltpu.make_async_copy(landed, landed, recv2_sem.at[h]).wait()
        for e in reversed(range(nf)):

            def finish(x, carry, e=e, h=h):
                sigma_two(h, lax.rem(c + e, nf) * half_blocks + x * group)
                piece_copy(h, e, x).start()
                return carry

            lax.fori_loop(0, pieces, finish, 0)

    for q in range(qc):
        sent = send1[q].at[pl.ds(0, everyone - 1)]
        pltpu.make_async_copy(sent, sent, send1_sem.at[q]).wait()
        for h in range(HALVES):
            sent = send2[q].at[h, pl.ds(0, everyone - 1)]
            pltpu.make_async_copy(sent, sent, send2_sem.at[q, h]).wait()
        for e in range(nf):
            share_copy(q, e).wait()
    for e in range(nf):
        sent = staged.at[:, pl.ds(0, half_blocks * bs)]
        pltpu.make_async_copy(sent, sent, o2_send.at[e]).wait()
        if e > 0:
            pltpu.make_async_copy(sent, sent, o2_recv.at[e]).wait()


def split_body(
    vector,
    alpha_tiles,
    alpha_pattern,
    beta_tiles,
    beta_pattern,
    alpha_sector,
    beta_sector,
    alpha_diag,
    beta_diag,
    energy,
):
    n = lax.axis_size("str")
    nf = lax.axis_size("fac")
    sc, bs = alpha_tiles.shape[1], alpha_tiles.shape[2]
    nab, nbb = alpha_sector.shape[0], beta_sector.shape[0]
    qc = nbb // (n * nf)
    rows = vector.shape[0]
    numbers = jnp.concatenate(
        [alpha_pattern.reshape(-1), beta_pattern.reshape(-1), alpha_sector, beta_sector]
    )
    length = -(-numbers.shape[0] // 1024) * 1024
    numbers = jnp.pad(numbers, (0, length - numbers.shape[0]))
    smem = pl.BlockSpec(memory_space=pltpu.SMEM)
    anywhere = pl.BlockSpec(memory_space=pl.ANY)
    bf16 = jnp.bfloat16
    everyone = n * nf
    row_blocks = nab // n
    dma = pltpu.SemaphoreType.DMA
    first_update, second_update = pl.pallas_call(
        functools.partial(exchange_kernel, (n, nf, bs, sc, qc, nab, nbb, length)),
        out_shape=(
            jax.ShapeDtypeStruct((nab // nf, bs, nbb * bs // n), bf16),
            jax.ShapeDtypeStruct((rows, nbb * bs // nf), bf16),
        ),
        in_specs=[smem] + [anywhere] * 6,
        out_specs=(anywhere, anywhere),
        scratch_shapes=[
            pltpu.VMEM((nbb, rows, bs), bf16),
            pltpu.VMEM((nf * sc * bs, bs), bf16),
            pltpu.VMEM((nf * sc * bs, bs), bf16),
            pltpu.VMEM((bs, nf * sc * bs), bf16),
            pltpu.SMEM((nf * length,), jnp.int32),
            pltpu.VMEM((nab, bs), jnp.float32),
            pltpu.VMEM((nbb, bs), jnp.float32),
            [pltpu.VMEM((everyone, row_blocks, bs, bs), bf16) for _ in range(qc)],
            [pltpu.VMEM((nf * nab, bs, bs), bf16) for _ in range(qc)],
            [pltpu.VMEM((nab, bs, bs), bf16) for _ in range(qc)],
            [pltpu.VMEM((HALVES, everyone, nf, bs // HALVES, bs), bf16) for _ in range(qc)],
            [pltpu.VMEM((nbb, nf, bs // HALVES, bs), bf16) for _ in range(HALVES)],
            pltpu.VMEM((bs, nbb * bs), bf16),
            dma,
            dma((2,)),
            dma((3,)),
            dma((nf - 1, 3)),
            dma((nf - 1, 3)),
            dma((qc,)),
            dma((qc,)),
            dma((qc, HALVES)),
            dma((HALVES,)),
            dma((qc, nf)),
            dma((qc, nf)),
            dma((nf,)),
            dma((nf,)),
        ],
        compiler_params=pltpu.CompilerParams(
            collective_id=0, has_side_effects=True, vmem_limit_bytes=40 * 1024 * 1024
        ),
    )(
        energy,
        vector,
        alpha_tiles.reshape(sc * bs, bs),
        beta_tiles.reshape(sc * bs, bs),
        numbers,
        alpha_diag.reshape(nab, bs),
        beta_diag.reshape(nbb, bs),
    )
    return first_update.reshape(nab * bs // nf, nbb * bs // n), second_update


def fits_split(*args):
    vector, alpha_tiles, _, _, _, alpha_sector, beta_sector = args[:7]
    n, nf = lax.axis_size("str"), lax.axis_size("fac")
    bs = alpha_tiles.shape[2]
    nab, nbb = alpha_sector.shape[0], beta_sector.shape[0]
    return (
        n % PLANES == 0
        and nf > 1
        and alpha_tiles.shape[0] == 1
        and bs % 128 == 0
        and nab == n * nf
        and nbb % (n * nf) == 0
    )


def either_body(*args):
    return split_body(*args) if fits_split(*args) else body(*args)


def solution(mesh):
    return jax.shard_map(
        either_body,
        mesh=mesh,
        in_specs=(
            P("str", None),
            P("fac", None, None, None),
            P("fac", None, None),
            P("fac", None, None, None),
            P("fac", None, None),
            P(),
            P(),
            P(),
            P(),
            P(),
        ),
        out_specs=(P("fac", "str"), P("str", "fac")),
        check_vma=False,
    )
```

```python
import functools

import jax
import jax.numpy as jnp
from jax import lax
from jax.experimental import pallas as pl
from jax.experimental.pallas import tpu as pltpu
from jax.sharding import PartitionSpec as P

MESH = pl.DeviceIdType.MESH


def beta_apply(matrix, tile_set, pattern):
    height, width = matrix.shape
    slot_count, block_size = tile_set.shape[:2]
    stacked = tile_set.reshape(slot_count * block_size, block_size)

    def one(j, result):
        picked = jnp.concatenate(
            [
                lax.dynamic_slice_in_dim(matrix, pattern[j, s] * block_size, block_size, 1)
                for s in range(slot_count)
            ],
            axis=1,
        )
        image = jnp.dot(picked, stacked, preferred_element_type=jnp.float32)
        return lax.dynamic_update_slice_in_dim(result, image, j * block_size, 1)

    return lax.fori_loop(
        0, width // block_size, one, jnp.zeros((height, width), jnp.float32)
    )


def alpha_apply(matrix, tile_set, pattern):
    height, width = matrix.shape
    slot_count, block_size = tile_set.shape[:2]
    stacked = tile_set.transpose(1, 0, 2).reshape(block_size, slot_count * block_size)

    def one(i, result):
        picked = jnp.concatenate(
            [
                lax.dynamic_slice_in_dim(matrix, pattern[i, s] * block_size, block_size, 0)
                for s in range(slot_count)
            ],
            axis=0,
        )
        image = jnp.dot(stacked, picked, preferred_element_type=jnp.float32)
        return lax.dynamic_update_slice_in_dim(result, image, i * block_size, 0)

    return lax.fori_loop(
        0, height // block_size, one, jnp.zeros((height, width), jnp.float32)
    )


def precondition(
    sigma_part,
    row_start,
    col_start,
    block_size,
    alpha_sector,
    beta_sector,
    alpha_diag,
    beta_diag,
    energy,
):
    row_count, col_count = sigma_part.shape
    row_blocks = row_count // block_size
    col_blocks = col_count // block_size
    alpha_labels = lax.dynamic_slice_in_dim(alpha_sector, row_start // block_size, row_blocks)
    beta_labels = lax.dynamic_slice_in_dim(beta_sector, col_start // block_size, col_blocks)
    live_mask = (alpha_labels[:, None, None, None] == beta_labels[None, None, :, None]).astype(
        jnp.float32
    )
    masked = (
        sigma_part.reshape(row_blocks, block_size, col_blocks, block_size) * live_mask
    ).reshape(row_count, col_count)
    alpha_part = lax.dynamic_slice_in_dim(alpha_diag, row_start, row_count)
    beta_part = lax.dynamic_slice_in_dim(beta_diag, col_start, col_count)
    denominator = alpha_part[:, None] + beta_part[None, :] - energy[0]
    return (masked / denominator).astype(jnp.bfloat16)


def body(
    vector,
    alpha_tiles,
    alpha_pattern,
    beta_tiles,
    beta_pattern,
    alpha_sector,
    beta_sector,
    alpha_diag,
    beta_diag,
    energy,
):
    string_index = lax.axis_index("str")
    group_index = lax.axis_index("fac")
    string_count = lax.axis_size("str")
    block_size = alpha_tiles.shape[2]
    row_count = vector.shape[0]
    col_count = vector.shape[1] // string_count
    factor = 0
    image = beta_apply(vector, beta_tiles[factor], beta_pattern[factor]).astype(jnp.bfloat16)
    moved_one = lax.all_to_all(image, "str", split_axis=1, concat_axis=0, tiled=True)
    partial_value = alpha_apply(moved_one, alpha_tiles[factor], alpha_pattern[factor])
    share_rows = lax.psum_scatter(partial_value, "fac", scatter_dimension=0, tiled=True)
    first_update = precondition(
        share_rows,
        group_index * share_rows.shape[0],
        string_index * col_count,
        block_size,
        alpha_sector,
        beta_sector,
        alpha_diag,
        beta_diag,
        energy,
    )
    whole_first = lax.all_gather(first_update, "fac", axis=0, tiled=True)
    factor = 0
    back_image = alpha_apply(whole_first, alpha_tiles[factor], alpha_pattern[factor]).astype(
        jnp.bfloat16
    )
    returned_one = lax.all_to_all(back_image, "str", split_axis=0, concat_axis=1, tiled=True)
    partial_back = beta_apply(returned_one, beta_tiles[factor], beta_pattern[factor])
    share_cols = lax.psum_scatter(partial_back, "fac", scatter_dimension=1, tiled=True)
    second_update = precondition(
        share_cols,
        string_index * row_count,
        group_index * share_cols.shape[1],
        block_size,
        alpha_sector,
        beta_sector,
        alpha_diag,
        beta_diag,
        energy,
    )
    return (first_update, second_update)


PLANES = 4
HALVES = 2


def exchange_kernel(
    sizes,
    energy,
    vec,
    ta_in,
    tb_in,
    pa_in,
    pb_in,
    sa_in,
    sb_in,
    ad_in,
    bd_in,
    out1,
    out2,
    held,
    ta_all,
    tb_all,
    tiles_row,
    pa,
    pb,
    sa,
    sb,
    adiag,
    bdiag,
    send1,
    recv1,
    first,
    send2,
    recv2,
    staged,
    held_sem,
    early_sem,
    late_sem,
    give_send,
    give_recv,
    send1_sem,
    recv1_sem,
    send2_sem,
    recv2_sem,
    o1_send,
    o1_recv,
    o2_send,
    o2_recv,
):
    n, nf, bs, sc, qc, nab, nbb = sizes
    me = lax.axis_index("str")
    c = lax.axis_index("fac")
    everyone = n * nf
    lanes = n // PLANES
    per = lanes * nf
    row_blocks = nab // n
    half_rows = nab // nf
    half_blocks = nbb // nf
    kb = sc * bs
    hb = bs // HALVES
    plane = me // lanes
    lane = lax.rem(me, lanes)

    def target(v):
        step = v // per
        u = lax.rem(v, per)
        high = lax.rem(plane // 2 + 1 - step // 2, 2)
        low = lax.rem(lax.rem(plane, 2) + step + step // 2, 2)
        d = (2 * high + low) * lanes + lax.rem(lane + u // nf, lanes)
        return d, lax.rem(c + lax.rem(u, nf), nf)

    own = 3 * per

    def partner(t):
        return t + t // own

    barrier = pltpu.get_barrier_semaphore()

    def greet(t, carry):
        d, f = target(partner(t))
        pl.semaphore_signal(
            barrier, inc=1, device_id={"fac": f, "str": d}, device_id_type=MESH
        )
        return carry

    lax.fori_loop(0, everyone - 1, greet, 0)

    def load(b, carry):
        columns = pl.ds(pl.multiple_of(b * bs, bs), bs)
        pltpu.make_async_copy(vec.at[:, columns], held.at[b], held_sem).start()
        return carry

    own_kb = pl.ds(pl.multiple_of(c * kb, kb), kb)
    early = [
        pltpu.make_async_copy(tb_in, tb_all.at[own_kb], early_sem.at[0]),
        pltpu.make_async_copy(pb_in, pb.at[c], early_sem.at[1]),
    ]
    late = [
        pltpu.make_async_copy(ta_in, ta_all.at[own_kb], late_sem.at[0]),
        pltpu.make_async_copy(ad_in, adiag, late_sem.at[1]),
        pltpu.make_async_copy(bd_in, bdiag, late_sem.at[2]),
        pltpu.make_async_copy(pa_in, pa.at[c], late_sem.at[3]),
        pltpu.make_async_copy(sa_in, sa, late_sem.at[4]),
        pltpu.make_async_copy(sb_in, sb, late_sem.at[5]),
    ]
    for copy in early:
        copy.start()
    lax.fori_loop(0, nbb, load, 0)
    for copy in late:
        copy.start()

    def gives():
        for e in range(1, nf):
            f = lax.rem(c + e, nf)
            for x, (a, b) in enumerate(
                [
                    (tb_in, tb_all.at[own_kb]),
                    (ta_in, ta_all.at[own_kb]),
                    (pb_in, pb.at[c]),
                    (pa_in, pa.at[c]),
                ]
            ):
                yield pltpu.make_async_remote_copy(
                    src_ref=a,
                    dst_ref=b,
                    send_sem=give_send.at[e - 1, x],
                    recv_sem=give_recv.at[e - 1, x],
                    device_id={"fac": f, "str": me},
                    device_id_type=MESH,
                )

    def a_index(k, i, s):
        return pa[k, s, i]

    def b_index(k, j, s):
        return pb[k, s, j]

    def column(ref, index):
        return jnp.transpose(jnp.broadcast_to(ref[pl.ds(index, 1), :], (bs, bs)))

    def alive(i, j):
        return jnp.where(sa[i] == sb[j], 1.0, 0.0).astype(jnp.float32)

    def beta_image(q, v, dst):
        d, f = target(v)
        j = (d * nf + f) * qc + q
        picked = jnp.concatenate([held[b_index(c, j, s)] for s in range(sc)], axis=1)
        image = jnp.dot(picked, tb_all[own_kb, :], preferred_element_type=jnp.float32)
        for x in range(row_blocks):
            dst[x] = image[x * bs : (x + 1) * bs].astype(jnp.bfloat16)

    def first_copy(q, t):
        v = partner(t)
        d, f = target(v)
        return pltpu.make_async_remote_copy(
            src_ref=send1[q].at[v],
            dst_ref=recv1[q].at[pl.ds(c * nab + me * row_blocks, row_blocks)],
            send_sem=send1_sem.at[q],
            recv_sem=recv1_sem.at[q],
            device_id={"fac": f, "str": d},
            device_id_type=MESH,
        )

    pltpu.make_async_copy(held, held, held_sem).wait()
    for copy in early:
        copy.wait()
    beta_image(0, 0, send1[0].at[0])
    pl.semaphore_wait(barrier, everyone - 1)
    for copy in gives():
        copy.start()

    for q in range(qc):
        if q > 0:
            beta_image(q, 0, send1[q].at[0])

        def step_one(t, carry, q=q):
            v = partner(t)
            beta_image(q, v, send1[q].at[v])
            first_copy(q, t - 1).start()
            return carry

        lax.fori_loop(1, everyone - 1, step_one, 0)
        first_copy(q, everyone - 2).start()
        beta_image(q, own, recv1[q].at[pl.ds(c * nab + me * row_blocks, row_blocks)])

    for copy in late:
        copy.wait()
    for copy in gives():
        copy.wait()
    for x in range(nf * sc):
        tiles_row[:, x * bs : (x + 1) * bs] = ta_all[x * bs : (x + 1) * bs, :]

    def second_copy(q, h, t):
        v = partner(t)
        d, f = target(v)
        return pltpu.make_async_remote_copy(
            src_ref=send2[q].at[h, v],
            dst_ref=recv2[h].at[(me * nf + c) * qc + q],
            send_sem=send2_sem.at[q, h],
            recv_sem=recv2_sem.at[h],
            device_id={"fac": f, "str": d},
            device_id_type=MESH,
        )

    def share_copy(q, e):
        f = lax.rem(c + e, nf)
        src = first[q].at[pl.ds(f * half_rows, half_rows)]
        dst = out1.at[:, :, pl.ds(pl.multiple_of((c * qc + q) * bs, bs), bs)]
        if e == 0:
            return pltpu.make_async_copy(src, dst, o1_send.at[q, e])
        return pltpu.make_async_remote_copy(
            src_ref=src,
            dst_ref=dst,
            send_sem=o1_send.at[q, e],
            recv_sem=o1_recv.at[q, e],
            device_id={"fac": f, "str": me},
            device_id_type=MESH,
        )

    for q in range(qc):
        landed = recv1[q].at[pl.ds(0, (everyone - 1) * row_blocks)]
        pltpu.make_async_copy(landed, landed, recv1_sem.at[q]).wait()
        j = (me * nf + c) * qc + q

        def sigma_one(i, carry, q=q, j=j):
            parts = [
                recv1[q][k * nab + a_index(k, i, s)] for k in range(nf) for s in range(sc)
            ]
            sigma = jnp.dot(
                tiles_row[...], jnp.concatenate(parts, axis=0), preferred_element_type=jnp.float32
            )
            denominator = column(adiag, i) + bdiag[pl.ds(j, 1), :] - energy[0]
            first[q][i] = (sigma * alive(i, j) / denominator).astype(jnp.bfloat16)
            return carry

        lax.fori_loop(0, nab, sigma_one, 0)

        def alpha_image(v, store, q=q):
            d, f = target(v)
            i = d * nf + f
            for k in range(nf):
                picked = jnp.concatenate(
                    [first[q][a_index(k, i, s)] for s in range(sc)], axis=0
                )
                image = jnp.dot(
                    tiles_row[:, k * kb : (k + 1) * kb],
                    picked,
                    preferred_element_type=jnp.float32,
                ).astype(jnp.bfloat16)
                for h in range(HALVES):
                    store(h, k, image[h * hb : (h + 1) * hb])

        def step_two(t, carry, q=q, alpha_image=alpha_image):
            v = partner(t)

            def store(h, k, value):
                send2[q][h, v, k] = value

            alpha_image(v, store)

            @pl.when(t > 0)
            def _():
                second_copy(q, 0, t - 1).start()

            return carry

        lax.fori_loop(0, everyone - 1, step_two, 0)
        second_copy(q, 0, everyone - 2).start()

        def keep(h, k, value, j=j):
            recv2[h][j, k] = value

        alpha_image(own, keep)
        for e in range(nf):
            share_copy(q, e).start()

    for h in range(1, HALVES):
        for q in range(qc):

            def rest(t, carry, q=q, h=h):
                second_copy(q, h, t).start()
                return carry

            lax.fori_loop(0, everyone - 1, rest, 0)

    mine = me * nf + c
    group = max(g for g in (1, 2, 4, 8) if half_blocks % g == 0)
    pieces = half_blocks // group

    def sigma_two(h, first_block):
        rows = []
        for g in range(group):
            parts = [
                recv2[h][b_index(k, first_block + g, s), k]
                for k in range(nf)
                for s in range(sc)
            ]
            rows.append(jnp.concatenate(parts, axis=1))
        sigma = jnp.dot(
            jnp.concatenate(rows, axis=0), tb_all[...], preferred_element_type=jnp.float32
        )
        alpha_part = column(adiag, mine)[h * hb : (h + 1) * hb]
        for g in range(group):
            j = first_block + g
            denominator = alpha_part + bdiag[pl.ds(j, 1), :] - energy[0]
            value = sigma[g * hb : (g + 1) * hb] * alive(mine, j) / denominator
            staged[h * hb : (h + 1) * hb, pl.ds(pl.multiple_of(j * bs, bs), bs)] = value.astype(
                jnp.bfloat16
            )

    def piece_copy(h, e, x):
        f = lax.rem(c + e, nf)
        src_start = pl.multiple_of((f * half_blocks + x * group) * bs, bs)
        dst_start = pl.multiple_of(x * group * bs, bs)
        src = staged.at[pl.ds(h * hb, hb), pl.ds(src_start, group * bs)]
        dst = out2.at[
            pl.ds(pl.multiple_of(c * bs + h * hb, hb), hb), pl.ds(dst_start, group * bs)
        ]
        if e == 0:
            return pltpu.make_async_copy(src, dst, o2_send.at[e])
        return pltpu.make_async_remote_copy(
            src_ref=src,
            dst_ref=dst,
            send_sem=o2_send.at[e],
            recv_sem=o2_recv.at[e],
            device_id={"fac": f, "str": me},
            device_id_type=MESH,
        )

    for h in range(HALVES):
        landed = recv2[h].at[pl.ds(0, (everyone - 1) * qc)]
        pltpu.make_async_copy(landed, landed, recv2_sem.at[h]).wait()
        for e in reversed(range(nf)):

            def finish(x, carry, e=e, h=h):
                sigma_two(h, lax.rem(c + e, nf) * half_blocks + x * group)
                piece_copy(h, e, x).start()
                return carry

            lax.fori_loop(0, pieces, finish, 0)

    for q in range(qc):
        sent = send1[q].at[pl.ds(0, everyone - 1)]
        pltpu.make_async_copy(sent, sent, send1_sem.at[q]).wait()
        for h in range(HALVES):
            sent = send2[q].at[h, pl.ds(0, everyone - 1)]
            pltpu.make_async_copy(sent, sent, send2_sem.at[q, h]).wait()
        for e in range(nf):
            share_copy(q, e).wait()
    for e in range(nf):
        sent = staged.at[:, pl.ds(0, half_blocks * bs)]
        pltpu.make_async_copy(sent, sent, o2_send.at[e]).wait()
        if e > 0:
            pltpu.make_async_copy(sent, sent, o2_recv.at[e]).wait()


def split_body(
    vector,
    alpha_tiles,
    alpha_pattern,
    beta_tiles,
    beta_pattern,
    alpha_sector,
    beta_sector,
    alpha_diag,
    beta_diag,
    energy,
):
    n = lax.axis_size("str")
    nf = lax.axis_size("fac")
    sc, bs = alpha_tiles.shape[1], alpha_tiles.shape[2]
    nab, nbb = alpha_sector.shape[0], beta_sector.shape[0]
    qc = nbb // (n * nf)
    rows = vector.shape[0]
    smem = pl.BlockSpec(memory_space=pltpu.SMEM)
    anywhere = pl.BlockSpec(memory_space=pl.ANY)
    hbm = pl.BlockSpec(memory_space=pltpu.HBM)
    bf16 = jnp.bfloat16
    everyone = n * nf
    row_blocks = nab // n
    dma = pltpu.SemaphoreType.DMA
    first_update, second_update = pl.pallas_call(
        functools.partial(exchange_kernel, (n, nf, bs, sc, qc, nab, nbb)),
        out_shape=(
            jax.ShapeDtypeStruct((nab // nf, bs, nbb * bs // n), bf16),
            jax.ShapeDtypeStruct((rows, nbb * bs // nf), bf16),
        ),
        in_specs=[smem] + [hbm] * 9,
        out_specs=(anywhere, anywhere),
        scratch_shapes=[
            pltpu.VMEM((nbb, rows, bs), bf16),
            pltpu.VMEM((nf * sc * bs, bs), bf16),
            pltpu.VMEM((nf * sc * bs, bs), bf16),
            pltpu.VMEM((bs, nf * sc * bs), bf16),
            pltpu.SMEM((nf, sc, nab), jnp.int32),
            pltpu.SMEM((nf, sc, nbb), jnp.int32),
            pltpu.SMEM((nab,), jnp.int32),
            pltpu.SMEM((nbb,), jnp.int32),
            pltpu.VMEM((nab, bs), jnp.float32),
            pltpu.VMEM((nbb, bs), jnp.float32),
            [pltpu.VMEM((everyone, row_blocks, bs, bs), bf16) for _ in range(qc)],
            [pltpu.VMEM((nf * nab, bs, bs), bf16) for _ in range(qc)],
            [pltpu.VMEM((nab, bs, bs), bf16) for _ in range(qc)],
            [pltpu.VMEM((HALVES, everyone, nf, bs // HALVES, bs), bf16) for _ in range(qc)],
            [pltpu.VMEM((nbb, nf, bs // HALVES, bs), bf16) for _ in range(HALVES)],
            pltpu.VMEM((bs, nbb * bs), bf16),
            dma,
            dma((2,)),
            dma((6,)),
            dma((nf - 1, 4)),
            dma((nf - 1, 4)),
            dma((qc,)),
            dma((qc,)),
            dma((qc, HALVES)),
            dma((HALVES,)),
            dma((qc, nf)),
            dma((qc, nf)),
            dma((nf,)),
            dma((nf,)),
        ],
        compiler_params=pltpu.CompilerParams(
            collective_id=0, has_side_effects=True, vmem_limit_bytes=61 * 1024 * 1024
        ),
    )(
        energy,
        vector,
        alpha_tiles.reshape(sc * bs, bs),
        beta_tiles.reshape(sc * bs, bs),
        alpha_pattern[0].T,
        beta_pattern[0].T,
        alpha_sector,
        beta_sector,
        alpha_diag.reshape(nab, bs),
        beta_diag.reshape(nbb, bs),
    )
    return first_update.reshape(nab * bs // nf, nbb * bs // n), second_update


def fits_split(*args):
    vector, alpha_tiles, _, _, _, alpha_sector, beta_sector = args[:7]
    n, nf = lax.axis_size("str"), lax.axis_size("fac")
    bs = alpha_tiles.shape[2]
    nab, nbb = alpha_sector.shape[0], beta_sector.shape[0]
    return (
        n % PLANES == 0
        and nf > 1
        and alpha_tiles.shape[0] == 1
        and bs % 128 == 0
        and nab == n * nf
        and nbb % (n * nf) == 0
    )


def either_body(*args):
    return split_body(*args) if fits_split(*args) else body(*args)


def solution(mesh):
    return jax.shard_map(
        either_body,
        mesh=mesh,
        in_specs=(
            P("str", None),
            P("fac", None, None, None),
            P("fac", None, None),
            P("fac", None, None, None),
            P("fac", None, None),
            P(),
            P(),
            P(),
            P(),
            P(),
        ),
        out_specs=(P("fac", "str"), P("str", "fac")),
        check_vma=False,
    )
```

```python
import functools

import jax
import jax.numpy as jnp
from jax import lax
from jax.experimental import pallas as pl
from jax.experimental.pallas import tpu as pltpu
from jax.sharding import PartitionSpec as P

MESH = pl.DeviceIdType.MESH


def beta_apply(matrix, tile_set, pattern):
    height, width = matrix.shape
    slot_count, block_size = tile_set.shape[:2]
    stacked = tile_set.reshape(slot_count * block_size, block_size)

    def one(j, result):
        picked = jnp.concatenate(
            [
                lax.dynamic_slice_in_dim(matrix, pattern[j, s] * block_size, block_size, 1)
                for s in range(slot_count)
            ],
            axis=1,
        )
        image = jnp.dot(picked, stacked, preferred_element_type=jnp.float32)
        return lax.dynamic_update_slice_in_dim(result, image, j * block_size, 1)

    return lax.fori_loop(
        0, width // block_size, one, jnp.zeros((height, width), jnp.float32)
    )


def alpha_apply(matrix, tile_set, pattern):
    height, width = matrix.shape
    slot_count, block_size = tile_set.shape[:2]
    stacked = tile_set.transpose(1, 0, 2).reshape(block_size, slot_count * block_size)

    def one(i, result):
        picked = jnp.concatenate(
            [
                lax.dynamic_slice_in_dim(matrix, pattern[i, s] * block_size, block_size, 0)
                for s in range(slot_count)
            ],
            axis=0,
        )
        image = jnp.dot(stacked, picked, preferred_element_type=jnp.float32)
        return lax.dynamic_update_slice_in_dim(result, image, i * block_size, 0)

    return lax.fori_loop(
        0, height // block_size, one, jnp.zeros((height, width), jnp.float32)
    )


def precondition(
    sigma_part,
    row_start,
    col_start,
    block_size,
    alpha_sector,
    beta_sector,
    alpha_diag,
    beta_diag,
    energy,
):
    row_count, col_count = sigma_part.shape
    row_blocks = row_count // block_size
    col_blocks = col_count // block_size
    alpha_labels = lax.dynamic_slice_in_dim(alpha_sector, row_start // block_size, row_blocks)
    beta_labels = lax.dynamic_slice_in_dim(beta_sector, col_start // block_size, col_blocks)
    live_mask = (alpha_labels[:, None, None, None] == beta_labels[None, None, :, None]).astype(
        jnp.float32
    )
    masked = (
        sigma_part.reshape(row_blocks, block_size, col_blocks, block_size) * live_mask
    ).reshape(row_count, col_count)
    alpha_part = lax.dynamic_slice_in_dim(alpha_diag, row_start, row_count)
    beta_part = lax.dynamic_slice_in_dim(beta_diag, col_start, col_count)
    denominator = alpha_part[:, None] + beta_part[None, :] - energy[0]
    return (masked / denominator).astype(jnp.bfloat16)


def body(
    vector,
    alpha_tiles,
    alpha_pattern,
    beta_tiles,
    beta_pattern,
    alpha_sector,
    beta_sector,
    alpha_diag,
    beta_diag,
    energy,
):
    string_index = lax.axis_index("str")
    group_index = lax.axis_index("fac")
    string_count = lax.axis_size("str")
    block_size = alpha_tiles.shape[2]
    row_count = vector.shape[0]
    col_count = vector.shape[1] // string_count
    factor = 0
    image = beta_apply(vector, beta_tiles[factor], beta_pattern[factor]).astype(jnp.bfloat16)
    moved_one = lax.all_to_all(image, "str", split_axis=1, concat_axis=0, tiled=True)
    partial_value = alpha_apply(moved_one, alpha_tiles[factor], alpha_pattern[factor])
    share_rows = lax.psum_scatter(partial_value, "fac", scatter_dimension=0, tiled=True)
    first_update = precondition(
        share_rows,
        group_index * share_rows.shape[0],
        string_index * col_count,
        block_size,
        alpha_sector,
        beta_sector,
        alpha_diag,
        beta_diag,
        energy,
    )
    whole_first = lax.all_gather(first_update, "fac", axis=0, tiled=True)
    factor = 0
    back_image = alpha_apply(whole_first, alpha_tiles[factor], alpha_pattern[factor]).astype(
        jnp.bfloat16
    )
    returned_one = lax.all_to_all(back_image, "str", split_axis=0, concat_axis=1, tiled=True)
    partial_back = beta_apply(returned_one, beta_tiles[factor], beta_pattern[factor])
    share_cols = lax.psum_scatter(partial_back, "fac", scatter_dimension=1, tiled=True)
    second_update = precondition(
        share_cols,
        string_index * row_count,
        group_index * share_cols.shape[1],
        block_size,
        alpha_sector,
        beta_sector,
        alpha_diag,
        beta_diag,
        energy,
    )
    return (first_update, second_update)


PLANES = 4
HALVES = 2


def row_chunks(bs):
    shares = (3, 3, 1, 1)
    unit = bs // sum(shares)
    starts = [unit * sum(shares[:x]) for x in range(len(shares))]
    return [(start, unit * share) for start, share in zip(starts, shares)]


def exchange_kernel(
    sizes,
    energy,
    vec,
    ta_in,
    tb_in,
    pa_in,
    pb_in,
    sa_in,
    sb_in,
    ad_in,
    bd_in,
    out1,
    out2,
    held,
    far,
    ta_all,
    tb_all,
    tiles_row,
    pa,
    pb,
    sa,
    sb,
    adiag,
    bdiag,
    send1,
    send_far,
    recv1,
    first,
    send2,
    recv2,
    staged,
    held_sem,
    early_sem,
    late_sem,
    give_send,
    give_recv,
    raw_send,
    raw_recv,
    send1_sem,
    far_sem,
    recv1_sem,
    send2_sem,
    recv2_sem,
    o1_send,
    o1_recv,
    o2_send,
    o2_recv,
):
    n, nf, bs, sc, qc, nab, nbb = sizes
    slots = qc + 1
    me = lax.axis_index("str")
    c = lax.axis_index("fac")
    everyone = n * nf
    lanes = n // PLANES
    per = lanes * nf
    row_blocks = nab // n
    plane_blocks = lanes * row_blocks
    half_rows = nab // nf
    half_blocks = nbb // nf
    kb = sc * bs
    hb = bs // HALVES
    plane = me // lanes
    lane = lax.rem(me, lanes)
    side = plane // 2
    inner = lax.rem(plane, 2) != side
    near = 2 * per
    near_count = 2 * per - 1
    own = 3 * per
    chunks = row_chunks(bs)

    def target(v):
        step = v // per
        u = lax.rem(v, per)
        high = lax.rem(side + 1 - step // 2, 2)
        low = lax.rem(lax.rem(plane, 2) + step + step // 2, 2)
        d = (2 * high + low) * lanes + lax.rem(lane + u // nf, lanes)
        return d, lax.rem(c + lax.rem(u, nf), nf)

    def partner(t):
        return t + t // own

    def near_partner(t):
        return near + t + t // per

    def column_of(d, f, q):
        if q < qc:
            return (d * nf + f) * qc + q
        mirror = (PLANES - 1 - d // lanes) * lanes + lax.rem(d, lanes)
        return (mirror * nf + f) * qc

    barrier = pltpu.get_barrier_semaphore()

    def greet(t, carry):
        d, f = target(partner(t))
        pl.semaphore_signal(
            barrier, inc=1, device_id={"fac": f, "str": d}, device_id_type=MESH
        )
        return carry

    lax.fori_loop(0, everyone - 1, greet, 0)

    def block(index):
        return pl.ds(pl.multiple_of(index * bs, bs), bs)

    own_kb = pl.ds(pl.multiple_of(c * kb, kb), kb)
    early = [
        pltpu.make_async_copy(tb_in, tb_all.at[own_kb], early_sem.at[0]),
        pltpu.make_async_copy(pb_in, pb.at[c], early_sem.at[1]),
    ]
    late = [
        pltpu.make_async_copy(ta_in, ta_all.at[own_kb], late_sem.at[0]),
        pltpu.make_async_copy(ad_in, adiag, late_sem.at[1]),
        pltpu.make_async_copy(bd_in, bdiag, late_sem.at[2]),
        pltpu.make_async_copy(pa_in, pa.at[c], late_sem.at[3]),
        pltpu.make_async_copy(sa_in, sa, late_sem.at[4]),
        pltpu.make_async_copy(sb_in, sb, late_sem.at[5]),
    ]
    for copy in early:
        copy.start()

    def load(b, carry):
        pltpu.make_async_copy(vec.at[:, block(b)], held.at[b], held_sem).start()
        return carry

    lax.fori_loop(0, nbb, load, 0)
    for copy in late:
        copy.start()

    def gives():
        for e in range(1, nf):
            f = lax.rem(c + e, nf)
            for x, (a, b) in enumerate(
                [
                    (tb_in, tb_all.at[own_kb]),
                    (ta_in, ta_all.at[own_kb]),
                    (pb_in, pb.at[c]),
                    (pa_in, pa.at[c]),
                ]
            ):
                yield pltpu.make_async_remote_copy(
                    src_ref=a,
                    dst_ref=b,
                    send_sem=give_send.at[e - 1, x],
                    recv_sem=give_recv.at[e - 1, x],
                    device_id={"fac": f, "str": me},
                    device_id_type=MESH,
                )

    def raw_copy(x):
        start, rows = chunks[x]
        return pltpu.make_async_remote_copy(
            src_ref=held.at[:, pl.ds(pl.multiple_of(c * bs + start, 16), rows)],
            dst_ref=far[x].at[:, lax.rem(plane, 2)],
            send_sem=raw_send.at[x],
            recv_sem=raw_recv.at[x],
            device_id={"fac": c, "str": (2 - side) * lanes + lane},
            device_id_type=MESH,
        )

    def column(ref, index):
        return jnp.transpose(jnp.broadcast_to(ref[pl.ds(index, 1), :], (bs, bs)))

    def alive(i, j):
        return jnp.where(sa[i] == sb[j], 1.0, 0.0).astype(jnp.float32)

    def beta_image(q, v, store):
        d, f = target(v)
        j = column_of(d, f, q)
        picked = jnp.concatenate([held[pb[c, s, j]] for s in range(sc)], axis=1)
        image = jnp.dot(picked, tb_all[own_kb, :], preferred_element_type=jnp.float32)
        for x in range(row_blocks):
            store(x, image[x * bs : (x + 1) * bs].astype(jnp.bfloat16))

    def stored_out(q, v):
        def store(x, value):
            send1[q][v - near, x] = value

        return store

    def stored_here(q):
        def store(x, value):
            recv1[q][plane * nf + c, lane * row_blocks + x] = value

        return store

    def first_copy(q, v):
        d, f = target(v)
        return pltpu.make_async_remote_copy(
            src_ref=send1[q].at[v - near],
            dst_ref=recv1[q].at[plane * nf + c, pl.ds(lane * row_blocks, row_blocks)],
            send_sem=send1_sem.at[q],
            recv_sem=recv1_sem.at[q],
            device_id={"fac": f, "str": d},
            device_id_type=MESH,
        )

    pltpu.make_async_copy(held, held, held_sem).wait()
    for copy in early:
        copy.wait()
    beta_image(0, near, stored_out(0, near))
    pl.semaphore_wait(barrier, everyone - 1)
    raw_copy(0).start()
    for copy in gives():
        copy.start()

    for q in range(qc):
        if q > 0:
            beta_image(q, near, stored_out(q, near))

        def step_one(t, carry, q=q):
            v = near_partner(t)
            beta_image(q, v, stored_out(q, v))
            first_copy(q, near_partner(t - 1)).start()
            return carry

        lax.fori_loop(1, near_count, step_one, 0)
        first_copy(q, near_partner(near_count - 1)).start()
        beta_image(q, own, stored_here(q))
        raw_copy(q + 1).start()

    extra_base = jnp.where(inner, own, near)
    extra_start = jnp.where(inner, 1, 0)

    def step_extra(t, carry):
        v = extra_base + t
        beta_image(qc, v, stored_out(qc, v))
        first_copy(qc, v).start()
        return carry

    lax.fori_loop(extra_start, per, step_extra, 0)

    @pl.when(inner)
    def _():
        beta_image(qc, own, stored_here(qc))

    for x in range(qc + 1, len(chunks)):
        raw_copy(x).start()

    for copy in late:
        copy.wait()
    for copy in gives():
        copy.wait()
    for x in range(nf * sc):
        tiles_row[:, x * bs : (x + 1) * bs] = ta_all[x * bs : (x + 1) * bs, :]

    def far_image(x, v, qs, store):
        rows = chunks[x][1]
        d, f = target(v)
        for k in range(nf):
            picked = []
            for q in qs:
                j = column_of(d, f, q)
                picked.append(
                    jnp.concatenate(
                        [
                            far[x][pb[k, s, j]].reshape(2 * rows, bs)
                            for s in range(sc)
                        ],
                        axis=1,
                    )
                )
            image = jnp.dot(
                jnp.concatenate(picked, axis=0),
                tb_all[k * kb : (k + 1) * kb, :],
                preferred_element_type=jnp.float32,
            ).astype(jnp.bfloat16)
            for y, q in enumerate(qs):
                for z in range(2):
                    at = (2 * y + z) * rows
                    store(q, z * nf + k, image[at : at + rows])

    def far_out(x, v):
        start, rows = chunks[x]

        def store(q, b, value):
            send_far[((v - near) * slots + q) * 2 * nf + b, start : start + rows] = value

        return store

    def far_here(x):
        start, rows = chunks[x]

        def store(q, b, value):
            at = 2 * (1 - side) * nf + b
            recv1[q][at, lane * row_blocks + c, start : start + rows] = value

        return store

    def far_copy(x, v, q):
        start, rows = chunks[x]
        d, f = target(v)
        return pltpu.make_async_remote_copy(
            src_ref=send_far.at[
                pl.ds(((v - near) * slots + q) * 2 * nf, 2 * nf), pl.ds(start, rows)
            ],
            dst_ref=recv1[q].at[
                pl.ds(2 * (1 - side) * nf, 2 * nf),
                lane * row_blocks + c,
                pl.ds(start, rows),
            ],
            send_sem=far_sem.at[x],
            recv_sem=recv1_sem.at[q],
            device_id={"fac": f, "str": d},
            device_id_type=MESH,
        )

    @pl.when(inner)
    def _():
        for x in range(len(chunks)):
            pltpu.make_async_copy(far[x], far[x], raw_recv.at[x]).wait()

            def far_step(t, carry, x=x):
                v = near_partner(t)
                far_image(x, v, tuple(range(qc)), far_out(x, v))
                for q in range(qc):
                    far_copy(x, v, q).start()
                return carry

            def far_extra(t, carry, x=x):
                v = own + t
                far_image(x, v, (qc,), far_out(x, v))
                far_copy(x, v, qc).start()
                return carry

            lax.fori_loop(0, near_count, far_step, 0)
            lax.fori_loop(1, per, far_extra, 0)
            far_image(x, own, tuple(range(slots)), far_here(x))

    def blocks_wait(count, sem):
        some = send_far.at[pl.ds(0, count)]
        pltpu.make_async_copy(some, some, sem).wait()

    def second_copy(q, h, t):
        v = partner(t)
        d, f = target(v)
        return pltpu.make_async_remote_copy(
            src_ref=send2[q].at[h, v],
            dst_ref=recv2[h].at[column_of(me, c, q)],
            send_sem=send2_sem.at[q, h],
            recv_sem=recv2_sem.at[h],
            device_id={"fac": f, "str": d},
            device_id_type=MESH,
        )

    def share_copy(q, e):
        f = lax.rem(c + e, nf)
        src = first[q].at[pl.ds(f * half_rows, half_rows)]
        dst = out1.at[:, :, pl.ds(pl.multiple_of((c * qc + q) * bs, bs), bs)]
        if e == 0:
            return pltpu.make_async_copy(src, dst, o1_send.at[q, e])
        return pltpu.make_async_remote_copy(
            src_ref=src,
            dst_ref=dst,
            send_sem=o1_send.at[q, e],
            recv_sem=o1_recv.at[q, e],
            device_id={"fac": f, "str": me},
            device_id_type=MESH,
        )

    def begin(q):
        return jnp.where(inner, near, 0) if q == 0 else near if q == qc else 0

    def correct(q):
        j = column_of(me, c, q)

        def sigma_one(i, carry):
            parts = []
            for k in range(nf):
                for s in range(sc):
                    p = pa[k, s, i]
                    parts.append(
                        recv1[q][lax.div(p, plane_blocks) * nf + k, lax.rem(p, plane_blocks)]
                    )
            sigma = jnp.dot(
                tiles_row[...], jnp.concatenate(parts, axis=0), preferred_element_type=jnp.float32
            )
            denominator = column(adiag, i) + bdiag[pl.ds(j, 1), :] - energy[0]
            first[q][i] = (sigma * alive(i, j) / denominator).astype(jnp.bfloat16)
            return carry

        lax.fori_loop(0, nab, sigma_one, 0)

        def alpha_image(v, store):
            d, f = target(v)
            i = d * nf + f
            for k in range(nf):
                picked = jnp.concatenate([first[q][pa[k, s, i]] for s in range(sc)], axis=0)
                image = jnp.dot(
                    tiles_row[:, k * kb : (k + 1) * kb],
                    picked,
                    preferred_element_type=jnp.float32,
                ).astype(jnp.bfloat16)
                for h in range(HALVES):
                    store(h, k, image[h * hb : (h + 1) * hb])

        start = begin(q)

        def step_two(t, carry):
            v = partner(t)

            def store(h, k, value):
                send2[q][h, v, k] = value

            alpha_image(v, store)

            @pl.when(t > start)
            def _():
                second_copy(q, 0, t - 1).start()

            return carry

        lax.fori_loop(start, everyone - 1, step_two, 0)
        second_copy(q, 0, everyone - 2).start()

        def keep(h, k, value):
            recv2[h][j, k] = value

        alpha_image(own, keep)

    order = [1, 0] + list(range(2, qc)) if qc > 1 else [0]
    here = 2 * nf
    for q in order:

        @pl.when(inner)
        def _(q=q):
            blocks_wait(nf * nab - row_blocks - here, recv1_sem.at[q])

        @pl.when(jnp.logical_not(inner))
        def _(q=q):
            blocks_wait(nf * nab - row_blocks, recv1_sem.at[q])

        correct(q)
        for e in range(nf):
            share_copy(q, e).start()

    @pl.when(inner)
    def _():
        blocks_wait(nf * nab - row_blocks - here, recv1_sem.at[qc])
        correct(qc)

    def send_rest(q, h):
        def rest(t, carry):
            second_copy(q, h, t).start()
            return carry

        lax.fori_loop(begin(q), everyone - 1, rest, 0)

    for h in range(1, HALVES):
        for q in order:
            send_rest(q, h)

        @pl.when(inner)
        def _(h=h):
            send_rest(qc, h)

    mine = me * nf + c
    group = max(g for g in (1, 2, 4, 8) if half_blocks % g == 0)
    pieces = half_blocks // group

    def sigma_two(h, first_block):
        rows = []
        for g in range(group):
            parts = [
                recv2[h][pb[k, s, first_block + g], k] for k in range(nf) for s in range(sc)
            ]
            rows.append(jnp.concatenate(parts, axis=1))
        sigma = jnp.dot(
            jnp.concatenate(rows, axis=0), tb_all[...], preferred_element_type=jnp.float32
        )
        alpha_part = column(adiag, mine)[h * hb : (h + 1) * hb]
        for g in range(group):
            j = first_block + g
            denominator = alpha_part + bdiag[pl.ds(j, 1), :] - energy[0]
            value = sigma[g * hb : (g + 1) * hb] * alive(mine, j) / denominator
            staged[h * hb : (h + 1) * hb, block(j)] = value.astype(jnp.bfloat16)

    def piece_copy(h, e, x):
        f = lax.rem(c + e, nf)
        src_start = pl.multiple_of((f * half_blocks + x * group) * bs, bs)
        dst_start = pl.multiple_of(x * group * bs, bs)
        src = staged.at[pl.ds(h * hb, hb), pl.ds(src_start, group * bs)]
        dst = out2.at[
            pl.ds(pl.multiple_of(c * bs + h * hb, hb), hb), pl.ds(dst_start, group * bs)
        ]
        if e == 0:
            return pltpu.make_async_copy(src, dst, o2_send.at[e])
        return pltpu.make_async_remote_copy(
            src_ref=src,
            dst_ref=dst,
            send_sem=o2_send.at[e],
            recv_sem=o2_recv.at[e],
            device_id={"fac": f, "str": me},
            device_id_type=MESH,
        )

    for h in range(HALVES):

        def second_wait(count, h=h):
            some = recv2[h].at[pl.ds(0, count)]
            pltpu.make_async_copy(some, some, recv2_sem.at[h]).wait()

        @pl.when(inner)
        def _(second_wait=second_wait):
            second_wait(nbb - slots)

        @pl.when(jnp.logical_not(inner))
        def _(second_wait=second_wait):
            second_wait(nbb - qc)

        for e in reversed(range(nf)):

            def finish(x, carry, e=e, h=h):
                sigma_two(h, lax.rem(c + e, nf) * half_blocks + x * group)
                piece_copy(h, e, x).start()
                return carry

            lax.fori_loop(0, pieces, finish, 0)

    def second_sent(q, h, count):
        sent = send2[q].at[h, pl.ds(0, count)]
        pltpu.make_async_copy(sent, sent, send2_sem.at[q, h]).wait()

    for q in range(qc):
        blocks_wait(near_count * row_blocks, send1_sem.at[q])
        for e in range(nf):
            share_copy(q, e).wait()
    for x, (start, rows) in enumerate(chunks):
        raw_copy(x).wait_send()

    @pl.when(inner)
    def _():
        blocks_wait((per - 1) * row_blocks, send1_sem.at[qc])
        for x, (start, rows) in enumerate(chunks):
            messages = near_count * qc + per - 1
            some = send_far.at[pl.ds(0, messages * 2 * nf), pl.ds(start, rows)]
            pltpu.make_async_copy(some, some, far_sem.at[x]).wait()
        for h in range(HALVES):
            for q in range(slots):
                second_sent(q, h, near_count if q in (0, qc) else everyone - 1)

    @pl.when(jnp.logical_not(inner))
    def _():
        blocks_wait(per * row_blocks, send1_sem.at[qc])
        for h in range(HALVES):
            for q in range(qc):
                second_sent(q, h, everyone - 1)

    for e in range(nf):
        sent = staged.at[:, pl.ds(0, half_blocks * bs)]
        pltpu.make_async_copy(sent, sent, o2_send.at[e]).wait()
        if e > 0:
            pltpu.make_async_copy(sent, sent, o2_recv.at[e]).wait()


def split_body(
    vector,
    alpha_tiles,
    alpha_pattern,
    beta_tiles,
    beta_pattern,
    alpha_sector,
    beta_sector,
    alpha_diag,
    beta_diag,
    energy,
):
    n = lax.axis_size("str")
    nf = lax.axis_size("fac")
    sc, bs = alpha_tiles.shape[1], alpha_tiles.shape[2]
    nab, nbb = alpha_sector.shape[0], beta_sector.shape[0]
    qc = nbb // (n * nf)
    slots = qc + 1
    rows = vector.shape[0]
    smem = pl.BlockSpec(memory_space=pltpu.SMEM)
    anywhere = pl.BlockSpec(memory_space=pl.ANY)
    hbm = pl.BlockSpec(memory_space=pltpu.HBM)
    bf16 = jnp.bfloat16
    everyone = n * nf
    row_blocks = nab // n
    near = everyone // 2
    hb = bs // HALVES
    chunks = row_chunks(bs)
    dma = pltpu.SemaphoreType.DMA
    first_update, second_update = pl.pallas_call(
        functools.partial(exchange_kernel, (n, nf, bs, sc, qc, nab, nbb)),
        out_shape=(
            jax.ShapeDtypeStruct((nab // nf, bs, nbb * bs // n), bf16),
            jax.ShapeDtypeStruct((rows, nbb * bs // nf), bf16),
        ),
        in_specs=[smem] + [hbm] * 9,
        out_specs=(anywhere, anywhere),
        scratch_shapes=[
            pltpu.VMEM((nbb, rows, bs), bf16),
            [pltpu.VMEM((nbb, 2, count, bs), bf16) for _, count in chunks],
            pltpu.VMEM((nf * sc * bs, bs), bf16),
            pltpu.VMEM((nf * sc * bs, bs), bf16),
            pltpu.VMEM((bs, nf * sc * bs), bf16),
            pltpu.SMEM((nf, sc, nab), jnp.int32),
            pltpu.SMEM((nf, sc, nbb), jnp.int32),
            pltpu.SMEM((nab,), jnp.int32),
            pltpu.SMEM((nbb,), jnp.int32),
            pltpu.VMEM((nab, bs), jnp.float32),
            pltpu.VMEM((nbb, bs), jnp.float32),
            [pltpu.VMEM((near, row_blocks, bs, bs), bf16) for _ in range(slots)],
            pltpu.VMEM((near * slots * 2 * nf, bs, bs), bf16),
            [
                pltpu.VMEM((PLANES * nf, nab // PLANES, bs, bs), bf16)
                for _ in range(slots)
            ],
            [pltpu.VMEM((nab, bs, bs), bf16) for _ in range(slots)],
            [pltpu.VMEM((HALVES, everyone, nf, hb, bs), bf16) for _ in range(slots)],
            [pltpu.VMEM((nbb, nf, hb, bs), bf16) for _ in range(HALVES)],
            pltpu.VMEM((bs, nbb * bs), bf16),
            dma,
            dma((2,)),
            dma((6,)),
            dma((nf - 1, 4)),
            dma((nf - 1, 4)),
            dma((len(chunks),)),
            dma((len(chunks),)),
            dma((slots,)),
            dma((len(chunks),)),
            dma((slots,)),
            dma((slots, HALVES)),
            dma((HALVES,)),
            dma((qc, nf)),
            dma((qc, nf)),
            dma((nf,)),
            dma((nf,)),
        ],
        compiler_params=pltpu.CompilerParams(
            collective_id=0, has_side_effects=True, vmem_limit_bytes=61 * 1024 * 1024
        ),
    )(
        energy,
        vector,
        alpha_tiles.reshape(sc * bs, bs),
        beta_tiles.reshape(sc * bs, bs),
        alpha_pattern[0].T,
        beta_pattern[0].T,
        alpha_sector,
        beta_sector,
        alpha_diag.reshape(nab, bs),
        beta_diag.reshape(nbb, bs),
    )
    return first_update.reshape(nab * bs // nf, nbb * bs // n), second_update


def fits_split(*args):
    vector, alpha_tiles, _, _, _, alpha_sector, beta_sector = args[:7]
    n, nf = lax.axis_size("str"), lax.axis_size("fac")
    bs = alpha_tiles.shape[2]
    nab, nbb = alpha_sector.shape[0], beta_sector.shape[0]
    return (
        n % PLANES == 0
        and nf > 1
        and alpha_tiles.shape[0] == 1
        and bs % 128 == 0
        and nab == n * nf
        and nbb == 2 * n * nf
    )


def either_body(*args):
    return split_body(*args) if fits_split(*args) else body(*args)


def solution(mesh):
    return jax.shard_map(
        either_body,
        mesh=mesh,
        in_specs=(
            P("str", None),
            P("fac", None, None, None),
            P("fac", None, None),
            P("fac", None, None, None),
            P("fac", None, None),
            P(),
            P(),
            P(),
            P(),
            P(),
        ),
        out_specs=(P("fac", "str"), P("str", "fac")),
        check_vma=False,
    )
```

```python
import functools

import jax
import jax.numpy as jnp
from jax import lax
from jax.experimental import pallas as pl
from jax.experimental.pallas import tpu as pltpu
from jax.sharding import PartitionSpec as P

MESH = pl.DeviceIdType.MESH


def beta_apply(matrix, tile_set, pattern):
    height, width = matrix.shape
    slot_count, block_size = tile_set.shape[:2]
    stacked = tile_set.reshape(slot_count * block_size, block_size)

    def one(j, result):
        picked = jnp.concatenate(
            [
                lax.dynamic_slice_in_dim(matrix, pattern[j, s] * block_size, block_size, 1)
                for s in range(slot_count)
            ],
            axis=1,
        )
        image = jnp.dot(picked, stacked, preferred_element_type=jnp.float32)
        return lax.dynamic_update_slice_in_dim(result, image, j * block_size, 1)

    return lax.fori_loop(
        0, width // block_size, one, jnp.zeros((height, width), jnp.float32)
    )


def alpha_apply(matrix, tile_set, pattern):
    height, width = matrix.shape
    slot_count, block_size = tile_set.shape[:2]
    stacked = tile_set.transpose(1, 0, 2).reshape(block_size, slot_count * block_size)

    def one(i, result):
        picked = jnp.concatenate(
            [
                lax.dynamic_slice_in_dim(matrix, pattern[i, s] * block_size, block_size, 0)
                for s in range(slot_count)
            ],
            axis=0,
        )
        image = jnp.dot(stacked, picked, preferred_element_type=jnp.float32)
        return lax.dynamic_update_slice_in_dim(result, image, i * block_size, 0)

    return lax.fori_loop(
        0, height // block_size, one, jnp.zeros((height, width), jnp.float32)
    )


def precondition(
    sigma_part,
    row_start,
    col_start,
    block_size,
    alpha_sector,
    beta_sector,
    alpha_diag,
    beta_diag,
    energy,
):
    row_count, col_count = sigma_part.shape
    row_blocks = row_count // block_size
    col_blocks = col_count // block_size
    alpha_labels = lax.dynamic_slice_in_dim(alpha_sector, row_start // block_size, row_blocks)
    beta_labels = lax.dynamic_slice_in_dim(beta_sector, col_start // block_size, col_blocks)
    live_mask = (alpha_labels[:, None, None, None] == beta_labels[None, None, :, None]).astype(
        jnp.float32
    )
    masked = (
        sigma_part.reshape(row_blocks, block_size, col_blocks, block_size) * live_mask
    ).reshape(row_count, col_count)
    alpha_part = lax.dynamic_slice_in_dim(alpha_diag, row_start, row_count)
    beta_part = lax.dynamic_slice_in_dim(beta_diag, col_start, col_count)
    denominator = alpha_part[:, None] + beta_part[None, :] - energy[0]
    return (masked / denominator).astype(jnp.bfloat16)


def body(
    vector,
    alpha_tiles,
    alpha_pattern,
    beta_tiles,
    beta_pattern,
    alpha_sector,
    beta_sector,
    alpha_diag,
    beta_diag,
    energy,
):
    string_index = lax.axis_index("str")
    group_index = lax.axis_index("fac")
    string_count = lax.axis_size("str")
    block_size = alpha_tiles.shape[2]
    row_count = vector.shape[0]
    col_count = vector.shape[1] // string_count
    factor = 0
    image = beta_apply(vector, beta_tiles[factor], beta_pattern[factor]).astype(jnp.bfloat16)
    moved_one = lax.all_to_all(image, "str", split_axis=1, concat_axis=0, tiled=True)
    partial_value = alpha_apply(moved_one, alpha_tiles[factor], alpha_pattern[factor])
    share_rows = lax.psum_scatter(partial_value, "fac", scatter_dimension=0, tiled=True)
    first_update = precondition(
        share_rows,
        group_index * share_rows.shape[0],
        string_index * col_count,
        block_size,
        alpha_sector,
        beta_sector,
        alpha_diag,
        beta_diag,
        energy,
    )
    whole_first = lax.all_gather(first_update, "fac", axis=0, tiled=True)
    factor = 0
    back_image = alpha_apply(whole_first, alpha_tiles[factor], alpha_pattern[factor]).astype(
        jnp.bfloat16
    )
    returned_one = lax.all_to_all(back_image, "str", split_axis=0, concat_axis=1, tiled=True)
    partial_back = beta_apply(returned_one, beta_tiles[factor], beta_pattern[factor])
    share_cols = lax.psum_scatter(partial_back, "fac", scatter_dimension=1, tiled=True)
    second_update = precondition(
        share_cols,
        string_index * row_count,
        group_index * share_cols.shape[1],
        block_size,
        alpha_sector,
        beta_sector,
        alpha_diag,
        beta_diag,
        energy,
    )
    return (first_update, second_update)


PLANES = 4
HALVES = 2


def row_chunks(bs):
    shares = (2, 2, 2, 1, 1)
    unit = bs // sum(shares)
    starts = [unit * sum(shares[:x]) for x in range(len(shares))]
    return [(start, unit * share) for start, share in zip(starts, shares)]


def exchange_kernel(
    sizes,
    energy,
    vec,
    ta_in,
    tb_in,
    pa_in,
    pb_in,
    sa_in,
    sb_in,
    ad_in,
    bd_in,
    out1,
    out2,
    held,
    far,
    ta_all,
    tb_all,
    tiles_row,
    tiles_turned,
    pa,
    pb,
    sa,
    sb,
    adiag,
    bdiag,
    send1,
    send_far,
    recv1,
    total,
    scale,
    first,
    send2,
    recv2,
    staged,
    held_sem,
    early_sem,
    late_sem,
    give_send,
    give_recv,
    raw_send,
    raw_recv,
    send1_sem,
    far_sem,
    recv1_sem,
    send2_sem,
    recv2_sem,
    o1_send,
    o1_recv,
    o2_send,
    o2_recv,
):
    n, nf, bs, sc, qc, nab, nbb = sizes
    slots = qc + 1
    me = lax.axis_index("str")
    c = lax.axis_index("fac")
    everyone = n * nf
    lanes = n // PLANES
    per = lanes * nf
    row_blocks = nab // n
    plane_blocks = lanes * row_blocks
    half_rows = nab // nf
    half_blocks = nbb // nf
    kb = sc * bs
    hb = bs // HALVES
    plane = me // lanes
    lane = lax.rem(me, lanes)
    side = plane // 2
    inner = lax.rem(plane, 2) != side
    near = 2 * per
    near_count = 2 * per - 1
    own = 3 * per
    chunks = row_chunks(bs)

    def target(v):
        step = v // per
        u = lax.rem(v, per)
        high = lax.rem(side + 1 - step // 2, 2)
        low = lax.rem(lax.rem(plane, 2) + step + step // 2, 2)
        d = (2 * high + low) * lanes + lax.rem(lane + u // nf, lanes)
        return d, lax.rem(c + lax.rem(u, nf), nf)

    def partner(t):
        return t + t // own

    def near_partner(t):
        return near + t + t // per

    def column_of(d, f, q):
        if q < qc:
            return (d * nf + f) * qc + q
        mirror = (PLANES - 1 - d // lanes) * lanes + lax.rem(d, lanes)
        return (mirror * nf + f) * qc

    barrier = pltpu.get_barrier_semaphore()

    def greet(t, carry):
        d, f = target(partner(t))
        pl.semaphore_signal(
            barrier, inc=1, device_id={"fac": f, "str": d}, device_id_type=MESH
        )
        return carry

    lax.fori_loop(0, everyone - 1, greet, 0)

    def block(index):
        return pl.ds(pl.multiple_of(index * bs, bs), bs)

    own_kb = pl.ds(pl.multiple_of(c * kb, kb), kb)
    early = [
        pltpu.make_async_copy(tb_in, tb_all.at[own_kb], early_sem.at[0]),
        pltpu.make_async_copy(pb_in, pb.at[c], early_sem.at[1]),
    ]
    late = [
        pltpu.make_async_copy(ta_in, ta_all.at[own_kb], late_sem.at[0]),
        pltpu.make_async_copy(ad_in, adiag, late_sem.at[1]),
        pltpu.make_async_copy(bd_in, bdiag, late_sem.at[2]),
        pltpu.make_async_copy(pa_in, pa.at[c], late_sem.at[3]),
        pltpu.make_async_copy(sa_in, sa, late_sem.at[4]),
        pltpu.make_async_copy(sb_in, sb, late_sem.at[5]),
    ]
    for copy in early:
        copy.start()

    def load(b, carry):
        pltpu.make_async_copy(vec.at[:, block(b)], held.at[b], held_sem).start()
        return carry

    lax.fori_loop(0, nbb, load, 0)
    for copy in late:
        copy.start()

    def gives():
        for e in range(1, nf):
            f = lax.rem(c + e, nf)
            for x, (a, b) in enumerate(
                [
                    (tb_in, tb_all.at[own_kb]),
                    (ta_in, ta_all.at[own_kb]),
                    (pb_in, pb.at[c]),
                    (pa_in, pa.at[c]),
                ]
            ):
                yield pltpu.make_async_remote_copy(
                    src_ref=a,
                    dst_ref=b,
                    send_sem=give_send.at[e - 1, x],
                    recv_sem=give_recv.at[e - 1, x],
                    device_id={"fac": f, "str": me},
                    device_id_type=MESH,
                )

    def raw_copy(x):
        start, rows = chunks[x]
        return pltpu.make_async_remote_copy(
            src_ref=held.at[:, pl.ds(pl.multiple_of(c * bs + start, 16), rows)],
            dst_ref=far[x].at[:, lax.rem(plane, 2)],
            send_sem=raw_send.at[x],
            recv_sem=raw_recv.at[x],
            device_id={"fac": c, "str": (2 - side) * lanes + lane},
            device_id_type=MESH,
        )

    def column(ref, index):
        return jnp.transpose(jnp.broadcast_to(ref[pl.ds(index, 1), :], (bs, bs)))

    def alive(i, j):
        return jnp.where(sa[i] == sb[j], 1.0, 0.0).astype(jnp.float32)

    def beta_image(q, v, store):
        d, f = target(v)
        j = column_of(d, f, q)
        picked = jnp.concatenate([held[pb[c, s, j]] for s in range(sc)], axis=1)
        image = jnp.dot(picked, tb_all[own_kb, :], preferred_element_type=jnp.float32)
        for x in range(row_blocks):
            store(x, image[x * bs : (x + 1) * bs].astype(jnp.bfloat16))

    def stored_out(q, v):
        def store(x, value):
            send1[q][v - near, x] = value

        return store

    def first_copy(q, v, x):
        start, rows = chunks[x]
        src = send1[q].at[v - near, :, pl.ds(start, rows)]
        dst = recv1[x].at[q, pl.ds(lane * row_blocks, row_blocks), plane * nf + c]
        if isinstance(v, int) and v == own:
            return pltpu.make_async_copy(src, dst, recv1_sem.at[x])
        d, f = target(v)
        return pltpu.make_async_remote_copy(
            src_ref=src,
            dst_ref=dst,
            send_sem=send1_sem.at[q],
            recv_sem=recv1_sem.at[x],
            device_id={"fac": f, "str": d},
            device_id_type=MESH,
        )

    def first_copies(q, v):
        for x in range(len(chunks)):
            first_copy(q, v, x).start()

    pltpu.make_async_copy(held, held, held_sem).wait()
    for copy in early:
        copy.wait()
    beta_image(0, near, stored_out(0, near))
    pl.semaphore_wait(barrier, everyone - 1)
    raw_copy(0).start()
    for copy in gives():
        copy.start()

    raw_copy(1).start()
    for q in range(qc):
        if q > 0:
            beta_image(q, near, stored_out(q, near))

        def step_one(t, carry, q=q):
            v = near_partner(t)
            beta_image(q, v, stored_out(q, v))
            first_copies(q, near_partner(t - 1))
            return carry

        lax.fori_loop(1, near_count, step_one, 0)
        first_copies(q, near_partner(near_count - 1))
        beta_image(q, own, stored_out(q, own))
        first_copies(q, own)

    extra_base = jnp.where(inner, own, near)
    extra_start = jnp.where(inner, 1, 0)

    def step_extra(t, carry):
        v = extra_base + t
        beta_image(qc, v, stored_out(qc, v))
        first_copies(qc, v)
        return carry

    lax.fori_loop(extra_start, per, step_extra, 0)

    @pl.when(inner)
    def _():
        beta_image(qc, own, stored_out(qc, own))
        first_copies(qc, own)

    for copy in late:
        copy.wait()
    for copy in gives():
        copy.wait()
    for x in range(nf * sc):
        tiles_row[:, x * bs : (x + 1) * bs] = ta_all[x * bs : (x + 1) * bs, :]

    width = nf * kb
    spot = lax.broadcasted_iota(jnp.int32, (width, width), 1)
    origin = jnp.zeros((width, width), jnp.int32)
    for start, rows in chunks:
        inside = spot - start * nf * sc
        source = inside // rows * bs + start + lax.rem(inside, rows)
        origin = jnp.where(inside >= 0, source, origin)
    turn = jnp.where(
        lax.broadcasted_iota(jnp.int32, (width, width), 0) == origin, 1.0, 0.0
    ).astype(jnp.bfloat16)
    tiles_turned[...] = jnp.dot(
        tiles_row[...], turn, preferred_element_type=jnp.float32
    ).astype(jnp.bfloat16)

    def scale_columns(q):
        j = column_of(me, c, q)

        def one(i, carry):
            denominator = column(adiag, i) + bdiag[pl.ds(j, 1), :] - energy[0]
            value = alive(i, j) / denominator
            if q < qc:
                scale[0][i, :, q * bs : (q + 1) * bs] = value
            else:
                scale[1][i] = value
            return carry

        lax.fori_loop(0, nab, one, 0)

    for q in range(qc):
        scale_columns(q)

    @pl.when(inner)
    def _():
        scale_columns(qc)

    bunch = 4 if per % 4 == 0 else 1

    def far_images(x, base, count, qs):
        rows = chunks[x][1]
        places = [target(base + u) for u in range(count)]
        for k in range(nf):
            picked = []
            for d, f in places:
                for q in qs:
                    j = column_of(d, f, q)
                    picked.append(
                        jnp.concatenate(
                            [far[x][pb[k, s, j]].reshape(2 * rows, bs) for s in range(sc)],
                            axis=1,
                        )
                    )
            image = jnp.dot(
                jnp.concatenate(picked, axis=0),
                tb_all[k * kb : (k + 1) * kb, :],
                preferred_element_type=jnp.float32,
            ).astype(jnp.bfloat16)
            at = 0
            for u in range(count):
                for q in qs:
                    for z in range(2):
                        send_far[x][(base - near + u) * slots + q, z * nf + k] = image[
                            at : at + rows
                        ]
                        at += rows

    def far_copy(x, v, q, stay=False):
        src = send_far[x].at[(v - near) * slots + q]
        dst = recv1[x].at[q, lane * row_blocks + c, pl.ds(2 * (1 - side) * nf, 2 * nf)]
        if stay:
            return pltpu.make_async_copy(src, dst, recv1_sem.at[x])
        d, f = target(v)
        return pltpu.make_async_remote_copy(
            src_ref=src,
            dst_ref=dst,
            send_sem=far_sem.at[x],
            recv_sem=recv1_sem.at[x],
            device_id={"fac": f, "str": d},
            device_id_type=MESH,
        )

    def far_step(x):
        def step(g, carry):
            base = near + g * bunch
            far_images(x, base, bunch, tuple(range(qc)))
            for q in range(qc):

                @pl.when(base == own)
                def _(q=q):
                    far_copy(x, own, q, stay=True).start()

                @pl.when(base != own)
                def _(q=q):
                    far_copy(x, base, q).start()

                for u in range(1, bunch):
                    far_copy(x, base + u, q).start()
            return carry

        lax.fori_loop(0, 2 * per // bunch, step, 0)
        far_images(x, own, per, (qc,))
        far_copy(x, own, qc, stay=True).start()
        for u in range(1, per):
            far_copy(x, own + u, qc).start()

    def partial(x, i, cols):
        start, rows = chunks[x]
        parts = []
        for k in range(nf):
            for s in range(sc):
                p = pa[k, s, i]
                a, b = lax.rem(p, plane_blocks), lax.div(p, plane_blocks) * nf + k
                parts.append(jnp.concatenate([recv1[x][q, a, b] for q in cols], axis=1))
        return jnp.dot(
            tiles_turned[:, start * nf * sc : (start + rows) * nf * sc],
            jnp.concatenate(parts, axis=0),
            preferred_element_type=jnp.float32,
        )

    def accumulate(x, which):
        cols = tuple(range(qc)) if which == 0 else (qc,)

        def one(i, carry):
            value = partial(x, i, cols)
            if x > 0:
                value = value + total[which][i]
            if x < len(chunks) - 1:
                total[which][i] = value
            else:
                first[which][i] = (value * scale[which][i]).astype(jnp.bfloat16)
            return carry

        lax.fori_loop(0, nab, one, 0)

    def landed(x):
        @pl.when(inner)
        def _():
            pltpu.make_async_copy(recv1[x], recv1[x], recv1_sem.at[x]).wait()

        @pl.when(jnp.logical_not(inner))
        def _():
            some = recv1[x].at[pl.ds(0, qc)]
            pltpu.make_async_copy(some, some, recv1_sem.at[x]).wait()

    for x in range(len(chunks)):

        @pl.when(inner)
        def _(x=x):
            pltpu.make_async_copy(far[x], far[x], raw_recv.at[x]).wait()

        raw_copy(x).wait_send()
        if x + 2 < len(chunks):
            raw_copy(x + 2).start()

        @pl.when(inner)
        def _(x=x):
            far_step(x)

        if x > 0:
            landed(x - 1)
            accumulate(x - 1, 0)

            @pl.when(inner)
            def _(x=x):
                accumulate(x - 1, 1)

    landed(len(chunks) - 1)
    accumulate(len(chunks) - 1, 0)

    def second_copy(q, h, t):
        v = partner(t)
        d, f = target(v)
        return pltpu.make_async_remote_copy(
            src_ref=send2[q].at[h, v],
            dst_ref=recv2[h].at[column_of(me, c, q)],
            send_sem=send2_sem.at[q, h],
            recv_sem=recv2_sem.at[h],
            device_id={"fac": f, "str": d},
            device_id_type=MESH,
        )

    def share_copy(e):
        f = lax.rem(c + e, nf)
        src = first[0].at[pl.ds(f * half_rows, half_rows)]
        dst = out1.at[:, :, pl.ds(pl.multiple_of(c * qc * bs, bs), qc * bs)]
        if e == 0:
            return pltpu.make_async_copy(src, dst, o1_send.at[e])
        return pltpu.make_async_remote_copy(
            src_ref=src,
            dst_ref=dst,
            send_sem=o1_send.at[e],
            recv_sem=o1_recv.at[e],
            device_id={"fac": f, "str": me},
            device_id_type=MESH,
        )

    def begin(q):
        return jnp.where(inner, near, 0) if q == 0 else near if q == qc else 0

    def alpha_images(v, which, cols, store):
        d, f = target(v)
        i = d * nf + f
        for k in range(nf):
            picked = jnp.concatenate([first[which][pa[k, s, i]] for s in range(sc)], axis=0)
            image = jnp.dot(
                tiles_row[:, k * kb : (k + 1) * kb],
                picked,
                preferred_element_type=jnp.float32,
            ).astype(jnp.bfloat16)
            for y, q in enumerate(cols):
                for h in range(HALVES):
                    store(q, h, k, image[h * hb : (h + 1) * hb, y * bs : (y + 1) * bs])

    def images_out(which, cols):
        def sending(t):
            for q in reversed(cols):

                @pl.when(t >= begin(q))
                def _(q=q):
                    second_copy(q, 0, t).start()

        low = near if which else 0

        def step_two(t, carry):
            v = partner(t)

            def store(q, h, k, value):
                send2[q][h, v, k] = value

            alpha_images(v, which, cols, store)

            @pl.when(t > low)
            def _():
                sending(t - 1)

            return carry

        lax.fori_loop(low, everyone - 1, step_two, 0)
        sending(everyone - 2)

        def keep(q, h, k, value):
            recv2[h][column_of(me, c, q), k] = value

        alpha_images(own, which, cols, keep)

    order = list(reversed(range(qc)))
    images_out(0, tuple(range(qc)))
    for e in range(nf):
        share_copy(e).start()

    @pl.when(inner)
    def _():
        accumulate(len(chunks) - 1, 1)
        images_out(1, (qc,))

    def send_rest(q, h):
        def rest(t, carry):
            second_copy(q, h, t).start()
            return carry

        lax.fori_loop(begin(q), everyone - 1, rest, 0)

    for h in range(1, HALVES):
        for q in order:
            send_rest(q, h)

        @pl.when(inner)
        def _(h=h):
            send_rest(qc, h)

    mine = me * nf + c
    group = max(g for g in (1, 2, 4, 8) if half_blocks % g == 0)
    pieces = half_blocks // group

    def sigma_two(h, first_block):
        rows = []
        for g in range(group):
            parts = [
                recv2[h][pb[k, s, first_block + g], k] for k in range(nf) for s in range(sc)
            ]
            rows.append(jnp.concatenate(parts, axis=1))
        sigma = jnp.dot(
            jnp.concatenate(rows, axis=0), tb_all[...], preferred_element_type=jnp.float32
        )
        alpha_part = column(adiag, mine)[h * hb : (h + 1) * hb]
        for g in range(group):
            j = first_block + g
            denominator = alpha_part + bdiag[pl.ds(j, 1), :] - energy[0]
            value = sigma[g * hb : (g + 1) * hb] * alive(mine, j) / denominator
            staged[h * hb : (h + 1) * hb, block(j)] = value.astype(jnp.bfloat16)

    def piece_copy(h, e, x):
        f = lax.rem(c + e, nf)
        src_start = pl.multiple_of((f * half_blocks + x * group) * bs, bs)
        dst_start = pl.multiple_of(x * group * bs, bs)
        src = staged.at[pl.ds(h * hb, hb), pl.ds(src_start, group * bs)]
        dst = out2.at[
            pl.ds(pl.multiple_of(c * bs + h * hb, hb), hb), pl.ds(dst_start, group * bs)
        ]
        if e == 0:
            return pltpu.make_async_copy(src, dst, o2_send.at[e])
        return pltpu.make_async_remote_copy(
            src_ref=src,
            dst_ref=dst,
            send_sem=o2_send.at[e],
            recv_sem=o2_recv.at[e],
            device_id={"fac": f, "str": me},
            device_id_type=MESH,
        )

    for h in range(HALVES):

        def second_wait(count, h=h):
            some = recv2[h].at[pl.ds(0, count)]
            pltpu.make_async_copy(some, some, recv2_sem.at[h]).wait()

        @pl.when(inner)
        def _(second_wait=second_wait):
            second_wait(nbb - slots)

        @pl.when(jnp.logical_not(inner))
        def _(second_wait=second_wait):
            second_wait(nbb - qc)

        for e in reversed(range(nf)):

            def finish(x, carry, e=e, h=h):
                sigma_two(h, lax.rem(c + e, nf) * half_blocks + x * group)
                piece_copy(h, e, x).start()
                return carry

            lax.fori_loop(0, pieces, finish, 0)

    def second_sent(q, h, count):
        sent = send2[q].at[h, pl.ds(0, count)]
        pltpu.make_async_copy(sent, sent, send2_sem.at[q, h]).wait()

    def near_sent(q, count):
        sent = send1[q].at[pl.ds(0, count)]
        pltpu.make_async_copy(sent, sent, send1_sem.at[q]).wait()

    for q in range(qc):
        near_sent(q, near_count)
    for e in range(nf):
        share_copy(e).wait()

    @pl.when(inner)
    def _():
        near_sent(qc, per - 1)
        for x in range(len(chunks)):
            some = send_far[x].at[pl.ds(0, near_count * qc + per - 1)]
            pltpu.make_async_copy(some, some, far_sem.at[x]).wait()
        for h in range(HALVES):
            for q in range(slots):
                second_sent(q, h, near_count if q in (0, qc) else everyone - 1)

    @pl.when(jnp.logical_not(inner))
    def _():
        near_sent(qc, per)
        for h in range(HALVES):
            for q in range(qc):
                second_sent(q, h, everyone - 1)

    for e in range(nf):
        sent = staged.at[:, pl.ds(0, half_blocks * bs)]
        pltpu.make_async_copy(sent, sent, o2_send.at[e]).wait()
        if e > 0:
            pltpu.make_async_copy(sent, sent, o2_recv.at[e]).wait()


def split_body(
    vector,
    alpha_tiles,
    alpha_pattern,
    beta_tiles,
    beta_pattern,
    alpha_sector,
    beta_sector,
    alpha_diag,
    beta_diag,
    energy,
):
    n = lax.axis_size("str")
    nf = lax.axis_size("fac")
    sc, bs = alpha_tiles.shape[1], alpha_tiles.shape[2]
    nab, nbb = alpha_sector.shape[0], beta_sector.shape[0]
    qc = nbb // (n * nf)
    slots = qc + 1
    rows = vector.shape[0]
    smem = pl.BlockSpec(memory_space=pltpu.SMEM)
    anywhere = pl.BlockSpec(memory_space=pl.ANY)
    hbm = pl.BlockSpec(memory_space=pltpu.HBM)
    bf16 = jnp.bfloat16
    everyone = n * nf
    row_blocks = nab // n
    near = everyone // 2
    hb = bs // HALVES
    chunks = row_chunks(bs)
    dma = pltpu.SemaphoreType.DMA
    first_update, second_update = pl.pallas_call(
        functools.partial(exchange_kernel, (n, nf, bs, sc, qc, nab, nbb)),
        out_shape=(
            jax.ShapeDtypeStruct((nab // nf, bs, nbb * bs // n), bf16),
            jax.ShapeDtypeStruct((rows, nbb * bs // nf), bf16),
        ),
        in_specs=[smem] + [hbm] * 9,
        out_specs=(anywhere, anywhere),
        scratch_shapes=[
            pltpu.VMEM((nbb, rows, bs), bf16),
            [pltpu.VMEM((nbb, 2, count, bs), bf16) for _, count in chunks],
            pltpu.VMEM((nf * sc * bs, bs), bf16),
            pltpu.VMEM((nf * sc * bs, bs), bf16),
            pltpu.VMEM((bs, nf * sc * bs), bf16),
            pltpu.VMEM((bs, nf * sc * bs), bf16),
            pltpu.SMEM((nf, sc, nab), jnp.int32),
            pltpu.SMEM((nf, sc, nbb), jnp.int32),
            pltpu.SMEM((nab,), jnp.int32),
            pltpu.SMEM((nbb,), jnp.int32),
            pltpu.VMEM((nab, bs), jnp.float32),
            pltpu.VMEM((nbb, bs), jnp.float32),
            [pltpu.VMEM((near, row_blocks, bs, bs), bf16) for _ in range(slots)],
            [pltpu.VMEM((near * slots, 2 * nf, count, bs), bf16) for _, count in chunks],
            [
                pltpu.VMEM((slots, nab // PLANES, PLANES * nf, count, bs), bf16)
                for _, count in chunks
            ],
            [pltpu.VMEM((nab, bs, cols * bs), jnp.float32) for cols in (qc, 1)],
            [pltpu.VMEM((nab, bs, cols * bs), jnp.float32) for cols in (qc, 1)],
            [pltpu.VMEM((nab, bs, cols * bs), bf16) for cols in (qc, 1)],
            [pltpu.VMEM((HALVES, everyone, nf, hb, bs), bf16) for _ in range(slots)],
            [pltpu.VMEM((nbb, nf, hb, bs), bf16) for _ in range(HALVES)],
            pltpu.VMEM((bs, nbb * bs), bf16),
            dma,
            dma((2,)),
            dma((6,)),
            dma((nf - 1, 4)),
            dma((nf - 1, 4)),
            dma((len(chunks),)),
            dma((len(chunks),)),
            dma((slots,)),
            dma((len(chunks),)),
            dma((len(chunks),)),
            dma((slots, HALVES)),
            dma((HALVES,)),
            dma((nf,)),
            dma((nf,)),
            dma((nf,)),
            dma((nf,)),
        ],
        compiler_params=pltpu.CompilerParams(
            collective_id=0, has_side_effects=True, vmem_limit_bytes=61 * 1024 * 1024
        ),
    )(
        energy,
        vector,
        alpha_tiles.reshape(sc * bs, bs),
        beta_tiles.reshape(sc * bs, bs),
        alpha_pattern[0].T,
        beta_pattern[0].T,
        alpha_sector,
        beta_sector,
        alpha_diag.reshape(nab, bs),
        beta_diag.reshape(nbb, bs),
    )
    return first_update.reshape(nab * bs // nf, nbb * bs // n), second_update


def fits_split(*args):
    vector, alpha_tiles, _, _, _, alpha_sector, beta_sector = args[:7]
    n, nf = lax.axis_size("str"), lax.axis_size("fac")
    bs = alpha_tiles.shape[2]
    nab, nbb = alpha_sector.shape[0], beta_sector.shape[0]
    return (
        n % PLANES == 0
        and nf > 1
        and alpha_tiles.shape[0] == 1
        and bs % 128 == 0
        and nab == n * nf
        and nbb == 2 * n * nf
    )


def either_body(*args):
    return split_body(*args) if fits_split(*args) else body(*args)


def solution(mesh):
    return jax.shard_map(
        either_body,
        mesh=mesh,
        in_specs=(
            P("str", None),
            P("fac", None, None, None),
            P("fac", None, None),
            P("fac", None, None, None),
            P("fac", None, None),
            P(),
            P(),
            P(),
            P(),
            P(),
        ),
        out_specs=(P("fac", "str"), P("str", "fac")),
        check_vma=False,
    )
```

```python
import functools

import jax
import jax.numpy as jnp
from jax import lax
from jax.experimental import pallas as pl
from jax.experimental.pallas import tpu as pltpu
from jax.sharding import PartitionSpec as P

MESH = pl.DeviceIdType.MESH


def beta_apply(matrix, tile_set, pattern):
    height, width = matrix.shape
    slot_count, block_size = tile_set.shape[:2]
    stacked = tile_set.reshape(slot_count * block_size, block_size)

    def one(j, result):
        picked = jnp.concatenate(
            [
                lax.dynamic_slice_in_dim(matrix, pattern[j, s] * block_size, block_size, 1)
                for s in range(slot_count)
            ],
            axis=1,
        )
        image = jnp.dot(picked, stacked, preferred_element_type=jnp.float32)
        return lax.dynamic_update_slice_in_dim(result, image, j * block_size, 1)

    return lax.fori_loop(
        0, width // block_size, one, jnp.zeros((height, width), jnp.float32)
    )


def alpha_apply(matrix, tile_set, pattern):
    height, width = matrix.shape
    slot_count, block_size = tile_set.shape[:2]
    stacked = tile_set.transpose(1, 0, 2).reshape(block_size, slot_count * block_size)

    def one(i, result):
        picked = jnp.concatenate(
            [
                lax.dynamic_slice_in_dim(matrix, pattern[i, s] * block_size, block_size, 0)
                for s in range(slot_count)
            ],
            axis=0,
        )
        image = jnp.dot(stacked, picked, preferred_element_type=jnp.float32)
        return lax.dynamic_update_slice_in_dim(result, image, i * block_size, 0)

    return lax.fori_loop(
        0, height // block_size, one, jnp.zeros((height, width), jnp.float32)
    )


def precondition(
    sigma_part,
    row_start,
    col_start,
    block_size,
    alpha_sector,
    beta_sector,
    alpha_diag,
    beta_diag,
    energy,
):
    row_count, col_count = sigma_part.shape
    row_blocks = row_count // block_size
    col_blocks = col_count // block_size
    alpha_labels = lax.dynamic_slice_in_dim(alpha_sector, row_start // block_size, row_blocks)
    beta_labels = lax.dynamic_slice_in_dim(beta_sector, col_start // block_size, col_blocks)
    live_mask = (alpha_labels[:, None, None, None] == beta_labels[None, None, :, None]).astype(
        jnp.float32
    )
    masked = (
        sigma_part.reshape(row_blocks, block_size, col_blocks, block_size) * live_mask
    ).reshape(row_count, col_count)
    alpha_part = lax.dynamic_slice_in_dim(alpha_diag, row_start, row_count)
    beta_part = lax.dynamic_slice_in_dim(beta_diag, col_start, col_count)
    denominator = alpha_part[:, None] + beta_part[None, :] - energy[0]
    return (masked / denominator).astype(jnp.bfloat16)


def body(
    vector,
    alpha_tiles,
    alpha_pattern,
    beta_tiles,
    beta_pattern,
    alpha_sector,
    beta_sector,
    alpha_diag,
    beta_diag,
    energy,
):
    string_index = lax.axis_index("str")
    group_index = lax.axis_index("fac")
    string_count = lax.axis_size("str")
    block_size = alpha_tiles.shape[2]
    row_count = vector.shape[0]
    col_count = vector.shape[1] // string_count
    factor = 0
    image = beta_apply(vector, beta_tiles[factor], beta_pattern[factor]).astype(jnp.bfloat16)
    moved_one = lax.all_to_all(image, "str", split_axis=1, concat_axis=0, tiled=True)
    partial_value = alpha_apply(moved_one, alpha_tiles[factor], alpha_pattern[factor])
    share_rows = lax.psum_scatter(partial_value, "fac", scatter_dimension=0, tiled=True)
    first_update = precondition(
        share_rows,
        group_index * share_rows.shape[0],
        string_index * col_count,
        block_size,
        alpha_sector,
        beta_sector,
        alpha_diag,
        beta_diag,
        energy,
    )
    whole_first = lax.all_gather(first_update, "fac", axis=0, tiled=True)
    factor = 0
    back_image = alpha_apply(whole_first, alpha_tiles[factor], alpha_pattern[factor]).astype(
        jnp.bfloat16
    )
    returned_one = lax.all_to_all(back_image, "str", split_axis=0, concat_axis=1, tiled=True)
    partial_back = beta_apply(returned_one, beta_tiles[factor], beta_pattern[factor])
    share_cols = lax.psum_scatter(partial_back, "fac", scatter_dimension=1, tiled=True)
    second_update = precondition(
        share_cols,
        string_index * row_count,
        group_index * share_cols.shape[1],
        block_size,
        alpha_sector,
        beta_sector,
        alpha_diag,
        beta_diag,
        energy,
    )
    return (first_update, second_update)


PLANES = 4
HALVES = 2


def row_chunks(bs):
    shares = (3, 2, 2, 1)
    unit = bs // sum(shares)
    starts = [unit * sum(shares[:x]) for x in range(len(shares))]
    return [(start, unit * share) for start, share in zip(starts, shares)]


def exchange_kernel(
    sizes,
    energy,
    vec,
    ta_in,
    tb_in,
    pa_in,
    pb_in,
    sa_in,
    sb_in,
    ad_in,
    bd_in,
    out1,
    out2,
    held,
    far,
    ta_all,
    tb_all,
    tiles_row,
    tiles_turned,
    pa,
    pb,
    sa,
    sb,
    adiag,
    bdiag,
    send1,
    send_far,
    recv1,
    total,
    scale,
    scale_last,
    first,
    send2,
    recv2,
    staged,
    held_sem,
    early_sem,
    late_sem,
    give_send,
    give_recv,
    raw_send,
    raw_recv,
    send1_sem,
    far_sem,
    recv1_sem,
    send2_sem,
    recv2_sem,
    o1_send,
    o1_recv,
    o2_send,
    o2_recv,
):
    n, nf, bs, sc, qc, nab, nbb = sizes
    slots = qc + 1
    me = lax.axis_index("str")
    c = lax.axis_index("fac")
    everyone = n * nf
    lanes = n // PLANES
    per = lanes * nf
    row_blocks = nab // n
    plane_blocks = lanes * row_blocks
    half_rows = nab // nf
    half_blocks = nbb // nf
    kb = sc * bs
    hb = bs // HALVES
    plane = me // lanes
    lane = lax.rem(me, lanes)
    side = plane // 2
    inner = lax.rem(plane, 2) != side
    near = 2 * per
    near_count = 2 * per - 1
    bunch = 4 if per % 4 == 0 else 1
    own = 3 * per
    chunks = row_chunks(bs)

    def target(v):
        step = v // per
        u = lax.rem(v, per)
        high = lax.rem(side + 1 - step // 2, 2)
        low = lax.rem(lax.rem(plane, 2) + step + step // 2, 2)
        d = (2 * high + low) * lanes + lax.rem(lane + u // nf, lanes)
        return d, lax.rem(c + lax.rem(u, nf), nf)

    def partner(t):
        return t + t // own

    def column_of(d, f, q):
        if q < qc:
            return (d * nf + f) * qc + q
        mirror = (PLANES - 1 - d // lanes) * lanes + lax.rem(d, lanes)
        return (mirror * nf + f) * qc

    barrier = pltpu.get_barrier_semaphore()

    def block(index):
        return pl.ds(pl.multiple_of(index * bs, bs), bs)

    own_kb = pl.ds(pl.multiple_of(c * kb, kb), kb)
    early = [
        pltpu.make_async_copy(tb_in, tb_all.at[own_kb], early_sem.at[0]),
        pltpu.make_async_copy(pb_in, pb.at[c], early_sem.at[1]),
    ]
    late = [
        pltpu.make_async_copy(ta_in, ta_all.at[own_kb], late_sem.at[0]),
        pltpu.make_async_copy(ad_in, adiag, late_sem.at[1]),
        pltpu.make_async_copy(bd_in, bdiag, late_sem.at[2]),
        pltpu.make_async_copy(pa_in, pa.at[c], late_sem.at[3]),
        pltpu.make_async_copy(sa_in, sa, late_sem.at[4]),
        pltpu.make_async_copy(sb_in, sb, late_sem.at[5]),
    ]
    for copy in early:
        copy.start()

    def load(b, carry):
        pltpu.make_async_copy(vec.at[:, block(b)], held.at[b], held_sem).start()
        return carry

    lax.fori_loop(0, nbb, load, 0, unroll=8)

    def greet(t, carry):
        d, f = target(partner(t))
        pl.semaphore_signal(
            barrier, inc=1, device_id={"fac": f, "str": d}, device_id_type=MESH
        )
        return carry

    lax.fori_loop(0, everyone - 1, greet, 0)

    for copy in late:
        copy.start()

    def gives():
        for e in range(1, nf):
            f = lax.rem(c + e, nf)
            for x, (a, b) in enumerate(
                [
                    (tb_in, tb_all.at[own_kb]),
                    (ta_in, ta_all.at[own_kb]),
                    (pb_in, pb.at[c]),
                    (pa_in, pa.at[c]),
                ]
            ):
                yield pltpu.make_async_remote_copy(
                    src_ref=a,
                    dst_ref=b,
                    send_sem=give_send.at[e - 1, x],
                    recv_sem=give_recv.at[e - 1, x],
                    device_id={"fac": f, "str": me},
                    device_id_type=MESH,
                )

    def raw_copy(x):
        start, rows = chunks[x]
        return pltpu.make_async_remote_copy(
            src_ref=held.at[:, pl.ds(pl.multiple_of(c * bs + start, 16), rows)],
            dst_ref=far[x].at[:, lax.rem(plane, 2)],
            send_sem=raw_send.at[x],
            recv_sem=raw_recv.at[x],
            device_id={"fac": c, "str": (2 - side) * lanes + lane},
            device_id_type=MESH,
        )

    def column(ref, index):
        return jnp.transpose(jnp.broadcast_to(ref[pl.ds(index, 1), :], (bs, bs)))

    def alive(i, j):
        return jnp.where(sa[i] == sb[j], 1.0, 0.0).astype(jnp.float32)

    def near_images(q, base):
        picked = []
        for u in range(bunch):
            d, f = target(base + u)
            j = column_of(d, f, q)
            picked.append(jnp.concatenate([held[pb[c, s, j]] for s in range(sc)], axis=1))
        image = jnp.dot(
            jnp.concatenate(picked, axis=0),
            tb_all[own_kb, :],
            preferred_element_type=jnp.float32,
        ).astype(jnp.bfloat16)
        at = 0
        for u in range(bunch):
            for x in range(row_blocks):
                send1[q][base - near + u, x] = image[at : at + bs]
                at += bs

    def first_copy(q, v, x, stay=False):
        start, rows = chunks[x]
        src = send1[q].at[v - near, :, pl.ds(start, rows)]
        dst = recv1[x].at[q, pl.ds(lane * row_blocks, row_blocks), plane * nf + c]
        if stay:
            return pltpu.make_async_copy(src, dst, recv1_sem.at[x])
        d, f = target(v)
        return pltpu.make_async_remote_copy(
            src_ref=src,
            dst_ref=dst,
            send_sem=send1_sem.at[q],
            recv_sem=recv1_sem.at[x],
            device_id={"fac": f, "str": d},
            device_id_type=MESH,
        )

    def first_copies(q, base):
        for x in range(len(chunks)):

            @pl.when(base == own)
            def _():
                first_copy(q, own, x, stay=True).start()

            @pl.when(base != own)
            def _():
                first_copy(q, base, x).start()

            for u in range(1, bunch):
                first_copy(q, base + u, x).start()

    pltpu.make_async_copy(held, held, held_sem).wait()
    for copy in early:
        copy.wait()
    pl.semaphore_wait(barrier, everyone - 1)
    raw_copy(0).start()
    for copy in gives():
        copy.start()

    raw_copy(1).start()
    for q in range(qc):

        def step_one(g, carry, q=q):
            near_images(q, near + g * bunch)
            first_copies(q, near + g * bunch)
            return carry

        lax.fori_loop(0, 2 * per // bunch, step_one, 0)

    extra_base = jnp.where(inner, own, near)

    def step_extra(g, carry):
        near_images(qc, extra_base + g * bunch)
        first_copies(qc, extra_base + g * bunch)
        return carry

    lax.fori_loop(0, per // bunch, step_extra, 0)

    for copy in late:
        copy.wait()
    for copy in gives():
        copy.wait()
    for x in range(nf * sc):
        tiles_row[:, x * bs : (x + 1) * bs] = ta_all[x * bs : (x + 1) * bs, :]

    width = nf * kb
    spot = lax.broadcasted_iota(jnp.int32, (width, width), 1)
    origin = jnp.zeros((width, width), jnp.int32)
    for start, rows in chunks:
        inside = spot - start * nf * sc
        source = inside // rows * bs + start + lax.rem(inside, rows)
        origin = jnp.where(inside >= 0, source, origin)
    turn = jnp.where(
        lax.broadcasted_iota(jnp.int32, (width, width), 0) == origin, 1.0, 0.0
    ).astype(jnp.bfloat16)
    tiles_turned[...] = jnp.dot(
        tiles_row[...], turn, preferred_element_type=jnp.float32
    ).astype(jnp.bfloat16)

    def scale_columns(q):
        j = column_of(me, c, q)

        def one(i, carry):
            denominator = column(adiag, i) + bdiag[pl.ds(j, 1), :] - energy[0]
            value = alive(i, j) / denominator
            if q < qc:
                scale[0][i, :, q * bs : (q + 1) * bs] = value
            else:
                scale[1][i] = value
            return carry

        lax.fori_loop(0, nab, one, 0)

    for q in range(qc):
        scale_columns(q)

    @pl.when(inner)
    def _():
        scale_columns(qc)

    def far_images(x, base, count, qs):
        rows = chunks[x][1]
        places = [target(base + u) for u in range(count)]
        for k in range(nf):
            picked = []
            for d, f in places:
                for q in qs:
                    j = column_of(d, f, q)
                    picked.append(
                        jnp.concatenate(
                            [far[x][pb[k, s, j]].reshape(2 * rows, bs) for s in range(sc)],
                            axis=1,
                        )
                    )
            image = jnp.dot(
                jnp.concatenate(picked, axis=0),
                tb_all[k * kb : (k + 1) * kb, :],
                preferred_element_type=jnp.float32,
            ).astype(jnp.bfloat16)
            at = 0
            for u in range(count):
                for q in qs:
                    for z in range(2):
                        send_far[x][(base - near + u) * slots + q, z * nf + k] = image[
                            at : at + rows
                        ]
                        at += rows

    def far_copy(x, v, q, stay=False):
        src = send_far[x].at[(v - near) * slots + q]
        dst = recv1[x].at[q, lane * row_blocks + c, pl.ds(2 * (1 - side) * nf, 2 * nf)]
        if stay:
            return pltpu.make_async_copy(src, dst, recv1_sem.at[x])
        d, f = target(v)
        return pltpu.make_async_remote_copy(
            src_ref=src,
            dst_ref=dst,
            send_sem=far_sem.at[x],
            recv_sem=recv1_sem.at[x],
            device_id={"fac": f, "str": d},
            device_id_type=MESH,
        )

    def far_step(x):
        def step(g, carry):
            base = near + g * bunch
            far_images(x, base, bunch, tuple(range(qc)))
            for q in range(qc):

                @pl.when(base == own)
                def _(q=q):
                    far_copy(x, own, q, stay=True).start()

                @pl.when(base != own)
                def _(q=q):
                    far_copy(x, base, q).start()

                for u in range(1, bunch):
                    far_copy(x, base + u, q).start()
            return carry

        lax.fori_loop(0, 2 * per // bunch, step, 0)
        far_images(x, own, per, (qc,))
        far_copy(x, own, qc, stay=True).start()
        for u in range(1, per):
            far_copy(x, own + u, qc).start()

    def partial(x, i, cols):
        start, rows = chunks[x]
        parts = []
        for k in range(nf):
            for s in range(sc):
                p = pa[k, s, i]
                a, b = lax.rem(p, plane_blocks), lax.div(p, plane_blocks) * nf + k
                parts.append(jnp.concatenate([recv1[x][q, a, b] for q in cols], axis=1))
        return jnp.dot(
            tiles_turned[:, start * nf * sc : (start + rows) * nf * sc],
            jnp.concatenate(parts, axis=0),
            preferred_element_type=jnp.float32,
        )

    def accumulate(x, which):
        cols = tuple(range(qc)) if which == 0 else (qc,)

        def one(i, carry):
            value = partial(x, i, cols)
            if x > 0:
                value = value + total[which][i]
            if x < len(chunks) - 1:
                total[which][i] = value
            else:
                first[which][i] = (value * scale[which][i]).astype(jnp.bfloat16)
            return carry

        lax.fori_loop(0, nab, one, 0, unroll=4)

    def landed(x):
        @pl.when(inner)
        def _():
            pltpu.make_async_copy(recv1[x], recv1[x], recv1_sem.at[x]).wait()

        @pl.when(jnp.logical_not(inner))
        def _():
            some = recv1[x].at[pl.ds(0, qc)]
            pltpu.make_async_copy(some, some, recv1_sem.at[x]).wait()

    for x in range(len(chunks)):

        @pl.when(inner)
        def _(x=x):
            pltpu.make_async_copy(far[x], far[x], raw_recv.at[x]).wait()

        raw_copy(x).wait_send()
        if x + 2 < len(chunks):
            raw_copy(x + 2).start()

        @pl.when(inner)
        def _(x=x):
            far_step(x)

        if x > 0:
            landed(x - 1)
            accumulate(x - 1, 0)

            @pl.when(inner)
            def _(x=x):
                accumulate(x - 1, 1)

    landed(len(chunks) - 1)
    accumulate(len(chunks) - 1, 0)

    def second_copy(q, h, v, stay=False):
        src = send2[q].at[h, v]
        dst = recv2[h].at[column_of(me, c, q)]
        if stay:
            return pltpu.make_async_copy(src, dst, recv2_sem.at[h])
        d, f = target(v)
        return pltpu.make_async_remote_copy(
            src_ref=src,
            dst_ref=dst,
            send_sem=send2_sem.at[q, h],
            recv_sem=recv2_sem.at[h],
            device_id={"fac": f, "str": d},
            device_id_type=MESH,
        )

    def share_copy(e):
        f = lax.rem(c + e, nf)
        src = first[0].at[pl.ds(f * half_rows, half_rows)]
        dst = out1.at[:, :, pl.ds(pl.multiple_of(c * qc * bs, bs), qc * bs)]
        if e == 0:
            return pltpu.make_async_copy(src, dst, o1_send.at[e])
        return pltpu.make_async_remote_copy(
            src_ref=src,
            dst_ref=dst,
            send_sem=o1_send.at[e],
            recv_sem=o1_recv.at[e],
            device_id={"fac": f, "str": me},
            device_id_type=MESH,
        )

    def begin(q):
        return jnp.where(inner, near, 0) if q == 0 else near if q == qc else 0

    def alpha_images(v, which, cols):
        d, f = target(v)
        i = d * nf + f
        for k in range(nf):
            picked = jnp.concatenate([first[which][pa[k, s, i]] for s in range(sc)], axis=0)
            image = jnp.dot(
                tiles_row[:, k * kb : (k + 1) * kb],
                picked,
                preferred_element_type=jnp.float32,
            ).astype(jnp.bfloat16)
            for y, q in enumerate(cols):
                for h in range(HALVES):
                    send2[q][h, v, k] = image[h * hb : (h + 1) * hb, y * bs : (y + 1) * bs]

    def second_copies(q, h, base):
        @pl.when(base == own)
        def _():
            second_copy(q, h, own, stay=True).start()

        @pl.when(base != own)
        def _():
            second_copy(q, h, base).start()

        for u in range(1, bunch):
            second_copy(q, h, base + u).start()

    def images_out(which, cols):
        def step_two(g, carry):
            base = g * bunch
            for u in range(bunch):
                alpha_images(base + u, which, cols)
            for q in reversed(cols):

                @pl.when(base >= begin(q))
                def _(q=q):
                    second_copies(q, 0, base)

            return carry

        lax.fori_loop((near if which else 0) // bunch, everyone // bunch, step_two, 0)

    order = list(reversed(range(qc)))
    images_out(0, tuple(range(qc)))
    for e in range(nf):
        share_copy(e).start()

    @pl.when(inner)
    def _():
        accumulate(len(chunks) - 1, 1)
        images_out(1, (qc,))

    def send_rest(q, h):
        def rest(g, carry):
            second_copies(q, h, g * bunch)
            return carry

        lax.fori_loop(begin(q) // bunch, everyone // bunch, rest, 0)

    for h in range(1, HALVES):
        for q in order:
            send_rest(q, h)

        @pl.when(inner)
        def _(h=h):
            send_rest(qc, h)

    mine = me * nf + c
    group = max(g for g in (1, 2, 4, 8) if half_blocks % g == 0)
    pieces = half_blocks // group

    def scale_row(j, carry):
        denominator = column(adiag, mine) + bdiag[pl.ds(j, 1), :] - energy[0]
        scale_last[j] = alive(mine, j) / denominator
        return carry

    lax.fori_loop(0, nbb, scale_row, 0)

    def sigma_two(h, first_block):
        rows = []
        for g in range(group):
            parts = [
                recv2[h][pb[k, s, first_block + g], k] for k in range(nf) for s in range(sc)
            ]
            rows.append(jnp.concatenate(parts, axis=1))
        sigma = jnp.dot(
            jnp.concatenate(rows, axis=0), tb_all[...], preferred_element_type=jnp.float32
        )
        for g in range(group):
            j = first_block + g
            value = sigma[g * hb : (g + 1) * hb] * scale_last[j, h * hb : (h + 1) * hb]
            staged[h * hb : (h + 1) * hb, block(j)] = value.astype(jnp.bfloat16)

    def piece_copy(h, e, x):
        f = lax.rem(c + e, nf)
        src_start = pl.multiple_of((f * half_blocks + x * group) * bs, bs)
        dst_start = pl.multiple_of(x * group * bs, bs)
        src = staged.at[pl.ds(h * hb, hb), pl.ds(src_start, group * bs)]
        dst = out2.at[
            pl.ds(pl.multiple_of(c * bs + h * hb, hb), hb), pl.ds(dst_start, group * bs)
        ]
        if e == 0:
            return pltpu.make_async_copy(src, dst, o2_send.at[e])
        return pltpu.make_async_remote_copy(
            src_ref=src,
            dst_ref=dst,
            send_sem=o2_send.at[e],
            recv_sem=o2_recv.at[e],
            device_id={"fac": f, "str": me},
            device_id_type=MESH,
        )

    for h in range(HALVES):
        pltpu.make_async_copy(recv2[h], recv2[h], recv2_sem.at[h]).wait()
        for e in reversed(range(nf)):

            def finish(x, carry, e=e, h=h):
                sigma_two(h, lax.rem(c + e, nf) * half_blocks + x * group)
                piece_copy(h, e, x).start()
                return carry

            lax.fori_loop(0, pieces, finish, 0)

    def second_sent(q, h, count):
        sent = send2[q].at[h, pl.ds(0, count)]
        pltpu.make_async_copy(sent, sent, send2_sem.at[q, h]).wait()

    def near_sent(q, count):
        sent = send1[q].at[pl.ds(0, count)]
        pltpu.make_async_copy(sent, sent, send1_sem.at[q]).wait()

    for q in range(qc):
        near_sent(q, near_count)
    for e in range(nf):
        share_copy(e).wait()

    @pl.when(inner)
    def _():
        near_sent(qc, per - 1)
        for x in range(len(chunks)):
            some = send_far[x].at[pl.ds(0, near_count * qc + per - 1)]
            pltpu.make_async_copy(some, some, far_sem.at[x]).wait()
        for h in range(HALVES):
            for q in range(slots):
                second_sent(q, h, near_count if q in (0, qc) else everyone - 1)

    @pl.when(jnp.logical_not(inner))
    def _():
        near_sent(qc, per)
        for h in range(HALVES):
            for q in range(qc):
                second_sent(q, h, everyone - 1)

    for e in range(nf):
        sent = staged.at[:, pl.ds(0, half_blocks * bs)]
        pltpu.make_async_copy(sent, sent, o2_send.at[e]).wait()
        if e > 0:
            pltpu.make_async_copy(sent, sent, o2_recv.at[e]).wait()


def split_body(
    vector,
    alpha_tiles,
    alpha_pattern,
    beta_tiles,
    beta_pattern,
    alpha_sector,
    beta_sector,
    alpha_diag,
    beta_diag,
    energy,
):
    n = lax.axis_size("str")
    nf = lax.axis_size("fac")
    sc, bs = alpha_tiles.shape[1], alpha_tiles.shape[2]
    nab, nbb = alpha_sector.shape[0], beta_sector.shape[0]
    qc = nbb // (n * nf)
    slots = qc + 1
    rows = vector.shape[0]
    smem = pl.BlockSpec(memory_space=pltpu.SMEM)
    anywhere = pl.BlockSpec(memory_space=pl.ANY)
    hbm = pl.BlockSpec(memory_space=pltpu.HBM)
    bf16 = jnp.bfloat16
    everyone = n * nf
    row_blocks = nab // n
    near = everyone // 2
    hb = bs // HALVES
    chunks = row_chunks(bs)
    dma = pltpu.SemaphoreType.DMA
    first_update, second_update = pl.pallas_call(
        functools.partial(exchange_kernel, (n, nf, bs, sc, qc, nab, nbb)),
        out_shape=(
            jax.ShapeDtypeStruct((nab // nf, bs, nbb * bs // n), bf16),
            jax.ShapeDtypeStruct((rows, nbb * bs // nf), bf16),
        ),
        in_specs=[smem] + [hbm] * 9,
        out_specs=(anywhere, anywhere),
        scratch_shapes=[
            pltpu.VMEM((nbb, rows, bs), bf16),
            [pltpu.VMEM((nbb, 2, count, bs), bf16) for _, count in chunks],
            pltpu.VMEM((nf * sc * bs, bs), bf16),
            pltpu.VMEM((nf * sc * bs, bs), bf16),
            pltpu.VMEM((bs, nf * sc * bs), bf16),
            pltpu.VMEM((bs, nf * sc * bs), bf16),
            pltpu.SMEM((nf, sc, nab), jnp.int32),
            pltpu.SMEM((nf, sc, nbb), jnp.int32),
            pltpu.SMEM((nab,), jnp.int32),
            pltpu.SMEM((nbb,), jnp.int32),
            pltpu.VMEM((nab, bs), jnp.float32),
            pltpu.VMEM((nbb, bs), jnp.float32),
            [pltpu.VMEM((near, row_blocks, bs, bs), bf16) for _ in range(slots)],
            [pltpu.VMEM((near * slots, 2 * nf, count, bs), bf16) for _, count in chunks],
            [
                pltpu.VMEM((slots, nab // PLANES, PLANES * nf, count, bs), bf16)
                for _, count in chunks
            ],
            [pltpu.VMEM((nab, bs, cols * bs), jnp.float32) for cols in (qc, 1)],
            [pltpu.VMEM((nab, bs, cols * bs), jnp.float32) for cols in (qc, 1)],
            pltpu.VMEM((nbb, bs, bs), jnp.float32),
            [pltpu.VMEM((nab, bs, cols * bs), bf16) for cols in (qc, 1)],
            [pltpu.VMEM((HALVES, everyone, nf, hb, bs), bf16) for _ in range(slots)],
            [pltpu.VMEM((nbb, nf, hb, bs), bf16) for _ in range(HALVES)],
            pltpu.VMEM((bs, nbb * bs), bf16),
            dma,
            dma((2,)),
            dma((6,)),
            dma((nf - 1, 4)),
            dma((nf - 1, 4)),
            dma((len(chunks),)),
            dma((len(chunks),)),
            dma((slots,)),
            dma((len(chunks),)),
            dma((len(chunks),)),
            dma((slots, HALVES)),
            dma((HALVES,)),
            dma((nf,)),
            dma((nf,)),
            dma((nf,)),
            dma((nf,)),
        ],
        compiler_params=pltpu.CompilerParams(
            collective_id=0, has_side_effects=True, vmem_limit_bytes=61 * 1024 * 1024
        ),
    )(
        energy,
        vector,
        alpha_tiles.reshape(sc * bs, bs),
        beta_tiles.reshape(sc * bs, bs),
        alpha_pattern[0].T,
        beta_pattern[0].T,
        alpha_sector,
        beta_sector,
        alpha_diag.reshape(nab, bs),
        beta_diag.reshape(nbb, bs),
    )
    return first_update.reshape(nab * bs // nf, nbb * bs // n), second_update


def fits_split(*args):
    vector, alpha_tiles, _, _, _, alpha_sector, beta_sector = args[:7]
    n, nf = lax.axis_size("str"), lax.axis_size("fac")
    bs = alpha_tiles.shape[2]
    nab, nbb = alpha_sector.shape[0], beta_sector.shape[0]
    return (
        n % PLANES == 0
        and nf > 1
        and alpha_tiles.shape[0] == 1
        and bs % 128 == 0
        and nab == n * nf
        and nbb == 2 * n * nf
    )


def either_body(*args):
    return split_body(*args) if fits_split(*args) else body(*args)


def solution(mesh):
    return jax.shard_map(
        either_body,
        mesh=mesh,
        in_specs=(
            P("str", None),
            P("fac", None, None, None),
            P("fac", None, None),
            P("fac", None, None, None),
            P("fac", None, None),
            P(),
            P(),
            P(),
            P(),
            P(),
        ),
        out_specs=(P("fac", "str"), P("str", "fac")),
        check_vma=False,
    )
```

```python
import functools

import jax
import jax.numpy as jnp
from jax import lax
from jax.experimental import pallas as pl
from jax.experimental.pallas import tpu as pltpu
from jax.sharding import PartitionSpec as P

MESH = pl.DeviceIdType.MESH


def beta_apply(matrix, tile_set, pattern):
    height, width = matrix.shape
    slot_count, block_size = tile_set.shape[:2]
    stacked = tile_set.reshape(slot_count * block_size, block_size)

    def one(j, result):
        picked = jnp.concatenate(
            [
                lax.dynamic_slice_in_dim(matrix, pattern[j, s] * block_size, block_size, 1)
                for s in range(slot_count)
            ],
            axis=1,
        )
        image = jnp.dot(picked, stacked, preferred_element_type=jnp.float32)
        return lax.dynamic_update_slice_in_dim(result, image, j * block_size, 1)

    return lax.fori_loop(
        0, width // block_size, one, jnp.zeros((height, width), jnp.float32)
    )


def alpha_apply(matrix, tile_set, pattern):
    height, width = matrix.shape
    slot_count, block_size = tile_set.shape[:2]
    stacked = tile_set.transpose(1, 0, 2).reshape(block_size, slot_count * block_size)

    def one(i, result):
        picked = jnp.concatenate(
            [
                lax.dynamic_slice_in_dim(matrix, pattern[i, s] * block_size, block_size, 0)
                for s in range(slot_count)
            ],
            axis=0,
        )
        image = jnp.dot(stacked, picked, preferred_element_type=jnp.float32)
        return lax.dynamic_update_slice_in_dim(result, image, i * block_size, 0)

    return lax.fori_loop(
        0, height // block_size, one, jnp.zeros((height, width), jnp.float32)
    )


def precondition(
    sigma_part,
    row_start,
    col_start,
    block_size,
    alpha_sector,
    beta_sector,
    alpha_diag,
    beta_diag,
    energy,
):
    row_count, col_count = sigma_part.shape
    row_blocks = row_count // block_size
    col_blocks = col_count // block_size
    alpha_labels = lax.dynamic_slice_in_dim(alpha_sector, row_start // block_size, row_blocks)
    beta_labels = lax.dynamic_slice_in_dim(beta_sector, col_start // block_size, col_blocks)
    live_mask = (alpha_labels[:, None, None, None] == beta_labels[None, None, :, None]).astype(
        jnp.float32
    )
    masked = (
        sigma_part.reshape(row_blocks, block_size, col_blocks, block_size) * live_mask
    ).reshape(row_count, col_count)
    alpha_part = lax.dynamic_slice_in_dim(alpha_diag, row_start, row_count)
    beta_part = lax.dynamic_slice_in_dim(beta_diag, col_start, col_count)
    denominator = alpha_part[:, None] + beta_part[None, :] - energy[0]
    return (masked / denominator).astype(jnp.bfloat16)


def body(
    vector,
    alpha_tiles,
    alpha_pattern,
    beta_tiles,
    beta_pattern,
    alpha_sector,
    beta_sector,
    alpha_diag,
    beta_diag,
    energy,
):
    string_index = lax.axis_index("str")
    group_index = lax.axis_index("fac")
    string_count = lax.axis_size("str")
    block_size = alpha_tiles.shape[2]
    row_count = vector.shape[0]
    col_count = vector.shape[1] // string_count
    factor = 0
    image = beta_apply(vector, beta_tiles[factor], beta_pattern[factor]).astype(jnp.bfloat16)
    moved_one = lax.all_to_all(image, "str", split_axis=1, concat_axis=0, tiled=True)
    partial_value = alpha_apply(moved_one, alpha_tiles[factor], alpha_pattern[factor])
    share_rows = lax.psum_scatter(partial_value, "fac", scatter_dimension=0, tiled=True)
    first_update = precondition(
        share_rows,
        group_index * share_rows.shape[0],
        string_index * col_count,
        block_size,
        alpha_sector,
        beta_sector,
        alpha_diag,
        beta_diag,
        energy,
    )
    whole_first = lax.all_gather(first_update, "fac", axis=0, tiled=True)
    factor = 0
    back_image = alpha_apply(whole_first, alpha_tiles[factor], alpha_pattern[factor]).astype(
        jnp.bfloat16
    )
    returned_one = lax.all_to_all(back_image, "str", split_axis=0, concat_axis=1, tiled=True)
    partial_back = beta_apply(returned_one, beta_tiles[factor], beta_pattern[factor])
    share_cols = lax.psum_scatter(partial_back, "fac", scatter_dimension=1, tiled=True)
    second_update = precondition(
        share_cols,
        string_index * row_count,
        group_index * share_cols.shape[1],
        block_size,
        alpha_sector,
        beta_sector,
        alpha_diag,
        beta_diag,
        energy,
    )
    return (first_update, second_update)


PLANES = 4
HALVES = 4


def row_chunks(bs):
    shares = (3, 2, 1, 1, 1)
    unit = bs // sum(shares)
    starts = [unit * sum(shares[:x]) for x in range(len(shares))]
    return [(start, unit * share) for start, share in zip(starts, shares)]


def exchange_kernel(
    sizes,
    energy,
    vec,
    ta_in,
    tb_in,
    pa_in,
    pb_in,
    sa_in,
    sb_in,
    ad_in,
    bd_in,
    out1,
    out2,
    held,
    far,
    ta_all,
    tb_all,
    tiles_row,
    tiles_turned,
    pa,
    pb,
    sa,
    sb,
    near_index,
    far_index,
    adiag,
    bdiag,
    send1,
    send_far,
    recv_near,
    recv_far,
    total,
    scale,
    scale_last,
    first,
    send2,
    recv2,
    staged,
    held_sem,
    early_sem,
    late_sem,
    give_send,
    give_recv,
    raw_send,
    raw_recv,
    send1_sem,
    far_sem,
    near_sem,
    far_recv,
    send2_sem,
    recv2_sem,
    o1_send,
    o1_recv,
    o2_send,
    o2_recv,
):
    n, nf, bs, sc, qc, nab, nbb = sizes
    slots = qc + 1
    me = lax.axis_index("str")
    c = lax.axis_index("fac")
    everyone = n * nf
    lanes = n // PLANES
    per = lanes * nf
    row_blocks = nab // n
    plane_blocks = lanes * row_blocks
    half_rows = nab // nf
    half_blocks = nbb // nf
    kb = sc * bs
    hb = bs // HALVES
    plane = me // lanes
    lane = lax.rem(me, lanes)
    side = plane // 2
    inner = lax.rem(plane, 2) != side
    near = 2 * per
    near_count = 2 * per - 1
    bunch = 4 if per % 4 == 0 else 1
    own = 3 * per
    chunks = row_chunks(bs)

    def target(v):
        step = v // per
        u = lax.rem(v, per)
        high = lax.rem(side + 1 - step // 2, 2)
        low = lax.rem(lax.rem(plane, 2) + step + step // 2, 2)
        d = (2 * high + low) * lanes + lax.rem(lane + u // nf, lanes)
        return d, lax.rem(c + lax.rem(u, nf), nf)

    def partner(t):
        return t + t // own

    def column_of(d, f, q):
        if q < qc:
            return (d * nf + f) * qc + q
        mirror = (PLANES - 1 - d // lanes) * lanes + lax.rem(d, lanes)
        return (mirror * nf + f) * qc

    barrier = pltpu.get_barrier_semaphore()

    def block(index):
        return pl.ds(pl.multiple_of(index * bs, bs), bs)

    own_kb = pl.ds(pl.multiple_of(c * kb, kb), kb)
    early = [
        pltpu.make_async_copy(tb_in, tb_all.at[own_kb], early_sem.at[0]),
        pltpu.make_async_copy(pb_in, pb.at[c], early_sem.at[1]),
    ]
    late = [
        pltpu.make_async_copy(ta_in, ta_all.at[own_kb], late_sem.at[0]),
        pltpu.make_async_copy(ad_in, adiag, late_sem.at[1]),
        pltpu.make_async_copy(bd_in, bdiag, late_sem.at[2]),
        pltpu.make_async_copy(pa_in, pa.at[c], late_sem.at[3]),
        pltpu.make_async_copy(sa_in, sa, late_sem.at[4]),
        pltpu.make_async_copy(sb_in, sb, late_sem.at[5]),
    ]
    for copy in early:
        copy.start()

    def load(b, carry):
        pltpu.make_async_copy(vec.at[:, block(b)], held.at[b], held_sem).start()
        return carry

    lax.fori_loop(0, nbb, load, 0, unroll=8)

    def greet(t, carry):
        d, f = target(partner(t))
        pl.semaphore_signal(
            barrier, inc=1, device_id={"fac": f, "str": d}, device_id_type=MESH
        )
        return carry

    lax.fori_loop(0, everyone - 1, greet, 0)

    for copy in late:
        copy.start()

    def gives():
        for e in range(1, nf):
            f = lax.rem(c + e, nf)
            for x, (a, b) in enumerate(
                [
                    (tb_in, tb_all.at[own_kb]),
                    (ta_in, ta_all.at[own_kb]),
                    (pb_in, pb.at[c]),
                    (pa_in, pa.at[c]),
                ]
            ):
                yield pltpu.make_async_remote_copy(
                    src_ref=a,
                    dst_ref=b,
                    send_sem=give_send.at[e - 1, x],
                    recv_sem=give_recv.at[e - 1, x],
                    device_id={"fac": f, "str": me},
                    device_id_type=MESH,
                )

    def raw_copy(x):
        start, rows = chunks[x]
        return pltpu.make_async_remote_copy(
            src_ref=held.at[:, pl.ds(pl.multiple_of(c * bs + start, 16), rows)],
            dst_ref=far[x].at[:, lax.rem(plane, 2)],
            send_sem=raw_send.at[x],
            recv_sem=raw_recv.at[x],
            device_id={"fac": c, "str": (2 - side) * lanes + lane},
            device_id_type=MESH,
        )

    def column(ref, index):
        return jnp.transpose(jnp.broadcast_to(ref[pl.ds(index, 1), :], (bs, bs)))

    def alive(i, j):
        return jnp.where(sa[i] == sb[j], 1.0, 0.0).astype(jnp.float32)

    def near_images(q, base):
        picked = []
        for u in range(bunch):
            d, f = target(base + u)
            j = column_of(d, f, q)
            picked.append(jnp.concatenate([held[pb[c, s, j]] for s in range(sc)], axis=1))
        image = jnp.dot(
            jnp.concatenate(picked, axis=0),
            tb_all[own_kb, :],
            preferred_element_type=jnp.float32,
        ).astype(jnp.bfloat16)
        at = 0
        for u in range(bunch):
            for x in range(row_blocks):
                send1[q][base - near + u, x] = image[at : at + bs]
                at += bs

    def first_copy(q, v, x, stay=False):
        src = send1[q].at[v - near, x]
        level = lax.rem(plane, 2) * nf + c
        dst = recv_near.at[q, (lane * row_blocks + x) * 2 * nf + level]
        if stay:
            return pltpu.make_async_copy(src, dst, near_sem)
        d, f = target(v)
        return pltpu.make_async_remote_copy(
            src_ref=src,
            dst_ref=dst,
            send_sem=send1_sem.at[q],
            recv_sem=near_sem,
            device_id={"fac": f, "str": d},
            device_id_type=MESH,
        )

    def first_copies(q, base):
        for x in range(row_blocks):

            @pl.when(base == own)
            def _(x=x):
                first_copy(q, own, x, stay=True).start()

            @pl.when(base != own)
            def _(x=x):
                first_copy(q, base, x).start()

            for u in range(1, bunch):
                first_copy(q, base + u, x).start()

    pltpu.make_async_copy(held, held, held_sem).wait()
    for copy in early:
        copy.wait()
    pl.semaphore_wait(barrier, everyone - 1)
    raw_copy(0).start()
    for copy in gives():
        copy.start()

    raw_copy(1).start()
    for q in range(qc):

        def step_one(g, carry, q=q):
            near_images(q, near + g * bunch)
            first_copies(q, near + g * bunch)
            return carry

        lax.fori_loop(0, 2 * per // bunch, step_one, 0)

    extra_base = jnp.where(inner, own, near)

    def step_extra(g, carry):
        near_images(qc, extra_base + g * bunch)
        first_copies(qc, extra_base + g * bunch)
        return carry

    lax.fori_loop(0, per // bunch, step_extra, 0)

    for copy in late:
        copy.wait()
    for copy in gives():
        copy.wait()
    for x in range(nf * sc):
        tiles_row[:, x * bs : (x + 1) * bs] = ta_all[x * bs : (x + 1) * bs, :]

    width = nf * kb
    spot = lax.broadcasted_iota(jnp.int32, (width, width), 1)
    origin = jnp.zeros((width, width), jnp.int32)
    for start, rows in chunks:
        inside = spot - start * nf * sc
        source = inside // rows * bs + start + lax.rem(inside, rows)
        origin = jnp.where(inside >= 0, source, origin)
    turn = jnp.where(
        lax.broadcasted_iota(jnp.int32, (width, width), 0) == origin, 1.0, 0.0
    ).astype(jnp.bfloat16)
    tiles_turned[...] = jnp.dot(
        tiles_row[...], turn, preferred_element_type=jnp.float32
    ).astype(jnp.bfloat16)

    def scale_columns(q):
        j = column_of(me, c, q)

        def one(i, carry):
            denominator = column(adiag, i) + bdiag[pl.ds(j, 1), :] - energy[0]
            value = alive(i, j) / denominator
            if q < qc:
                scale[0][i, :, q * bs : (q + 1) * bs] = value
            else:
                scale[1][i] = value
            return carry

        lax.fori_loop(0, nab, one, 0)

    for q in range(qc):
        scale_columns(q)

    @pl.when(inner)
    def _():
        scale_columns(qc)

    def far_images(x, base, count, qs):
        rows = chunks[x][1]
        places = [target(base + u) for u in range(count)]
        for k in range(nf):
            picked = []
            for d, f in places:
                for q in qs:
                    j = column_of(d, f, q)
                    picked.append(
                        jnp.concatenate(
                            [far[x][pb[k, s, j]].reshape(2 * rows, bs) for s in range(sc)],
                            axis=1,
                        )
                    )
            image = jnp.dot(
                jnp.concatenate(picked, axis=0),
                tb_all[k * kb : (k + 1) * kb, :],
                preferred_element_type=jnp.float32,
            ).astype(jnp.bfloat16)
            at = 0
            for u in range(count):
                for q in qs:
                    for z in range(2):
                        send_far[x][(base - near + u) * slots + q, z * nf + k] = image[
                            at : at + rows
                        ]
                        at += rows

    def far_copy(x, v, q, stay=False):
        src = send_far[x].at[(v - near) * slots + q]
        dst = recv_far[x].at[q, pl.ds((lane * row_blocks + c) * 2 * nf, 2 * nf)]
        if stay:
            return pltpu.make_async_copy(src, dst, far_recv.at[x])
        d, f = target(v)
        return pltpu.make_async_remote_copy(
            src_ref=src,
            dst_ref=dst,
            send_sem=far_sem.at[x],
            recv_sem=far_recv.at[x],
            device_id={"fac": f, "str": d},
            device_id_type=MESH,
        )

    def far_step(x):
        def step(g, carry):
            base = near + g * bunch
            far_images(x, base, bunch, tuple(range(qc)))
            for q in range(qc):

                @pl.when(base == own)
                def _(q=q):
                    far_copy(x, own, q, stay=True).start()

                @pl.when(base != own)
                def _(q=q):
                    far_copy(x, base, q).start()

                for u in range(1, bunch):
                    far_copy(x, base + u, q).start()
            return carry

        lax.fori_loop(0, 2 * per // bunch, step, 0)
        far_images(x, own, per, (qc,))
        far_copy(x, own, qc, stay=True).start()
        for u in range(1, per):
            far_copy(x, own + u, qc).start()

    last = len(chunks) - 1

    nothing = plane_blocks * 2 * nf
    for q in range(slots):
        recv_near[q, nothing] = jnp.zeros((bs, bs), jnp.bfloat16)
        for x, (_, rows) in enumerate(chunks):
            recv_far[x][q, nothing] = jnp.zeros((rows, bs), jnp.bfloat16)

    def number(i, carry):
        for k in range(nf):
            for s in range(sc):
                p = pa[k, s, i]
                level = lax.div(p, plane_blocks)
                place = (lax.rem(p, plane_blocks) * 2 + lax.rem(level, 2)) * nf + k
                here = lax.div(level, 2) == side
                near_index[k, s, i] = jnp.where(here, place, nothing)
                far_index[k, s, i] = jnp.where(here, nothing, place)
        return carry

    lax.fori_loop(0, nab, number, 0)

    def partial(x, i, cols):
        parts = []
        source, index = (recv_near, near_index) if x < 0 else (recv_far[x], far_index)
        for k in range(nf):
            for s in range(sc):
                at = index[k, s, i]
                parts.append(jnp.concatenate([source[q, at] for q in cols], axis=1))
        if x < 0:
            tiles = tiles_row[...]
        else:
            start, rows = chunks[x]
            tiles = tiles_turned[:, start * nf * sc : (start + rows) * nf * sc]
        return jnp.dot(
            tiles, jnp.concatenate(parts, axis=0), preferred_element_type=jnp.float32
        )

    def accumulate(x, which):
        cols = tuple(range(qc)) if which == 0 else (qc,)

        def one(i, carry):
            value = partial(x, i, cols)
            if x >= 0:
                value = value + total[which][i]
            if x < last:
                total[which][i] = value
            else:
                first[which][i] = (value * scale[which][i]).astype(jnp.bfloat16)
            return carry

        lax.fori_loop(0, nab, one, 0, unroll=4)

    def landed(x):
        source, sem = (recv_near, near_sem) if x < 0 else (recv_far[x], far_recv.at[x])

        def wait(count):
            some = source.at[pl.ds(0, count), pl.ds(0, nothing)]
            pltpu.make_async_copy(some, some, sem).wait()

        @pl.when(inner)
        def _():
            wait(slots)

        @pl.when(jnp.logical_not(inner))
        def _():
            wait(qc)

    schedule = [[] for _ in chunks]
    for y in range(-1, last):
        schedule[min(y + 2, last)].append(y)
    later = (last - 2, last - 1)

    for x in range(len(chunks)):

        @pl.when(inner)
        def _(x=x):
            pltpu.make_async_copy(far[x], far[x], raw_recv.at[x]).wait()

        raw_copy(x).wait_send()
        if x + 2 < len(chunks):
            raw_copy(x + 2).start()

        @pl.when(inner)
        def _(x=x):
            far_step(x)

        for y in schedule[x]:
            landed(y)
            accumulate(y, 0)

            @pl.when(inner)
            def _(x=x, y=y):
                if y not in later:
                    accumulate(y, 1)

    landed(last)
    accumulate(last, 0)

    def second_copy(q, h, v, stay=False):
        src = send2[q].at[h, v]
        dst = recv2[h].at[column_of(me, c, q)]
        if stay:
            return pltpu.make_async_copy(src, dst, recv2_sem.at[h])
        d, f = target(v)
        return pltpu.make_async_remote_copy(
            src_ref=src,
            dst_ref=dst,
            send_sem=send2_sem.at[q, h],
            recv_sem=recv2_sem.at[h],
            device_id={"fac": f, "str": d},
            device_id_type=MESH,
        )

    def share_copy(e):
        f = lax.rem(c + e, nf)
        src = first[0].at[pl.ds(f * half_rows, half_rows)]
        dst = out1.at[:, :, pl.ds(pl.multiple_of(c * qc * bs, bs), qc * bs)]
        if e == 0:
            return pltpu.make_async_copy(src, dst, o1_send.at[e])
        return pltpu.make_async_remote_copy(
            src_ref=src,
            dst_ref=dst,
            send_sem=o1_send.at[e],
            recv_sem=o1_recv.at[e],
            device_id={"fac": f, "str": me},
            device_id_type=MESH,
        )

    def begin(q):
        return jnp.where(inner, near, 0) if q == 0 else near if q == qc else 0

    def alpha_images(v, which, cols):
        d, f = target(v)
        i = d * nf + f
        for k in range(nf):
            picked = jnp.concatenate([first[which][pa[k, s, i]] for s in range(sc)], axis=0)
            image = jnp.dot(
                tiles_row[:, k * kb : (k + 1) * kb],
                picked,
                preferred_element_type=jnp.float32,
            ).astype(jnp.bfloat16)
            for y, q in enumerate(cols):
                for h in range(HALVES):
                    send2[q][h, v, k] = image[h * hb : (h + 1) * hb, y * bs : (y + 1) * bs]

    def second_copies(q, h, base):
        @pl.when(base == own)
        def _():
            second_copy(q, h, own, stay=True).start()

        @pl.when(base != own)
        def _():
            second_copy(q, h, base).start()

        for u in range(1, bunch):
            second_copy(q, h, base + u).start()

    def images_out(which, cols):
        def step_two(g, carry):
            base = g * bunch
            for u in range(bunch):
                alpha_images(base + u, which, cols)
            for q in reversed(cols):

                @pl.when(base >= begin(q))
                def _(q=q):
                    second_copies(q, 0, base)

            return carry

        lax.fori_loop((near if which else 0) // bunch, everyone // bunch, step_two, 0)

    order = list(reversed(range(qc)))
    images_out(0, tuple(range(qc)))
    for e in range(nf):
        share_copy(e).start()

    @pl.when(inner)
    def _():
        for y in later + (last,):
            accumulate(y, 1)
        images_out(1, (qc,))

    def send_rest(q, h):
        def rest(g, carry):
            second_copies(q, h, g * bunch)
            return carry

        lax.fori_loop(begin(q) // bunch, everyone // bunch, rest, 0)

    for h in range(1, HALVES):
        for q in order:
            send_rest(q, h)

        @pl.when(inner)
        def _(h=h):
            send_rest(qc, h)

    mine = me * nf + c
    group = max(g for g in (1, 2, 4, 8) if half_blocks % g == 0)
    pieces = half_blocks // group

    def scale_row(j, carry):
        denominator = column(adiag, mine) + bdiag[pl.ds(j, 1), :] - energy[0]
        scale_last[j] = alive(mine, j) / denominator
        return carry

    lax.fori_loop(0, nbb, scale_row, 0)

    def sigma_two(h, first_block):
        rows = []
        for g in range(group):
            parts = [
                recv2[h][pb[k, s, first_block + g], k] for k in range(nf) for s in range(sc)
            ]
            rows.append(jnp.concatenate(parts, axis=1))
        sigma = jnp.dot(
            jnp.concatenate(rows, axis=0), tb_all[...], preferred_element_type=jnp.float32
        )
        for g in range(group):
            j = first_block + g
            value = sigma[g * hb : (g + 1) * hb] * scale_last[j, h * hb : (h + 1) * hb]
            staged[h * hb : (h + 1) * hb, block(j)] = value.astype(jnp.bfloat16)

    def piece_copy(h, e, x):
        f = lax.rem(c + e, nf)
        src_start = pl.multiple_of((f * half_blocks + x * group) * bs, bs)
        dst_start = pl.multiple_of(x * group * bs, bs)
        src = staged.at[pl.ds(h * hb, hb), pl.ds(src_start, group * bs)]
        dst = out2.at[
            pl.ds(pl.multiple_of(c * bs + h * hb, hb), hb), pl.ds(dst_start, group * bs)
        ]
        if e == 0:
            return pltpu.make_async_copy(src, dst, o2_send.at[e])
        return pltpu.make_async_remote_copy(
            src_ref=src,
            dst_ref=dst,
            send_sem=o2_send.at[e],
            recv_sem=o2_recv.at[e],
            device_id={"fac": f, "str": me},
            device_id_type=MESH,
        )

    for h in range(HALVES):
        pltpu.make_async_copy(recv2[h], recv2[h], recv2_sem.at[h]).wait()
        for e in reversed(range(nf)):

            def finish(x, carry, e=e, h=h):
                sigma_two(h, lax.rem(c + e, nf) * half_blocks + x * group)
                piece_copy(h, e, x).start()
                return carry

            lax.fori_loop(0, pieces, finish, 0)

    def second_sent(q, h, count):
        sent = send2[q].at[h, pl.ds(0, count)]
        pltpu.make_async_copy(sent, sent, send2_sem.at[q, h]).wait()

    def near_sent(q, count):
        sent = send1[q].at[pl.ds(0, count)]
        pltpu.make_async_copy(sent, sent, send1_sem.at[q]).wait()

    for q in range(qc):
        near_sent(q, near_count)
    for e in range(nf):
        share_copy(e).wait()

    @pl.when(inner)
    def _():
        near_sent(qc, per - 1)
        for x in range(len(chunks)):
            some = send_far[x].at[pl.ds(0, near_count * qc + per - 1)]
            pltpu.make_async_copy(some, some, far_sem.at[x]).wait()
        for h in range(HALVES):
            for q in range(slots):
                second_sent(q, h, near_count if q in (0, qc) else everyone - 1)

    @pl.when(jnp.logical_not(inner))
    def _():
        near_sent(qc, per)
        for h in range(HALVES):
            for q in range(qc):
                second_sent(q, h, everyone - 1)

    for e in range(nf):
        sent = staged.at[:, pl.ds(0, half_blocks * bs)]
        pltpu.make_async_copy(sent, sent, o2_send.at[e]).wait()
        if e > 0:
            pltpu.make_async_copy(sent, sent, o2_recv.at[e]).wait()


def split_body(
    vector,
    alpha_tiles,
    alpha_pattern,
    beta_tiles,
    beta_pattern,
    alpha_sector,
    beta_sector,
    alpha_diag,
    beta_diag,
    energy,
):
    n = lax.axis_size("str")
    nf = lax.axis_size("fac")
    sc, bs = alpha_tiles.shape[1], alpha_tiles.shape[2]
    nab, nbb = alpha_sector.shape[0], beta_sector.shape[0]
    qc = nbb // (n * nf)
    slots = qc + 1
    rows = vector.shape[0]
    smem = pl.BlockSpec(memory_space=pltpu.SMEM)
    anywhere = pl.BlockSpec(memory_space=pl.ANY)
    hbm = pl.BlockSpec(memory_space=pltpu.HBM)
    bf16 = jnp.bfloat16
    everyone = n * nf
    row_blocks = nab // n
    near = everyone // 2
    hb = bs // HALVES
    chunks = row_chunks(bs)
    dma = pltpu.SemaphoreType.DMA
    first_update, second_update = pl.pallas_call(
        functools.partial(exchange_kernel, (n, nf, bs, sc, qc, nab, nbb)),
        out_shape=(
            jax.ShapeDtypeStruct((nab // nf, bs, nbb * bs // n), bf16),
            jax.ShapeDtypeStruct((rows, nbb * bs // nf), bf16),
        ),
        in_specs=[smem] + [hbm] * 9,
        out_specs=(anywhere, anywhere),
        scratch_shapes=[
            pltpu.VMEM((nbb, rows, bs), bf16),
            [pltpu.VMEM((nbb, 2, count, bs), bf16) for _, count in chunks],
            pltpu.VMEM((nf * sc * bs, bs), bf16),
            pltpu.VMEM((nf * sc * bs, bs), bf16),
            pltpu.VMEM((bs, nf * sc * bs), bf16),
            pltpu.VMEM((bs, nf * sc * bs), bf16),
            pltpu.SMEM((nf, sc, nab), jnp.int32),
            pltpu.SMEM((nf, sc, nbb), jnp.int32),
            pltpu.SMEM((nab,), jnp.int32),
            pltpu.SMEM((nbb,), jnp.int32),
            pltpu.SMEM((nf, sc, nab), jnp.int32),
            pltpu.SMEM((nf, sc, nab), jnp.int32),
            pltpu.VMEM((nab, bs), jnp.float32),
            pltpu.VMEM((nbb, bs), jnp.float32),
            [pltpu.VMEM((near, row_blocks, bs, bs), bf16) for _ in range(slots)],
            [pltpu.VMEM((near * slots, 2 * nf, count, bs), bf16) for _, count in chunks],
            pltpu.VMEM((slots, nab // PLANES * 2 * nf + 1, bs, bs), bf16),
            [
                pltpu.VMEM((slots, nab // PLANES * 2 * nf + 1, count, bs), bf16)
                for _, count in chunks
            ],
            [pltpu.VMEM((nab, bs, cols * bs), jnp.float32) for cols in (qc, 1)],
            [pltpu.VMEM((nab, bs, cols * bs), jnp.float32) for cols in (qc, 1)],
            pltpu.VMEM((nbb, bs, bs), jnp.float32),
            [pltpu.VMEM((nab, bs, cols * bs), bf16) for cols in (qc, 1)],
            [pltpu.VMEM((HALVES, everyone, nf, hb, bs), bf16) for _ in range(slots)],
            [pltpu.VMEM((nbb, nf, hb, bs), bf16) for _ in range(HALVES)],
            pltpu.VMEM((bs, nbb * bs), bf16),
            dma,
            dma((2,)),
            dma((6,)),
            dma((nf - 1, 4)),
            dma((nf - 1, 4)),
            dma((len(chunks),)),
            dma((len(chunks),)),
            dma((slots,)),
            dma((len(chunks),)),
            dma,
            dma((len(chunks),)),
            dma((slots, HALVES)),
            dma((HALVES,)),
            dma((nf,)),
            dma((nf,)),
            dma((nf,)),
            dma((nf,)),
        ],
        compiler_params=pltpu.CompilerParams(
            collective_id=0, has_side_effects=True, vmem_limit_bytes=61 * 1024 * 1024
        ),
    )(
        energy,
        vector,
        alpha_tiles.reshape(sc * bs, bs),
        beta_tiles.reshape(sc * bs, bs),
        alpha_pattern[0].T,
        beta_pattern[0].T,
        alpha_sector,
        beta_sector,
        alpha_diag.reshape(nab, bs),
        beta_diag.reshape(nbb, bs),
    )
    return first_update.reshape(nab * bs // nf, nbb * bs // n), second_update


def fits_split(*args):
    vector, alpha_tiles, _, _, _, alpha_sector, beta_sector = args[:7]
    n, nf = lax.axis_size("str"), lax.axis_size("fac")
    bs = alpha_tiles.shape[2]
    nab, nbb = alpha_sector.shape[0], beta_sector.shape[0]
    return (
        n % PLANES == 0
        and nf > 1
        and alpha_tiles.shape[0] == 1
        and bs % 128 == 0
        and nab == n * nf
        and nbb == 2 * n * nf
    )


def either_body(*args):
    return split_body(*args) if fits_split(*args) else body(*args)


def solution(mesh):
    return jax.shard_map(
        either_body,
        mesh=mesh,
        in_specs=(
            P("str", None),
            P("fac", None, None, None),
            P("fac", None, None),
            P("fac", None, None, None),
            P("fac", None, None),
            P(),
            P(),
            P(),
            P(),
            P(),
        ),
        out_specs=(P("fac", "str"), P("str", "fac")),
        check_vma=False,
    )
```

```python
import functools

import jax
import jax.numpy as jnp
from jax import lax
from jax.experimental import pallas as pl
from jax.experimental.pallas import tpu as pltpu
from jax.sharding import PartitionSpec as P

MESH = pl.DeviceIdType.MESH


def beta_apply(matrix, tile_set, pattern):
    height, width = matrix.shape
    slot_count, block_size = tile_set.shape[:2]
    stacked = tile_set.reshape(slot_count * block_size, block_size)

    def one(j, result):
        picked = jnp.concatenate(
            [
                lax.dynamic_slice_in_dim(matrix, pattern[j, s] * block_size, block_size, 1)
                for s in range(slot_count)
            ],
            axis=1,
        )
        image = jnp.dot(picked, stacked, preferred_element_type=jnp.float32)
        return lax.dynamic_update_slice_in_dim(result, image, j * block_size, 1)

    return lax.fori_loop(
        0, width // block_size, one, jnp.zeros((height, width), jnp.float32)
    )


def alpha_apply(matrix, tile_set, pattern):
    height, width = matrix.shape
    slot_count, block_size = tile_set.shape[:2]
    stacked = tile_set.transpose(1, 0, 2).reshape(block_size, slot_count * block_size)

    def one(i, result):
        picked = jnp.concatenate(
            [
                lax.dynamic_slice_in_dim(matrix, pattern[i, s] * block_size, block_size, 0)
                for s in range(slot_count)
            ],
            axis=0,
        )
        image = jnp.dot(stacked, picked, preferred_element_type=jnp.float32)
        return lax.dynamic_update_slice_in_dim(result, image, i * block_size, 0)

    return lax.fori_loop(
        0, height // block_size, one, jnp.zeros((height, width), jnp.float32)
    )


def precondition(
    sigma_part,
    row_start,
    col_start,
    block_size,
    alpha_sector,
    beta_sector,
    alpha_diag,
    beta_diag,
    energy,
):
    row_count, col_count = sigma_part.shape
    row_blocks = row_count // block_size
    col_blocks = col_count // block_size
    alpha_labels = lax.dynamic_slice_in_dim(alpha_sector, row_start // block_size, row_blocks)
    beta_labels = lax.dynamic_slice_in_dim(beta_sector, col_start // block_size, col_blocks)
    live_mask = (alpha_labels[:, None, None, None] == beta_labels[None, None, :, None]).astype(
        jnp.float32
    )
    masked = (
        sigma_part.reshape(row_blocks, block_size, col_blocks, block_size) * live_mask
    ).reshape(row_count, col_count)
    alpha_part = lax.dynamic_slice_in_dim(alpha_diag, row_start, row_count)
    beta_part = lax.dynamic_slice_in_dim(beta_diag, col_start, col_count)
    denominator = alpha_part[:, None] + beta_part[None, :] - energy[0]
    return (masked / denominator).astype(jnp.bfloat16)


def body(
    vector,
    alpha_tiles,
    alpha_pattern,
    beta_tiles,
    beta_pattern,
    alpha_sector,
    beta_sector,
    alpha_diag,
    beta_diag,
    energy,
):
    string_index = lax.axis_index("str")
    group_index = lax.axis_index("fac")
    string_count = lax.axis_size("str")
    block_size = alpha_tiles.shape[2]
    row_count = vector.shape[0]
    col_count = vector.shape[1] // string_count
    factor = 0
    image = beta_apply(vector, beta_tiles[factor], beta_pattern[factor]).astype(jnp.bfloat16)
    moved_one = lax.all_to_all(image, "str", split_axis=1, concat_axis=0, tiled=True)
    partial_value = alpha_apply(moved_one, alpha_tiles[factor], alpha_pattern[factor])
    share_rows = lax.psum_scatter(partial_value, "fac", scatter_dimension=0, tiled=True)
    first_update = precondition(
        share_rows,
        group_index * share_rows.shape[0],
        string_index * col_count,
        block_size,
        alpha_sector,
        beta_sector,
        alpha_diag,
        beta_diag,
        energy,
    )
    whole_first = lax.all_gather(first_update, "fac", axis=0, tiled=True)
    factor = 0
    back_image = alpha_apply(whole_first, alpha_tiles[factor], alpha_pattern[factor]).astype(
        jnp.bfloat16
    )
    returned_one = lax.all_to_all(back_image, "str", split_axis=0, concat_axis=1, tiled=True)
    partial_back = beta_apply(returned_one, beta_tiles[factor], beta_pattern[factor])
    share_cols = lax.psum_scatter(partial_back, "fac", scatter_dimension=1, tiled=True)
    second_update = precondition(
        share_cols,
        string_index * row_count,
        group_index * share_cols.shape[1],
        block_size,
        alpha_sector,
        beta_sector,
        alpha_diag,
        beta_diag,
        energy,
    )
    return (first_update, second_update)


PLANES = 4
HALVES = 4
WINDOW = 3


def row_chunks(bs):
    shares = (1, 1, 2, 1, 1, 1, 1)
    unit = bs // sum(shares)
    starts = [unit * sum(shares[:x]) for x in range(len(shares))]
    return [(start, unit * share) for start, share in zip(starts, shares)]


def exchange_kernel(
    sizes,
    energy,
    vec,
    ta_in,
    tb_in,
    pa_in,
    pb_in,
    sa_in,
    sb_in,
    ad_in,
    bd_in,
    out1,
    out2,
    held,
    far,
    ta_all,
    tb_all,
    tiles_row,
    tiles_turned,
    pa,
    pb,
    sa,
    sb,
    near_index,
    far_index,
    adiag,
    bdiag,
    send1,
    send_far,
    recv_near,
    recv_far,
    total,
    scale,
    scale_last,
    first,
    send2,
    recv2,
    staged,
    held_sem,
    early_sem,
    late_sem,
    give_send,
    give_recv,
    raw_send,
    raw_recv,
    send1_sem,
    far_sem,
    near_sem,
    far_recv,
    send2_sem,
    recv2_sem,
    o1_send,
    o1_recv,
    o2_send,
    o2_recv,
):
    n, nf, bs, sc, qc, nab, nbb = sizes
    slots = qc + 1
    me = lax.axis_index("str")
    c = lax.axis_index("fac")
    everyone = n * nf
    lanes = n // PLANES
    per = lanes * nf
    row_blocks = nab // n
    plane_blocks = lanes * row_blocks
    half_rows = nab // nf
    half_blocks = nbb // nf
    kb = sc * bs
    hb = bs // HALVES
    plane = me // lanes
    lane = lax.rem(me, lanes)
    side = plane // 2
    inner = lax.rem(plane, 2) != side
    more = jnp.logical_or(inner, c == 0)
    near = 2 * per
    near_count = 2 * per - 1
    bunch = 4 if per % 4 == 0 else 1
    own = 3 * per
    chunks = row_chunks(bs)

    def target(v):
        step = v // per
        u = lax.rem(v, per)
        high = lax.rem(side + 1 - step // 2, 2)
        low = lax.rem(lax.rem(plane, 2) + step + step // 2, 2)
        d = (2 * high + low) * lanes + lax.rem(lane + u // nf, lanes)
        return d, lax.rem(c + lax.rem(u, nf), nf)

    def partner(t):
        return t + t // own

    def column_of(d, f, q):
        if q < qc:
            return (d * nf + f) * qc + q
        mirror = (PLANES - 1 - d // lanes) * lanes + lax.rem(d, lanes)
        return (mirror * nf + f) * qc

    barrier = pltpu.get_barrier_semaphore()

    def block(index):
        return pl.ds(pl.multiple_of(index * bs, bs), bs)

    own_kb = pl.ds(pl.multiple_of(c * kb, kb), kb)
    early = [
        pltpu.make_async_copy(tb_in, tb_all.at[own_kb], early_sem.at[0]),
        pltpu.make_async_copy(pb_in, pb.at[c], early_sem.at[1]),
    ]
    late = [
        pltpu.make_async_copy(ta_in, ta_all.at[own_kb], late_sem.at[0]),
        pltpu.make_async_copy(ad_in, adiag, late_sem.at[1]),
        pltpu.make_async_copy(bd_in, bdiag, late_sem.at[2]),
        pltpu.make_async_copy(pa_in, pa.at[c], late_sem.at[3]),
        pltpu.make_async_copy(sa_in, sa, late_sem.at[4]),
        pltpu.make_async_copy(sb_in, sb, late_sem.at[5]),
    ]
    for copy in early:
        copy.start()

    def load(b, carry):
        pltpu.make_async_copy(vec.at[:, block(b)], held.at[b], held_sem).start()
        return carry

    lax.fori_loop(0, nbb, load, 0, unroll=8)

    def greet(t, carry):
        d, f = target(partner(t))
        pl.semaphore_signal(
            barrier, inc=1, device_id={"fac": f, "str": d}, device_id_type=MESH
        )
        return carry

    lax.fori_loop(0, everyone - 1, greet, 0)

    for copy in late:
        copy.start()

    def gives():
        for e in range(1, nf):
            f = lax.rem(c + e, nf)
            for x, (a, b) in enumerate(
                [
                    (tb_in, tb_all.at[own_kb]),
                    (ta_in, ta_all.at[own_kb]),
                    (pb_in, pb.at[c]),
                    (pa_in, pa.at[c]),
                ]
            ):
                yield pltpu.make_async_remote_copy(
                    src_ref=a,
                    dst_ref=b,
                    send_sem=give_send.at[e - 1, x],
                    recv_sem=give_recv.at[e - 1, x],
                    device_id={"fac": f, "str": me},
                    device_id_type=MESH,
                )

    def raw_copy(x):
        start, rows = chunks[x]
        return pltpu.make_async_remote_copy(
            src_ref=held.at[:, pl.ds(pl.multiple_of(c * bs + start, 16), rows)],
            dst_ref=far[x].at[:, lax.rem(plane, 2)],
            send_sem=raw_send.at[x],
            recv_sem=raw_recv.at[x],
            device_id={"fac": c, "str": (2 - side) * lanes + lane},
            device_id_type=MESH,
        )

    def column(ref, index):
        return jnp.transpose(jnp.broadcast_to(ref[pl.ds(index, 1), :], (bs, bs)))

    def alive(i, j):
        return jnp.where(sa[i] == sb[j], 1.0, 0.0).astype(jnp.float32)

    def kind(q):
        return int(q == qc)

    def near_images(q, targets):
        picked = []
        for v in targets:
            d, f = target(v)
            j = column_of(d, f, q)
            picked.append(jnp.concatenate([held[pb[c, s, j]] for s in range(sc)], axis=1))
        image = jnp.dot(
            jnp.concatenate(picked, axis=0),
            tb_all[own_kb, :],
            preferred_element_type=jnp.float32,
        ).astype(jnp.bfloat16)
        at = 0
        for v in targets:
            for x in range(row_blocks):
                send1[q][v - near, x] = image[at : at + bs]
                at += bs

    def first_copy(q, v, x, stay=False):
        src = send1[q].at[v - near, x]
        level = lax.rem(plane, 2) * nf + c
        dst = recv_near[kind(q)].at[
            0 if kind(q) else q, (lane * row_blocks + x) * 2 * nf + level
        ]
        if stay:
            return pltpu.make_async_copy(src, dst, near_sem.at[kind(q)])
        d, f = target(v)
        return pltpu.make_async_remote_copy(
            src_ref=src,
            dst_ref=dst,
            send_sem=send1_sem.at[q],
            recv_sem=near_sem.at[kind(q)],
            device_id={"fac": f, "str": d},
            device_id_type=MESH,
        )

    def bunch_of(base):
        return [base + u for u in range(bunch)]

    def first_copies(q, targets):
        for x in range(row_blocks):

            @pl.when(targets[0] == own)
            def _(x=x):
                first_copy(q, own, x, stay=True).start()

            @pl.when(targets[0] != own)
            def _(x=x):
                first_copy(q, targets[0], x).start()

            for v in targets[1:]:
                first_copy(q, v, x).start()

    pltpu.make_async_copy(held, held, held_sem).wait()
    for copy in early:
        copy.wait()
    pl.semaphore_wait(barrier, everyone - 1)
    raw_copy(0).start()
    for copy in gives():
        copy.start()

    for x in range(1, WINDOW):
        raw_copy(x).start()
    for q in range(qc):

        def step_one(g, carry, q=q):
            near_images(q, bunch_of(near + g * bunch))
            first_copies(q, bunch_of(near + g * bunch))
            return carry

        lax.fori_loop(0, 2 * per // bunch, step_one, 0)

    extra_base = jnp.where(inner, own, near)

    def step_extra(g, carry):
        near_images(qc, bunch_of(extra_base + g * bunch))
        first_copies(qc, bunch_of(extra_base + g * bunch))
        return carry

    lax.fori_loop(0, per // bunch, step_extra, 0)

    def outer_extras(base):
        return [base + nf * w + lax.rem(nf - c, nf) for w in range(lanes)]

    outer_base = jnp.where(inner, near, own)
    near_images(qc, outer_extras(outer_base))
    first_copies(qc, outer_extras(outer_base))

    for copy in late:
        copy.wait()
    for copy in gives():
        copy.wait()
    for x in range(nf * sc):
        tiles_row[:, x * bs : (x + 1) * bs] = ta_all[x * bs : (x + 1) * bs, :]

    width = nf * kb
    spot = lax.broadcasted_iota(jnp.int32, (width, width), 1)
    origin = jnp.zeros((width, width), jnp.int32)
    for start, rows in chunks:
        inside = spot - start * nf * sc
        source = inside // rows * bs + start + lax.rem(inside, rows)
        origin = jnp.where(inside >= 0, source, origin)
    turn = jnp.where(
        lax.broadcasted_iota(jnp.int32, (width, width), 0) == origin, 1.0, 0.0
    ).astype(jnp.bfloat16)
    tiles_turned[...] = jnp.dot(
        tiles_row[...], turn, preferred_element_type=jnp.float32
    ).astype(jnp.bfloat16)

    def scale_columns(q):
        j = column_of(me, c, q)

        def one(i, carry):
            denominator = column(adiag, i) + bdiag[pl.ds(j, 1), :] - energy[0]
            value = alive(i, j) / denominator
            if q < qc:
                scale[0][i, :, q * bs : (q + 1) * bs] = value
            else:
                scale[1][i] = value
            return carry

        lax.fori_loop(0, nab, one, 0)

    for q in range(qc):
        scale_columns(q)

    @pl.when(more)
    def _():
        scale_columns(qc)

    def far_images(x, targets, qs):
        rows = chunks[x][1]
        places = [target(v) for v in targets]
        for k in range(nf):
            picked = []
            for d, f in places:
                for q in qs:
                    j = column_of(d, f, q)
                    picked.append(
                        jnp.concatenate(
                            [far[x][pb[k, s, j]].reshape(2 * rows, bs) for s in range(sc)],
                            axis=1,
                        )
                    )
            image = jnp.dot(
                jnp.concatenate(picked, axis=0),
                tb_all[k * kb : (k + 1) * kb, :],
                preferred_element_type=jnp.float32,
            ).astype(jnp.bfloat16)
            at = 0
            for v in targets:
                for q in qs:
                    for z in range(2):
                        send_far[x][(v - near) * slots + q, z * nf + k] = image[
                            at : at + rows
                        ]
                        at += rows

    def far_copy(x, v, q, stay=False):
        src = send_far[x].at[(v - near) * slots + q]
        dst = recv_far[x][kind(q)].at[
            0 if kind(q) else q, pl.ds((lane * row_blocks + c) * 2 * nf, 2 * nf)
        ]
        if stay:
            return pltpu.make_async_copy(src, dst, far_recv.at[x, kind(q)])
        d, f = target(v)
        return pltpu.make_async_remote_copy(
            src_ref=src,
            dst_ref=dst,
            send_sem=far_sem.at[x],
            recv_sem=far_recv.at[x, kind(q)],
            device_id={"fac": f, "str": d},
            device_id_type=MESH,
        )

    def far_step(x):
        def step(g, carry):
            base = near + g * bunch
            far_images(x, bunch_of(base), tuple(range(qc)))
            for q in range(qc):

                @pl.when(base == own)
                def _(q=q):
                    far_copy(x, own, q, stay=True).start()

                @pl.when(base != own)
                def _(q=q):
                    far_copy(x, base, q).start()

                for u in range(1, bunch):
                    far_copy(x, base + u, q).start()
            return carry

        lax.fori_loop(0, 2 * per // bunch, step, 0)
        extras = outer_extras(near) + [own + u for u in range(per)]
        far_images(x, extras, (qc,))
        for v in extras:
            far_copy(x, v, qc, stay=isinstance(v, int) and v == own).start()

    last = len(chunks) - 1

    nothing = plane_blocks * 2 * nf
    for q in range(slots):
        y = 0 if kind(q) else q
        recv_near[kind(q)][y, nothing] = jnp.zeros((bs, bs), jnp.bfloat16)
        for x, (_, rows) in enumerate(chunks):
            recv_far[x][kind(q)][y, nothing] = jnp.zeros((rows, bs), jnp.bfloat16)

    def number(i, carry):
        for k in range(nf):
            for s in range(sc):
                p = pa[k, s, i]
                level = lax.div(p, plane_blocks)
                place = (lax.rem(p, plane_blocks) * 2 + lax.rem(level, 2)) * nf + k
                here = lax.div(level, 2) == side
                near_index[k, s, i] = jnp.where(here, place, nothing)
                far_index[k, s, i] = jnp.where(here, nothing, place)
        return carry

    lax.fori_loop(0, nab, number, 0)

    def partial(x, i, which):
        parts = []
        source, index = (recv_near, near_index) if x < 0 else (recv_far[x], far_index)
        count = 1 if which else qc
        for k in range(nf):
            for s in range(sc):
                at = index[k, s, i]
                parts.append(
                    jnp.concatenate([source[which][y, at] for y in range(count)], axis=1)
                )
        if x < 0:
            tiles = tiles_row[...]
        else:
            start, rows = chunks[x]
            tiles = tiles_turned[:, start * nf * sc : (start + rows) * nf * sc]
        return jnp.dot(
            tiles, jnp.concatenate(parts, axis=0), preferred_element_type=jnp.float32
        )

    def accumulate(x, which):
        def one(i, carry):
            value = partial(x, i, which)
            if x != 0:
                value = value + total[which][i]
            if x < last:
                total[which][i] = value
            else:
                first[which][i] = (value * scale[which][i]).astype(jnp.bfloat16)
            return carry

        lax.fori_loop(0, nab, one, 0, unroll=4)

    def landed(x, which):
        source, sem = (recv_near, near_sem) if x < 0 else (recv_far[x], far_recv.at[x])
        some = source[which].at[:, pl.ds(0, nothing)]
        pltpu.make_async_copy(some, some, sem.at[which]).wait()

    schedule = [[(y - 2, w) for w in (0, 1)] for y in range(len(chunks))]
    schedule[:2] = [[], []]
    schedule[-3:] = [
        [(last - 4, 0), (-1, 0)],
        [(last - 3, 0)],
        [(last - 2, 0), (last - 1, 0)],
    ]
    later = (last - 4, -1, last - 3, last - 2, last - 1, last)

    for x in range(len(chunks)):

        @pl.when(inner)
        def _(x=x):
            pltpu.make_async_copy(far[x], far[x], raw_recv.at[x]).wait()

        raw_copy(x).wait_send()
        if x + WINDOW < len(chunks):
            raw_copy(x + WINDOW).start()

        @pl.when(inner)
        def _(x=x):
            far_step(x)

        for y, which in schedule[x]:
            if which == 0:
                landed(y, 0)
                accumulate(y, 0)
            else:

                @pl.when(more)
                def _(y=y):
                    landed(y, 1)
                    accumulate(y, 1)

    landed(last, 0)
    accumulate(last, 0)

    def second_copy(q, h, v, stay=False):
        src = send2[q].at[h, v]
        dst = recv2[h].at[column_of(me, c, q)]
        if stay:
            return pltpu.make_async_copy(src, dst, recv2_sem.at[h])
        d, f = target(v)
        return pltpu.make_async_remote_copy(
            src_ref=src,
            dst_ref=dst,
            send_sem=send2_sem.at[q, h],
            recv_sem=recv2_sem.at[h],
            device_id={"fac": f, "str": d},
            device_id_type=MESH,
        )

    def share_copy(e):
        f = lax.rem(c + e, nf)
        src = first[0].at[pl.ds(f * half_rows, half_rows)]
        dst = out1.at[:, :, pl.ds(pl.multiple_of(c * qc * bs, bs), qc * bs)]
        if e == 0:
            return pltpu.make_async_copy(src, dst, o1_send.at[e])
        return pltpu.make_async_remote_copy(
            src_ref=src,
            dst_ref=dst,
            send_sem=o1_send.at[e],
            recv_sem=o1_recv.at[e],
            device_id={"fac": f, "str": me},
            device_id_type=MESH,
        )

    def begin(q):
        return jnp.where(more, near, 0) if q == 0 else near if q == qc else 0

    def alpha_images(v, which, cols):
        d, f = target(v)
        i = d * nf + f
        for k in range(nf):
            picked = jnp.concatenate([first[which][pa[k, s, i]] for s in range(sc)], axis=0)
            image = jnp.dot(
                tiles_row[:, k * kb : (k + 1) * kb],
                picked,
                preferred_element_type=jnp.float32,
            ).astype(jnp.bfloat16)
            for y, q in enumerate(cols):
                for h in range(HALVES):
                    send2[q][h, v, k] = image[h * hb : (h + 1) * hb, y * bs : (y + 1) * bs]

    def second_copies(q, h, base):
        @pl.when(base == own)
        def _():
            second_copy(q, h, own, stay=True).start()

        @pl.when(base != own)
        def _():
            second_copy(q, h, base).start()

        for u in range(1, bunch):
            second_copy(q, h, base + u).start()

    def images_out(which, cols):
        def step_two(g, carry):
            base = g * bunch
            for u in range(bunch):
                alpha_images(base + u, which, cols)
            for q in reversed(cols):

                @pl.when(base >= begin(q))
                def _(q=q):
                    second_copies(q, 0, base)

            return carry

        lax.fori_loop((near if which else 0) // bunch, everyone // bunch, step_two, 0)

    order = list(reversed(range(qc)))
    images_out(0, tuple(range(qc)))
    for e in range(nf):
        share_copy(e).start()

    def send_rest(q, h):
        def rest(g, carry):
            second_copies(q, h, g * bunch)
            return carry

        lax.fori_loop(begin(q) // bunch, everyone // bunch, rest, 0)

    for q in order:
        send_rest(q, 1)

    @pl.when(more)
    def _():
        for y in later:
            landed(y, 1)
            accumulate(y, 1)
        images_out(1, (qc,))

    for h in range(1, HALVES):
        for q in order if h > 1 else []:
            send_rest(q, h)

        @pl.when(more)
        def _(h=h):
            send_rest(qc, h)

    mine = me * nf + c
    group = max(g for g in (1, 2, 4, 8, 16) if half_blocks % g == 0)
    pieces = half_blocks // group

    def scale_row(j, carry):
        denominator = column(adiag, mine) + bdiag[pl.ds(j, 1), :] - energy[0]
        scale_last[j] = alive(mine, j) / denominator
        return carry

    lax.fori_loop(0, nbb, scale_row, 0)

    def sigma_two(h, first_block):
        rows = []
        for g in range(group):
            parts = [
                recv2[h][pb[k, s, first_block + g], k] for k in range(nf) for s in range(sc)
            ]
            rows.append(jnp.concatenate(parts, axis=1))
        sigma = jnp.dot(
            jnp.concatenate(rows, axis=0), tb_all[...], preferred_element_type=jnp.float32
        )
        for g in range(group):
            j = first_block + g
            value = sigma[g * hb : (g + 1) * hb] * scale_last[j, h * hb : (h + 1) * hb]
            staged[h * hb : (h + 1) * hb, block(j)] = value.astype(jnp.bfloat16)

    def piece_copy(h, e, x):
        f = lax.rem(c + e, nf)
        src_start = pl.multiple_of((f * half_blocks + x * group) * bs, bs)
        dst_start = pl.multiple_of(x * group * bs, bs)
        src = staged.at[pl.ds(h * hb, hb), pl.ds(src_start, group * bs)]
        dst = out2.at[
            pl.ds(pl.multiple_of(c * bs + h * hb, hb), hb), pl.ds(dst_start, group * bs)
        ]
        if e == 0:
            return pltpu.make_async_copy(src, dst, o2_send.at[e])
        return pltpu.make_async_remote_copy(
            src_ref=src,
            dst_ref=dst,
            send_sem=o2_send.at[e],
            recv_sem=o2_recv.at[e],
            device_id={"fac": f, "str": me},
            device_id_type=MESH,
        )

    for h in range(HALVES):
        pltpu.make_async_copy(recv2[h], recv2[h], recv2_sem.at[h]).wait()
        for e in reversed(range(nf)):

            def finish(x, carry, e=e, h=h):
                sigma_two(h, lax.rem(c + e, nf) * half_blocks + x * group)
                piece_copy(h, e, x).start()
                return carry

            lax.fori_loop(0, pieces, finish, 0)

    def second_sent(q, h, count):
        sent = send2[q].at[h, pl.ds(0, count)]
        pltpu.make_async_copy(sent, sent, send2_sem.at[q, h]).wait()

    def near_sent(q, count):
        sent = send1[q].at[pl.ds(0, count)]
        pltpu.make_async_copy(sent, sent, send1_sem.at[q]).wait()

    for q in range(qc):
        near_sent(q, near_count)
    for e in range(nf):
        share_copy(e).wait()

    @pl.when(inner)
    def _():
        for x in range(len(chunks)):
            some = send_far[x].at[pl.ds(0, near_count * qc + per - 1 + lanes)]
            pltpu.make_async_copy(some, some, far_sem.at[x]).wait()

    @pl.when(more)
    def _():
        near_sent(qc, per + lanes - 1)
        for h in range(HALVES):
            for q in range(slots):
                second_sent(q, h, near_count if q in (0, qc) else everyone - 1)

    @pl.when(jnp.logical_not(more))
    def _():
        near_sent(qc, per + lanes)
        for h in range(HALVES):
            for q in range(qc):
                second_sent(q, h, everyone - 1)

    for e in range(nf):
        sent = staged.at[:, pl.ds(0, half_blocks * bs)]
        pltpu.make_async_copy(sent, sent, o2_send.at[e]).wait()
        if e > 0:
            pltpu.make_async_copy(sent, sent, o2_recv.at[e]).wait()


def split_body(
    vector,
    alpha_tiles,
    alpha_pattern,
    beta_tiles,
    beta_pattern,
    alpha_sector,
    beta_sector,
    alpha_diag,
    beta_diag,
    energy,
):
    n = lax.axis_size("str")
    nf = lax.axis_size("fac")
    sc, bs = alpha_tiles.shape[1], alpha_tiles.shape[2]
    nab, nbb = alpha_sector.shape[0], beta_sector.shape[0]
    qc = nbb // (n * nf)
    slots = qc + 1
    rows = vector.shape[0]
    smem = pl.BlockSpec(memory_space=pltpu.SMEM)
    anywhere = pl.BlockSpec(memory_space=pl.ANY)
    hbm = pl.BlockSpec(memory_space=pltpu.HBM)
    bf16 = jnp.bfloat16
    everyone = n * nf
    row_blocks = nab // n
    near = everyone // 2
    hb = bs // HALVES
    chunks = row_chunks(bs)
    dma = pltpu.SemaphoreType.DMA
    first_update, second_update = pl.pallas_call(
        functools.partial(exchange_kernel, (n, nf, bs, sc, qc, nab, nbb)),
        out_shape=(
            jax.ShapeDtypeStruct((nab // nf, bs, nbb * bs // n), bf16),
            jax.ShapeDtypeStruct((rows, nbb * bs // nf), bf16),
        ),
        in_specs=[smem] + [hbm] * 9,
        out_specs=(anywhere, anywhere),
        scratch_shapes=[
            pltpu.VMEM((nbb, rows, bs), bf16),
            [pltpu.VMEM((nbb, 2, count, bs), bf16) for _, count in chunks],
            pltpu.VMEM((nf * sc * bs, bs), bf16),
            pltpu.VMEM((nf * sc * bs, bs), bf16),
            pltpu.VMEM((bs, nf * sc * bs), bf16),
            pltpu.VMEM((bs, nf * sc * bs), bf16),
            pltpu.SMEM((nf, sc, nab), jnp.int32),
            pltpu.SMEM((nf, sc, nbb), jnp.int32),
            pltpu.SMEM((nab,), jnp.int32),
            pltpu.SMEM((nbb,), jnp.int32),
            pltpu.SMEM((nf, sc, nab), jnp.int32),
            pltpu.SMEM((nf, sc, nab), jnp.int32),
            pltpu.VMEM((nab, bs), jnp.float32),
            pltpu.VMEM((nbb, bs), jnp.float32),
            [pltpu.VMEM((near, row_blocks, bs, bs), bf16) for _ in range(slots)],
            [pltpu.VMEM((near * slots, 2 * nf, count, bs), bf16) for _, count in chunks],
            [
                pltpu.VMEM((cols, nab // PLANES * 2 * nf + 1, bs, bs), bf16)
                for cols in (qc, 1)
            ],
            [
                [
                    pltpu.VMEM((cols, nab // PLANES * 2 * nf + 1, count, bs), bf16)
                    for cols in (qc, 1)
                ]
                for _, count in chunks
            ],
            [pltpu.VMEM((nab, bs, cols * bs), jnp.float32) for cols in (qc, 1)],
            [pltpu.VMEM((nab, bs, cols * bs), jnp.float32) for cols in (qc, 1)],
            pltpu.VMEM((nbb, bs, bs), jnp.float32),
            [pltpu.VMEM((nab, bs, cols * bs), bf16) for cols in (qc, 1)],
            [pltpu.VMEM((HALVES, everyone, nf, hb, bs), bf16) for _ in range(slots)],
            [pltpu.VMEM((nbb, nf, hb, bs), bf16) for _ in range(HALVES)],
            pltpu.VMEM((bs, nbb * bs), bf16),
            dma,
            dma((2,)),
            dma((6,)),
            dma((nf - 1, 4)),
            dma((nf - 1, 4)),
            dma((len(chunks),)),
            dma((len(chunks),)),
            dma((slots,)),
            dma((len(chunks),)),
            dma((2,)),
            dma((len(chunks), 2)),
            dma((slots, HALVES)),
            dma((HALVES,)),
            dma((nf,)),
            dma((nf,)),
            dma((nf,)),
            dma((nf,)),
        ],
        compiler_params=pltpu.CompilerParams(
            collective_id=0, has_side_effects=True, vmem_limit_bytes=61 * 1024 * 1024
        ),
    )(
        energy,
        vector,
        alpha_tiles.reshape(sc * bs, bs),
        beta_tiles.reshape(sc * bs, bs),
        alpha_pattern[0].T,
        beta_pattern[0].T,
        alpha_sector,
        beta_sector,
        alpha_diag.reshape(nab, bs),
        beta_diag.reshape(nbb, bs),
    )
    return first_update.reshape(nab * bs // nf, nbb * bs // n), second_update


def fits_split(*args):
    vector, alpha_tiles, _, _, _, alpha_sector, beta_sector = args[:7]
    n, nf = lax.axis_size("str"), lax.axis_size("fac")
    bs = alpha_tiles.shape[2]
    nab, nbb = alpha_sector.shape[0], beta_sector.shape[0]
    return (
        n % PLANES == 0
        and nf > 1
        and alpha_tiles.shape[0] == 1
        and bs % 128 == 0
        and nab == n * nf
        and nbb == 2 * n * nf
    )


def either_body(*args):
    return split_body(*args) if fits_split(*args) else body(*args)


def solution(mesh):
    return jax.shard_map(
        either_body,
        mesh=mesh,
        in_specs=(
            P("str", None),
            P("fac", None, None, None),
            P("fac", None, None),
            P("fac", None, None, None),
            P("fac", None, None),
            P(),
            P(),
            P(),
            P(),
            P(),
        ),
        out_specs=(P("fac", "str"), P("str", "fac")),
        check_vma=False,
    )
```

```python
import functools

import jax
import jax.numpy as jnp
from jax import lax
from jax.experimental import pallas as pl
from jax.experimental.pallas import tpu as pltpu
from jax.sharding import PartitionSpec as P

MESH = pl.DeviceIdType.MESH


def beta_apply(matrix, tile_set, pattern):
    height, width = matrix.shape
    slot_count, block_size = tile_set.shape[:2]
    stacked = tile_set.reshape(slot_count * block_size, block_size)

    def one(j, result):
        picked = jnp.concatenate(
            [
                lax.dynamic_slice_in_dim(matrix, pattern[j, s] * block_size, block_size, 1)
                for s in range(slot_count)
            ],
            axis=1,
        )
        image = jnp.dot(picked, stacked, preferred_element_type=jnp.float32)
        return lax.dynamic_update_slice_in_dim(result, image, j * block_size, 1)

    return lax.fori_loop(
        0, width // block_size, one, jnp.zeros((height, width), jnp.float32)
    )


def alpha_apply(matrix, tile_set, pattern):
    height, width = matrix.shape
    slot_count, block_size = tile_set.shape[:2]
    stacked = tile_set.transpose(1, 0, 2).reshape(block_size, slot_count * block_size)

    def one(i, result):
        picked = jnp.concatenate(
            [
                lax.dynamic_slice_in_dim(matrix, pattern[i, s] * block_size, block_size, 0)
                for s in range(slot_count)
            ],
            axis=0,
        )
        image = jnp.dot(stacked, picked, preferred_element_type=jnp.float32)
        return lax.dynamic_update_slice_in_dim(result, image, i * block_size, 0)

    return lax.fori_loop(
        0, height // block_size, one, jnp.zeros((height, width), jnp.float32)
    )


def precondition(
    sigma_part,
    row_start,
    col_start,
    block_size,
    alpha_sector,
    beta_sector,
    alpha_diag,
    beta_diag,
    energy,
):
    row_count, col_count = sigma_part.shape
    row_blocks = row_count // block_size
    col_blocks = col_count // block_size
    alpha_labels = lax.dynamic_slice_in_dim(alpha_sector, row_start // block_size, row_blocks)
    beta_labels = lax.dynamic_slice_in_dim(beta_sector, col_start // block_size, col_blocks)
    live_mask = (alpha_labels[:, None, None, None] == beta_labels[None, None, :, None]).astype(
        jnp.float32
    )
    masked = (
        sigma_part.reshape(row_blocks, block_size, col_blocks, block_size) * live_mask
    ).reshape(row_count, col_count)
    alpha_part = lax.dynamic_slice_in_dim(alpha_diag, row_start, row_count)
    beta_part = lax.dynamic_slice_in_dim(beta_diag, col_start, col_count)
    denominator = alpha_part[:, None] + beta_part[None, :] - energy[0]
    return (masked / denominator).astype(jnp.bfloat16)


def body(
    vector,
    alpha_tiles,
    alpha_pattern,
    beta_tiles,
    beta_pattern,
    alpha_sector,
    beta_sector,
    alpha_diag,
    beta_diag,
    energy,
):
    string_index = lax.axis_index("str")
    group_index = lax.axis_index("fac")
    string_count = lax.axis_size("str")
    block_size = alpha_tiles.shape[2]
    row_count = vector.shape[0]
    col_count = vector.shape[1] // string_count
    factor = 0
    image = beta_apply(vector, beta_tiles[factor], beta_pattern[factor]).astype(jnp.bfloat16)
    moved_one = lax.all_to_all(image, "str", split_axis=1, concat_axis=0, tiled=True)
    partial_value = alpha_apply(moved_one, alpha_tiles[factor], alpha_pattern[factor])
    share_rows = lax.psum_scatter(partial_value, "fac", scatter_dimension=0, tiled=True)
    first_update = precondition(
        share_rows,
        group_index * share_rows.shape[0],
        string_index * col_count,
        block_size,
        alpha_sector,
        beta_sector,
        alpha_diag,
        beta_diag,
        energy,
    )
    whole_first = lax.all_gather(first_update, "fac", axis=0, tiled=True)
    factor = 0
    back_image = alpha_apply(whole_first, alpha_tiles[factor], alpha_pattern[factor]).astype(
        jnp.bfloat16
    )
    returned_one = lax.all_to_all(back_image, "str", split_axis=0, concat_axis=1, tiled=True)
    partial_back = beta_apply(returned_one, beta_tiles[factor], beta_pattern[factor])
    share_cols = lax.psum_scatter(partial_back, "fac", scatter_dimension=1, tiled=True)
    second_update = precondition(
        share_cols,
        string_index * row_count,
        group_index * share_cols.shape[1],
        block_size,
        alpha_sector,
        beta_sector,
        alpha_diag,
        beta_diag,
        energy,
    )
    return (first_update, second_update)


PLANES = 4
HALVES = 4
WINDOW = 3


def row_chunks(bs):
    shares = (1, 1, 2, 1, 1, 1, 1)
    unit = bs // sum(shares)
    starts = [unit * sum(shares[:x]) for x in range(len(shares))]
    return [(start, unit * share) for start, share in zip(starts, shares)]


def exchange_kernel(
    sizes,
    energy,
    vec,
    ta_in,
    tb_in,
    pa_in,
    pb_in,
    sa_in,
    sb_in,
    ad_in,
    bd_in,
    out1,
    out2,
    held,
    far,
    ta_all,
    tb_all,
    tiles_row,
    tiles_turned,
    pa,
    pb,
    sa,
    sb,
    near_index,
    far_index,
    adiag,
    bdiag,
    send1,
    send_far,
    recv_near,
    recv_far,
    total,
    scale,
    scale_last,
    first,
    send2,
    recv2,
    staged,
    held_sem,
    early_sem,
    late_sem,
    give_send,
    give_recv,
    raw_send,
    raw_recv,
    send1_sem,
    far_sem,
    near_sem,
    far_recv,
    send2_sem,
    recv2_sem,
    o1_send,
    o1_recv,
    o2_send,
    o2_recv,
):
    n, nf, bs, sc, qc, nab, nbb = sizes
    slots = qc + 1
    me = lax.axis_index("str")
    c = lax.axis_index("fac")
    everyone = n * nf
    lanes = n // PLANES
    per = lanes * nf
    row_blocks = nab // n
    plane_blocks = lanes * row_blocks
    half_rows = nab // nf
    half_blocks = nbb // nf
    kb = sc * bs
    hb = bs // HALVES
    plane = me // lanes
    lane = lax.rem(me, lanes)
    side = plane // 2
    inner = lax.rem(plane, 2) != side
    more = jnp.logical_or(inner, c == 0)
    near = 2 * per
    near_count = 2 * per - 1
    bunch = 4 if per % 4 == 0 else 1
    own = 3 * per
    chunks = row_chunks(bs)

    def target(v):
        step = v // per
        u = lax.rem(v, per)
        high = lax.rem(side + 1 - step // 2, 2)
        low = lax.rem(lax.rem(plane, 2) + step + step // 2, 2)
        d = (2 * high + low) * lanes + lax.rem(lane + u // nf, lanes)
        return d, lax.rem(c + lax.rem(u, nf), nf)

    def partner(t):
        return t + t // own

    def column_of(d, f, q):
        if q < qc:
            return (d * nf + f) * qc + q
        mirror = (PLANES - 1 - d // lanes) * lanes + lax.rem(d, lanes)
        return (mirror * nf + f) * qc

    barrier = pltpu.get_barrier_semaphore()

    def block(index):
        return pl.ds(pl.multiple_of(index * bs, bs), bs)

    own_kb = pl.ds(pl.multiple_of(c * kb, kb), kb)
    early = [
        pltpu.make_async_copy(tb_in, tb_all.at[own_kb], early_sem.at[0]),
        pltpu.make_async_copy(pb_in, pb.at[c], early_sem.at[1]),
    ]
    late = [
        pltpu.make_async_copy(ta_in, ta_all.at[own_kb], late_sem.at[0]),
        pltpu.make_async_copy(ad_in, adiag, late_sem.at[1]),
        pltpu.make_async_copy(bd_in, bdiag, late_sem.at[2]),
        pltpu.make_async_copy(pa_in, pa.at[c], late_sem.at[3]),
        pltpu.make_async_copy(sa_in, sa, late_sem.at[4]),
        pltpu.make_async_copy(sb_in, sb, late_sem.at[5]),
    ]
    for copy in early:
        copy.start()

    def load(b, carry):
        pltpu.make_async_copy(vec.at[:, block(b)], held.at[b], held_sem).start()
        return carry

    lax.fori_loop(0, nbb, load, 0, unroll=8)

    def greet(t, carry):
        d, f = target(partner(t))
        pl.semaphore_signal(
            barrier, inc=1, device_id={"fac": f, "str": d}, device_id_type=MESH
        )
        return carry

    lax.fori_loop(0, everyone - 1, greet, 0)

    for copy in late:
        copy.start()

    def gives():
        for e in range(1, nf):
            f = lax.rem(c + e, nf)
            for x, (a, b) in enumerate(
                [
                    (tb_in, tb_all.at[own_kb]),
                    (ta_in, ta_all.at[own_kb]),
                    (pb_in, pb.at[c]),
                    (pa_in, pa.at[c]),
                ]
            ):
                yield pltpu.make_async_remote_copy(
                    src_ref=a,
                    dst_ref=b,
                    send_sem=give_send.at[e - 1, x],
                    recv_sem=give_recv.at[e - 1, x],
                    device_id={"fac": f, "str": me},
                    device_id_type=MESH,
                )

    def raw_copy(x):
        start, rows = chunks[x]
        return pltpu.make_async_remote_copy(
            src_ref=held.at[:, pl.ds(pl.multiple_of(c * bs + start, 16), rows)],
            dst_ref=far[x].at[:, lax.rem(plane, 2)],
            send_sem=raw_send.at[x],
            recv_sem=raw_recv.at[x],
            device_id={"fac": c, "str": (2 - side) * lanes + lane},
            device_id_type=MESH,
        )

    def column(ref, index):
        return jnp.transpose(jnp.broadcast_to(ref[pl.ds(index, 1), :], (bs, bs)))

    def alive(i, j):
        return jnp.where(sa[i] == sb[j], 1.0, 0.0).astype(jnp.float32)

    def kind(q):
        return int(q == qc)

    def near_images(q, targets):
        picked = []
        for v in targets:
            d, f = target(v)
            j = column_of(d, f, q)
            picked.append(jnp.concatenate([held[pb[c, s, j]] for s in range(sc)], axis=1))
        image = jnp.dot(
            jnp.concatenate(picked, axis=0),
            tb_all[own_kb, :],
            preferred_element_type=jnp.float32,
        ).astype(jnp.bfloat16)
        at = 0
        for v in targets:
            for x in range(row_blocks):
                send1[q][v - near, x] = image[at : at + bs]
                at += bs

    def first_copy(q, v, x, stay=False):
        src = send1[q].at[v - near, x]
        level = lax.rem(plane, 2) * nf + c
        dst = recv_near[kind(q)].at[
            0 if kind(q) else q, (lane * row_blocks + x) * 2 * nf + level
        ]
        if stay:
            return pltpu.make_async_copy(src, dst, near_sem.at[kind(q)])
        d, f = target(v)
        return pltpu.make_async_remote_copy(
            src_ref=src,
            dst_ref=dst,
            send_sem=send1_sem.at[q],
            recv_sem=near_sem.at[kind(q)],
            device_id={"fac": f, "str": d},
            device_id_type=MESH,
        )

    def bunch_of(base):
        return [base + u for u in range(bunch)]

    def first_copies(q, targets):
        for x in range(row_blocks):

            @pl.when(targets[0] == own)
            def _(x=x):
                first_copy(q, own, x, stay=True).start()

            @pl.when(targets[0] != own)
            def _(x=x):
                first_copy(q, targets[0], x).start()

            for v in targets[1:]:
                first_copy(q, v, x).start()

    pltpu.make_async_copy(held, held, held_sem).wait()
    for copy in early:
        copy.wait()
    pl.semaphore_wait(barrier, everyone - 1)
    raw_copy(0).start()
    for copy in gives():
        copy.start()

    for x in range(1, WINDOW):
        raw_copy(x).start()
    for q in range(qc):

        def step_one(g, carry, q=q):
            near_images(q, bunch_of(near + g * bunch))
            first_copies(q, bunch_of(near + g * bunch))
            return carry

        lax.fori_loop(0, 2 * per // bunch, step_one, 0)

    extra_base = jnp.where(inner, own, near)

    def step_extra(g, carry):
        near_images(qc, bunch_of(extra_base + g * bunch))
        first_copies(qc, bunch_of(extra_base + g * bunch))
        return carry

    lax.fori_loop(0, per // bunch, step_extra, 0)

    def outer_extras(base):
        return [base + nf * w + lax.rem(nf - c, nf) for w in range(lanes)]

    outer_base = jnp.where(inner, near, own)
    near_images(qc, outer_extras(outer_base))
    first_copies(qc, outer_extras(outer_base))

    for copy in late:
        copy.wait()
    for copy in gives():
        copy.wait()
    for x in range(nf * sc):
        tiles_row[:, x * bs : (x + 1) * bs] = ta_all[x * bs : (x + 1) * bs, :]

    width = nf * kb
    spot = lax.broadcasted_iota(jnp.int32, (width, width), 1)
    origin = jnp.zeros((width, width), jnp.int32)
    for start, rows in chunks:
        inside = spot - start * nf * sc
        source = inside // rows * bs + start + lax.rem(inside, rows)
        origin = jnp.where(inside >= 0, source, origin)
    turn = jnp.where(
        lax.broadcasted_iota(jnp.int32, (width, width), 0) == origin, 1.0, 0.0
    ).astype(jnp.bfloat16)
    tiles_turned[...] = jnp.dot(
        tiles_row[...], turn, preferred_element_type=jnp.float32
    ).astype(jnp.bfloat16)

    def scale_columns(q):
        j = column_of(me, c, q)

        def one(i, carry):
            denominator = column(adiag, i) + bdiag[pl.ds(j, 1), :] - energy[0]
            value = alive(i, j) / denominator
            if q < qc:
                scale[0][i, :, q * bs : (q + 1) * bs] = value
            else:
                scale[1][i] = value
            return carry

        lax.fori_loop(0, nab, one, 0)

    for q in range(qc):
        scale_columns(q)

    @pl.when(more)
    def _():
        scale_columns(qc)

    def far_images(x, targets, qs):
        rows = chunks[x][1]
        places = [target(v) for v in targets]
        for k in range(nf):
            picked = []
            for d, f in places:
                for q in qs:
                    j = column_of(d, f, q)
                    picked.append(
                        jnp.concatenate(
                            [far[x][pb[k, s, j]].reshape(2 * rows, bs) for s in range(sc)],
                            axis=1,
                        )
                    )
            image = jnp.dot(
                jnp.concatenate(picked, axis=0),
                tb_all[k * kb : (k + 1) * kb, :],
                preferred_element_type=jnp.float32,
            ).astype(jnp.bfloat16)
            at = 0
            for v in targets:
                for q in qs:
                    for z in range(2):
                        send_far[x][(v - near) * slots + q, z * nf + k] = image[
                            at : at + rows
                        ]
                        at += rows

    def far_copy(x, v, q, stay=False):
        src = send_far[x].at[(v - near) * slots + q]
        dst = recv_far[x][kind(q)].at[
            0 if kind(q) else q, pl.ds((lane * row_blocks + c) * 2 * nf, 2 * nf)
        ]
        if stay:
            return pltpu.make_async_copy(src, dst, far_recv.at[x, kind(q)])
        d, f = target(v)
        return pltpu.make_async_remote_copy(
            src_ref=src,
            dst_ref=dst,
            send_sem=far_sem.at[x],
            recv_sem=far_recv.at[x, kind(q)],
            device_id={"fac": f, "str": d},
            device_id_type=MESH,
        )

    def far_step(x):
        def step(g, carry):
            base = near + g * bunch
            far_images(x, bunch_of(base), tuple(range(qc)))
            for q in range(qc):

                @pl.when(base == own)
                def _(q=q):
                    far_copy(x, own, q, stay=True).start()

                @pl.when(base != own)
                def _(q=q):
                    far_copy(x, base, q).start()

                for u in range(1, bunch):
                    far_copy(x, base + u, q).start()
            return carry

        lax.fori_loop(0, 2 * per // bunch, step, 0)

    def far_extras(x):
        extras = outer_extras(near) + [own + u for u in range(per)]
        far_images(x, extras, (qc,))
        for v in extras:
            far_copy(x, v, qc, stay=isinstance(v, int) and v == own).start()

    last = len(chunks) - 1

    nothing = plane_blocks * 2 * nf
    for q in range(slots):
        y = 0 if kind(q) else q
        recv_near[kind(q)][y, nothing] = jnp.zeros((bs, bs), jnp.bfloat16)
        for x, (_, rows) in enumerate(chunks):
            recv_far[x][kind(q)][y, nothing] = jnp.zeros((rows, bs), jnp.bfloat16)

    def number(i, carry):
        for k in range(nf):
            for s in range(sc):
                p = pa[k, s, i]
                level = lax.div(p, plane_blocks)
                place = (lax.rem(p, plane_blocks) * 2 + lax.rem(level, 2)) * nf + k
                here = lax.div(level, 2) == side
                near_index[k, s, i] = jnp.where(here, place, nothing)
                far_index[k, s, i] = jnp.where(here, nothing, place)
        return carry

    lax.fori_loop(0, nab, number, 0)

    def partial(x, i, which):
        parts = []
        source, index = (recv_near, near_index) if x < 0 else (recv_far[x], far_index)
        count = 1 if which else qc
        for k in range(nf):
            for s in range(sc):
                at = index[k, s, i]
                parts.append(
                    jnp.concatenate([source[which][y, at] for y in range(count)], axis=1)
                )
        if x < 0:
            tiles = tiles_row[...]
        else:
            start, rows = chunks[x]
            tiles = tiles_turned[:, start * nf * sc : (start + rows) * nf * sc]
        return jnp.dot(
            tiles, jnp.concatenate(parts, axis=0), preferred_element_type=jnp.float32
        )

    def accumulate(x, which):
        def one(i, carry):
            value = partial(x, i, which)
            if x != 0:
                value = value + total[which][i]
            if x < last:
                total[which][i] = value
            else:
                first[which][i] = (value * scale[which][i]).astype(jnp.bfloat16)
            return carry

        lax.fori_loop(0, nab, one, 0, unroll=4)

    def landed(x, which):
        source, sem = (recv_near, near_sem) if x < 0 else (recv_far[x], far_recv.at[x])
        some = source[which].at[:, pl.ds(0, nothing)]
        pltpu.make_async_copy(some, some, sem.at[which]).wait()

    schedule = [[(y - 2, w) for w in (0, 1)] for y in range(len(chunks))]
    schedule[:2] = [[], []]
    schedule[-3:] = [
        [(last - 4, 0), (-1, 0)],
        [(last - 3, 0), (last - 2, 0)],
        [(last - 1, 0)],
    ]
    later = (last - 4, -1, last - 3, last - 2, last - 1, last)

    for x in range(len(chunks)):

        @pl.when(inner)
        def _(x=x):
            pltpu.make_async_copy(far[x], far[x], raw_recv.at[x]).wait()

        raw_copy(x).wait_send()
        if x + WINDOW < len(chunks):
            raw_copy(x + WINDOW).start()

        @pl.when(inner)
        def _(x=x):
            far_step(x)
            for y in [x] if x < last - 1 else [last - 1, last] if x == last else []:
                far_extras(y)

        for y, which in schedule[x]:
            if which == 0:
                landed(y, 0)
                accumulate(y, 0)
            else:

                @pl.when(more)
                def _(y=y):
                    landed(y, 1)
                    accumulate(y, 1)

    landed(last, 0)
    accumulate(last, 0)

    def second_copy(q, h, v, stay=False):
        src = send2[q].at[h, v]
        dst = recv2[h].at[column_of(me, c, q)]
        if stay:
            return pltpu.make_async_copy(src, dst, recv2_sem.at[h])
        d, f = target(v)
        return pltpu.make_async_remote_copy(
            src_ref=src,
            dst_ref=dst,
            send_sem=send2_sem.at[q, h],
            recv_sem=recv2_sem.at[h],
            device_id={"fac": f, "str": d},
            device_id_type=MESH,
        )

    def share_copy(e):
        f = lax.rem(c + e, nf)
        src = first[0].at[pl.ds(f * half_rows, half_rows)]
        dst = out1.at[:, :, pl.ds(pl.multiple_of(c * qc * bs, bs), qc * bs)]
        if e == 0:
            return pltpu.make_async_copy(src, dst, o1_send.at[e])
        return pltpu.make_async_remote_copy(
            src_ref=src,
            dst_ref=dst,
            send_sem=o1_send.at[e],
            recv_sem=o1_recv.at[e],
            device_id={"fac": f, "str": me},
            device_id_type=MESH,
        )

    def begin(q):
        return jnp.where(more, near, 0) if q == 0 else near if q == qc else 0

    def alpha_images(v, which, cols):
        d, f = target(v)
        i = d * nf + f
        for k in range(nf):
            picked = jnp.concatenate([first[which][pa[k, s, i]] for s in range(sc)], axis=0)
            image = jnp.dot(
                tiles_row[:, k * kb : (k + 1) * kb],
                picked,
                preferred_element_type=jnp.float32,
            ).astype(jnp.bfloat16)
            for y, q in enumerate(cols):
                for h in range(HALVES):
                    send2[q][h, v, k] = image[h * hb : (h + 1) * hb, y * bs : (y + 1) * bs]

    def second_copies(q, h, base):
        @pl.when(base == own)
        def _():
            second_copy(q, h, own, stay=True).start()

        @pl.when(base != own)
        def _():
            second_copy(q, h, base).start()

        for u in range(1, bunch):
            second_copy(q, h, base + u).start()

    def images_out(which, cols):
        def step_two(g, carry):
            base = g * bunch
            for u in range(bunch):
                alpha_images(base + u, which, cols)
            for q in reversed(cols):

                @pl.when(base >= begin(q))
                def _(q=q):
                    second_copies(q, 0, base)

            return carry

        lax.fori_loop((near if which else 0) // bunch, everyone // bunch, step_two, 0)

    order = list(reversed(range(qc)))
    images_out(0, tuple(range(qc)))
    for e in range(nf):
        share_copy(e).start()

    def send_rest(q, h):
        def rest(g, carry):
            second_copies(q, h, g * bunch)
            return carry

        lax.fori_loop(begin(q) // bunch, everyone // bunch, rest, 0)

    for q in order:
        send_rest(q, 1)

    @pl.when(more)
    def _():
        for y in later:
            landed(y, 1)
            accumulate(y, 1)
        images_out(1, (qc,))

    for h in range(1, HALVES):
        for q in order if h > 1 else []:
            send_rest(q, h)

        @pl.when(more)
        def _(h=h):
            send_rest(qc, h)

    mine = me * nf + c
    group = max(g for g in (1, 2, 4, 8, 16) if half_blocks % g == 0)
    pieces = half_blocks // group

    def scale_row(j, carry):
        denominator = column(adiag, mine) + bdiag[pl.ds(j, 1), :] - energy[0]
        scale_last[j] = alive(mine, j) / denominator
        return carry

    lax.fori_loop(0, nbb, scale_row, 0)

    def sigma_two(h, first_block):
        rows = []
        for g in range(group):
            parts = [
                recv2[h][pb[k, s, first_block + g], k] for k in range(nf) for s in range(sc)
            ]
            rows.append(jnp.concatenate(parts, axis=1))
        sigma = jnp.dot(
            jnp.concatenate(rows, axis=0), tb_all[...], preferred_element_type=jnp.float32
        )
        for g in range(group):
            j = first_block + g
            value = sigma[g * hb : (g + 1) * hb] * scale_last[j, h * hb : (h + 1) * hb]
            staged[h * hb : (h + 1) * hb, block(j)] = value.astype(jnp.bfloat16)

    def piece_copy(h, e, x):
        f = lax.rem(c + e, nf)
        src_start = pl.multiple_of((f * half_blocks + x * group) * bs, bs)
        dst_start = pl.multiple_of(x * group * bs, bs)
        src = staged.at[pl.ds(h * hb, hb), pl.ds(src_start, group * bs)]
        dst = out2.at[
            pl.ds(pl.multiple_of(c * bs + h * hb, hb), hb), pl.ds(dst_start, group * bs)
        ]
        if e == 0:
            return pltpu.make_async_copy(src, dst, o2_send.at[e])
        return pltpu.make_async_remote_copy(
            src_ref=src,
            dst_ref=dst,
            send_sem=o2_send.at[e],
            recv_sem=o2_recv.at[e],
            device_id={"fac": f, "str": me},
            device_id_type=MESH,
        )

    for h in range(HALVES):
        pltpu.make_async_copy(recv2[h], recv2[h], recv2_sem.at[h]).wait()
        for e in reversed(range(nf)):

            def finish(x, carry, e=e, h=h):
                sigma_two(h, lax.rem(c + e, nf) * half_blocks + x * group)
                piece_copy(h, e, x).start()
                return carry

            lax.fori_loop(0, pieces, finish, 0)

    def second_sent(q, h, count):
        sent = send2[q].at[h, pl.ds(0, count)]
        pltpu.make_async_copy(sent, sent, send2_sem.at[q, h]).wait()

    def near_sent(q, count):
        sent = send1[q].at[pl.ds(0, count)]
        pltpu.make_async_copy(sent, sent, send1_sem.at[q]).wait()

    for q in range(qc):
        near_sent(q, near_count)
    for e in range(nf):
        share_copy(e).wait()

    @pl.when(inner)
    def _():
        for x in range(len(chunks)):
            some = send_far[x].at[pl.ds(0, near_count * qc + per - 1 + lanes)]
            pltpu.make_async_copy(some, some, far_sem.at[x]).wait()

    @pl.when(more)
    def _():
        near_sent(qc, per + lanes - 1)
        for h in range(HALVES):
            for q in range(slots):
                second_sent(q, h, near_count if q in (0, qc) else everyone - 1)

    @pl.when(jnp.logical_not(more))
    def _():
        near_sent(qc, per + lanes)
        for h in range(HALVES):
            for q in range(qc):
                second_sent(q, h, everyone - 1)

    for e in range(nf):
        sent = staged.at[:, pl.ds(0, half_blocks * bs)]
        pltpu.make_async_copy(sent, sent, o2_send.at[e]).wait()
        if e > 0:
            pltpu.make_async_copy(sent, sent, o2_recv.at[e]).wait()


COPIES = 4


def hand_over(source1, source2, out1, out2, stage1, stage2, sems_in, sems_out):
    loads, stores = [], []
    for y, (source, stage, out) in enumerate(
        [(source1, stage1, out1), (source2, stage2, out2)]
    ):
        step = source.shape[0] // COPIES
        for x in range(COPIES):
            part = pl.ds(x * step, step)
            loads.append(
                pltpu.make_async_copy(source.at[part], stage.at[part], sems_in.at[y, x])
            )
            stores.append(
                pltpu.make_async_copy(stage.at[part], out.at[part], sems_out.at[y, x])
            )
    for load in loads:
        load.start()
    for load, store in zip(loads, stores):
        load.wait()
        store.start()
    for store in stores:
        store.wait()


def split_body(
    vector,
    alpha_tiles,
    alpha_pattern,
    beta_tiles,
    beta_pattern,
    alpha_sector,
    beta_sector,
    alpha_diag,
    beta_diag,
    energy,
):
    n = lax.axis_size("str")
    nf = lax.axis_size("fac")
    sc, bs = alpha_tiles.shape[1], alpha_tiles.shape[2]
    nab, nbb = alpha_sector.shape[0], beta_sector.shape[0]
    qc = nbb // (n * nf)
    slots = qc + 1
    rows = vector.shape[0]
    smem = pl.BlockSpec(memory_space=pltpu.SMEM)
    anywhere = pl.BlockSpec(memory_space=pl.ANY)
    hbm = pl.BlockSpec(memory_space=pltpu.HBM)
    bf16 = jnp.bfloat16
    everyone = n * nf
    row_blocks = nab // n
    near = everyone // 2
    hb = bs // HALVES
    chunks = row_chunks(bs)
    dma = pltpu.SemaphoreType.DMA
    first_update, second_update = pl.pallas_call(
        functools.partial(exchange_kernel, (n, nf, bs, sc, qc, nab, nbb)),
        out_shape=(
            jax.ShapeDtypeStruct((nab // nf, bs, nbb * bs // n), bf16),
            jax.ShapeDtypeStruct((rows, nbb * bs // nf), bf16),
        ),
        in_specs=[smem] + [hbm] * 9,
        out_specs=(anywhere, anywhere),
        scratch_shapes=[
            pltpu.VMEM((nbb, rows, bs), bf16),
            [pltpu.VMEM((nbb, 2, count, bs), bf16) for _, count in chunks],
            pltpu.VMEM((nf * sc * bs, bs), bf16),
            pltpu.VMEM((nf * sc * bs, bs), bf16),
            pltpu.VMEM((bs, nf * sc * bs), bf16),
            pltpu.VMEM((bs, nf * sc * bs), bf16),
            pltpu.SMEM((nf, sc, nab), jnp.int32),
            pltpu.SMEM((nf, sc, nbb), jnp.int32),
            pltpu.SMEM((nab,), jnp.int32),
            pltpu.SMEM((nbb,), jnp.int32),
            pltpu.SMEM((nf, sc, nab), jnp.int32),
            pltpu.SMEM((nf, sc, nab), jnp.int32),
            pltpu.VMEM((nab, bs), jnp.float32),
            pltpu.VMEM((nbb, bs), jnp.float32),
            [pltpu.VMEM((near, row_blocks, bs, bs), bf16) for _ in range(slots)],
            [pltpu.VMEM((near * slots, 2 * nf, count, bs), bf16) for _, count in chunks],
            [
                pltpu.VMEM((cols, nab // PLANES * 2 * nf + 1, bs, bs), bf16)
                for cols in (qc, 1)
            ],
            [
                [
                    pltpu.VMEM((cols, nab // PLANES * 2 * nf + 1, count, bs), bf16)
                    for cols in (qc, 1)
                ]
                for _, count in chunks
            ],
            [pltpu.VMEM((nab, bs, cols * bs), jnp.float32) for cols in (qc, 1)],
            [pltpu.VMEM((nab, bs, cols * bs), jnp.float32) for cols in (qc, 1)],
            pltpu.VMEM((nbb, bs, bs), jnp.float32),
            [pltpu.VMEM((nab, bs, cols * bs), bf16) for cols in (qc, 1)],
            [pltpu.VMEM((HALVES, everyone, nf, hb, bs), bf16) for _ in range(slots)],
            [pltpu.VMEM((nbb, nf, hb, bs), bf16) for _ in range(HALVES)],
            pltpu.VMEM((bs, nbb * bs), bf16),
            dma,
            dma((2,)),
            dma((6,)),
            dma((nf - 1, 4)),
            dma((nf - 1, 4)),
            dma((len(chunks),)),
            dma((len(chunks),)),
            dma((slots,)),
            dma((len(chunks),)),
            dma((2,)),
            dma((len(chunks), 2)),
            dma((slots, HALVES)),
            dma((HALVES,)),
            dma((nf,)),
            dma((nf,)),
            dma((nf,)),
            dma((nf,)),
        ],
        compiler_params=pltpu.CompilerParams(
            collective_id=0, has_side_effects=True, vmem_limit_bytes=61 * 1024 * 1024
        ),
    )(
        energy,
        vector,
        alpha_tiles.reshape(sc * bs, bs),
        beta_tiles.reshape(sc * bs, bs),
        alpha_pattern[0].T,
        beta_pattern[0].T,
        alpha_sector,
        beta_sector,
        alpha_diag.reshape(nab, bs),
        beta_diag.reshape(nbb, bs),
    )
    first_update, second_update = pl.pallas_call(
        hand_over,
        out_shape=(
            jax.ShapeDtypeStruct(first_update.shape, bf16),
            jax.ShapeDtypeStruct(second_update.shape, bf16),
        ),
        in_specs=[hbm] * 2,
        out_specs=(hbm, hbm),
        scratch_shapes=[
            pltpu.VMEM(first_update.shape, bf16),
            pltpu.VMEM(second_update.shape, bf16),
            dma((2, COPIES)),
            dma((2, COPIES)),
        ],
        compiler_params=pltpu.CompilerParams(vmem_limit_bytes=61 * 1024 * 1024),
    )(first_update, second_update)
    return first_update.reshape(nab * bs // nf, nbb * bs // n), second_update


def fits_split(*args):
    vector, alpha_tiles, _, _, _, alpha_sector, beta_sector = args[:7]
    n, nf = lax.axis_size("str"), lax.axis_size("fac")
    bs = alpha_tiles.shape[2]
    nab, nbb = alpha_sector.shape[0], beta_sector.shape[0]
    return (
        n % PLANES == 0
        and nf > 1
        and alpha_tiles.shape[0] == 1
        and bs % 128 == 0
        and nab == n * nf
        and nbb == 2 * n * nf
    )


def either_body(*args):
    return split_body(*args) if fits_split(*args) else body(*args)


def solution(mesh):
    return jax.shard_map(
        either_body,
        mesh=mesh,
        in_specs=(
            P("str", None),
            P("fac", None, None, None),
            P("fac", None, None),
            P("fac", None, None, None),
            P("fac", None, None),
            P(),
            P(),
            P(),
            P(),
            P(),
        ),
        out_specs=(P("fac", "str"), P("str", "fac")),
        check_vma=False,
    )
```

```python
import functools

import jax
import jax.numpy as jnp
from jax import lax
from jax.experimental import pallas as pl
from jax.experimental.pallas import tpu as pltpu
from jax.sharding import PartitionSpec as P

MESH = pl.DeviceIdType.MESH


def beta_apply(matrix, tile_set, pattern):
    height, width = matrix.shape
    slot_count, block_size = tile_set.shape[:2]
    stacked = tile_set.reshape(slot_count * block_size, block_size)

    def one(j, result):
        picked = jnp.concatenate(
            [
                lax.dynamic_slice_in_dim(matrix, pattern[j, s] * block_size, block_size, 1)
                for s in range(slot_count)
            ],
            axis=1,
        )
        image = jnp.dot(picked, stacked, preferred_element_type=jnp.float32)
        return lax.dynamic_update_slice_in_dim(result, image, j * block_size, 1)

    return lax.fori_loop(
        0, width // block_size, one, jnp.zeros((height, width), jnp.float32)
    )


def alpha_apply(matrix, tile_set, pattern):
    height, width = matrix.shape
    slot_count, block_size = tile_set.shape[:2]
    stacked = tile_set.transpose(1, 0, 2).reshape(block_size, slot_count * block_size)

    def one(i, result):
        picked = jnp.concatenate(
            [
                lax.dynamic_slice_in_dim(matrix, pattern[i, s] * block_size, block_size, 0)
                for s in range(slot_count)
            ],
            axis=0,
        )
        image = jnp.dot(stacked, picked, preferred_element_type=jnp.float32)
        return lax.dynamic_update_slice_in_dim(result, image, i * block_size, 0)

    return lax.fori_loop(
        0, height // block_size, one, jnp.zeros((height, width), jnp.float32)
    )


def precondition(
    sigma_part,
    row_start,
    col_start,
    block_size,
    alpha_sector,
    beta_sector,
    alpha_diag,
    beta_diag,
    energy,
):
    row_count, col_count = sigma_part.shape
    row_blocks = row_count // block_size
    col_blocks = col_count // block_size
    alpha_labels = lax.dynamic_slice_in_dim(alpha_sector, row_start // block_size, row_blocks)
    beta_labels = lax.dynamic_slice_in_dim(beta_sector, col_start // block_size, col_blocks)
    live_mask = (alpha_labels[:, None, None, None] == beta_labels[None, None, :, None]).astype(
        jnp.float32
    )
    masked = (
        sigma_part.reshape(row_blocks, block_size, col_blocks, block_size) * live_mask
    ).reshape(row_count, col_count)
    alpha_part = lax.dynamic_slice_in_dim(alpha_diag, row_start, row_count)
    beta_part = lax.dynamic_slice_in_dim(beta_diag, col_start, col_count)
    denominator = alpha_part[:, None] + beta_part[None, :] - energy[0]
    return (masked / denominator).astype(jnp.bfloat16)


def body(
    vector,
    alpha_tiles,
    alpha_pattern,
    beta_tiles,
    beta_pattern,
    alpha_sector,
    beta_sector,
    alpha_diag,
    beta_diag,
    energy,
):
    string_index = lax.axis_index("str")
    group_index = lax.axis_index("fac")
    string_count = lax.axis_size("str")
    block_size = alpha_tiles.shape[2]
    row_count = vector.shape[0]
    col_count = vector.shape[1] // string_count
    factor = 0
    image = beta_apply(vector, beta_tiles[factor], beta_pattern[factor]).astype(jnp.bfloat16)
    moved_one = lax.all_to_all(image, "str", split_axis=1, concat_axis=0, tiled=True)
    partial_value = alpha_apply(moved_one, alpha_tiles[factor], alpha_pattern[factor])
    share_rows = lax.psum_scatter(partial_value, "fac", scatter_dimension=0, tiled=True)
    first_update = precondition(
        share_rows,
        group_index * share_rows.shape[0],
        string_index * col_count,
        block_size,
        alpha_sector,
        beta_sector,
        alpha_diag,
        beta_diag,
        energy,
    )
    whole_first = lax.all_gather(first_update, "fac", axis=0, tiled=True)
    factor = 0
    back_image = alpha_apply(whole_first, alpha_tiles[factor], alpha_pattern[factor]).astype(
        jnp.bfloat16
    )
    returned_one = lax.all_to_all(back_image, "str", split_axis=0, concat_axis=1, tiled=True)
    partial_back = beta_apply(returned_one, beta_tiles[factor], beta_pattern[factor])
    share_cols = lax.psum_scatter(partial_back, "fac", scatter_dimension=1, tiled=True)
    second_update = precondition(
        share_cols,
        string_index * row_count,
        group_index * share_cols.shape[1],
        block_size,
        alpha_sector,
        beta_sector,
        alpha_diag,
        beta_diag,
        energy,
    )
    return (first_update, second_update)


PLANES = 4
HALVES = 4
WINDOW = 3


def row_chunks(bs):
    shares = (1, 1, 2, 1, 1, 1, 1)
    unit = bs // sum(shares)
    starts = [unit * sum(shares[:x]) for x in range(len(shares))]
    return [(start, unit * share) for start, share in zip(starts, shares)]


def exchange_kernel(
    sizes,
    energy,
    vec,
    ta_in,
    tb_in,
    pa_in,
    pb_in,
    sa_in,
    sb_in,
    ad_in,
    bd_in,
    out1,
    out2,
    held,
    far,
    ta_all,
    tb_all,
    tiles_row,
    tiles_turned,
    pa,
    pb,
    sa,
    sb,
    near_index,
    far_index,
    adiag,
    bdiag,
    send1,
    send_far,
    recv_near,
    recv_far,
    total,
    scale,
    scale_last,
    first,
    send2,
    recv2,
    staged,
    held_sem,
    early_sem,
    late_sem,
    give_send,
    give_recv,
    raw_send,
    raw_recv,
    send1_sem,
    far_sem,
    near_sem,
    far_recv,
    send2_sem,
    recv2_sem,
    o1_send,
    o1_recv,
    o2_send,
    o2_recv,
):
    n, nf, bs, sc, qc, nab, nbb = sizes
    slots = qc + 1
    me = lax.axis_index("str")
    c = lax.axis_index("fac")
    everyone = n * nf
    lanes = n // PLANES
    per = lanes * nf
    row_blocks = nab // n
    plane_blocks = lanes * row_blocks
    half_rows = nab // nf
    half_blocks = nbb // nf
    kb = sc * bs
    hb = bs // HALVES
    plane = me // lanes
    lane = lax.rem(me, lanes)
    side = plane // 2
    inner = lax.rem(plane, 2) != side
    more = jnp.logical_or(inner, c == 0)
    near = 2 * per
    near_count = 2 * per - 1
    bunch = 4 if per % 4 == 0 else 1
    own = 3 * per
    chunks = row_chunks(bs)

    def target(v):
        step = v // per
        u = lax.rem(v, per)
        high = lax.rem(side + 1 - step // 2, 2)
        low = lax.rem(lax.rem(plane, 2) + step + step // 2, 2)
        d = (2 * high + low) * lanes + lax.rem(lane + u // nf, lanes)
        return d, lax.rem(c + lax.rem(u, nf), nf)

    def partner(t):
        return t + t // own

    def column_of(d, f, q):
        if q < qc:
            return (d * nf + f) * qc + q
        mirror = (PLANES - 1 - d // lanes) * lanes + lax.rem(d, lanes)
        return (mirror * nf + f) * qc

    barrier = pltpu.get_barrier_semaphore()

    def block(index):
        return pl.ds(pl.multiple_of(index * bs, bs), bs)

    own_kb = pl.ds(pl.multiple_of(c * kb, kb), kb)
    early = [
        pltpu.make_async_copy(tb_in, tb_all.at[own_kb], early_sem.at[0]),
        pltpu.make_async_copy(pb_in, pb.at[c], early_sem.at[1]),
    ]
    late = [
        pltpu.make_async_copy(ta_in, ta_all.at[own_kb], late_sem.at[0]),
        pltpu.make_async_copy(ad_in, adiag, late_sem.at[1]),
        pltpu.make_async_copy(bd_in, bdiag, late_sem.at[2]),
        pltpu.make_async_copy(pa_in, pa.at[c], late_sem.at[3]),
        pltpu.make_async_copy(sa_in, sa, late_sem.at[4]),
        pltpu.make_async_copy(sb_in, sb, late_sem.at[5]),
    ]
    for copy in early:
        copy.start()

    def load(b, carry):
        pltpu.make_async_copy(vec.at[:, block(b)], held.at[b], held_sem).start()
        return carry

    lax.fori_loop(0, nbb, load, 0, unroll=8)

    def greet(t, carry):
        d, f = target(partner(t))
        pl.semaphore_signal(
            barrier, inc=1, device_id={"fac": f, "str": d}, device_id_type=MESH
        )
        return carry

    lax.fori_loop(0, everyone - 1, greet, 0)

    for copy in late:
        copy.start()

    def gives():
        for e in range(1, nf):
            f = lax.rem(c + e, nf)
            for x, (a, b) in enumerate(
                [
                    (tb_in, tb_all.at[own_kb]),
                    (ta_in, ta_all.at[own_kb]),
                    (pb_in, pb.at[c]),
                    (pa_in, pa.at[c]),
                ]
            ):
                yield pltpu.make_async_remote_copy(
                    src_ref=a,
                    dst_ref=b,
                    send_sem=give_send.at[e - 1, x],
                    recv_sem=give_recv.at[e - 1, x],
                    device_id={"fac": f, "str": me},
                    device_id_type=MESH,
                )

    def raw_copy(x):
        start, rows = chunks[x]
        return pltpu.make_async_remote_copy(
            src_ref=held.at[:, pl.ds(pl.multiple_of(c * bs + start, 16), rows)],
            dst_ref=far[x].at[:, lax.rem(plane, 2)],
            send_sem=raw_send.at[x],
            recv_sem=raw_recv.at[x],
            device_id={"fac": c, "str": (2 - side) * lanes + lane},
            device_id_type=MESH,
        )

    def column(ref, index):
        return jnp.transpose(jnp.broadcast_to(ref[pl.ds(index, 1), :], (bs, bs)))

    def alive(i, j):
        return jnp.where(sa[i] == sb[j], 1.0, 0.0).astype(jnp.float32)

    def near_images(q, targets):
        picked = []
        for v in targets:
            d, f = target(v)
            j = column_of(d, f, q)
            picked.append(jnp.concatenate([held[pb[c, s, j]] for s in range(sc)], axis=1))
        image = jnp.dot(
            jnp.concatenate(picked, axis=0),
            tb_all[own_kb, :],
            preferred_element_type=jnp.float32,
        ).astype(jnp.bfloat16)
        at = 0
        for v in targets:
            for x in range(row_blocks):
                send1[q][v - near, x] = image[at : at + bs]
                at += bs

    def first_copy(q, v, x, stay=False):
        src = send1[q].at[v - near, x]
        level = lax.rem(plane, 2) * nf + c
        dst = recv_near[q].at[(lane * row_blocks + x) * 2 * nf + level]
        if stay:
            return pltpu.make_async_copy(src, dst, near_sem.at[q])
        d, f = target(v)
        return pltpu.make_async_remote_copy(
            src_ref=src,
            dst_ref=dst,
            send_sem=send1_sem.at[q],
            recv_sem=near_sem.at[q],
            device_id={"fac": f, "str": d},
            device_id_type=MESH,
        )

    def bunch_of(base):
        return [base + u for u in range(bunch)]

    def first_copies(q, targets):
        for x in range(row_blocks):

            @pl.when(targets[0] == own)
            def _(x=x):
                first_copy(q, own, x, stay=True).start()

            @pl.when(targets[0] != own)
            def _(x=x):
                first_copy(q, targets[0], x).start()

            for v in targets[1:]:
                first_copy(q, v, x).start()

    pltpu.make_async_copy(held, held, held_sem).wait()
    for copy in early:
        copy.wait()
    pl.semaphore_wait(barrier, everyone - 1)
    raw_copy(0).start()
    for copy in gives():
        copy.start()

    for x in range(1, WINDOW):
        raw_copy(x).start()
    for q in range(qc):

        def step_one(g, carry, q=q):
            near_images(q, bunch_of(near + g * bunch))
            first_copies(q, bunch_of(near + g * bunch))
            return carry

        lax.fori_loop(0, 2 * per // bunch, step_one, 0)

    extra_base = jnp.where(inner, own, near)

    def step_extra(g, carry):
        near_images(qc, bunch_of(extra_base + g * bunch))
        first_copies(qc, bunch_of(extra_base + g * bunch))
        return carry

    lax.fori_loop(0, per // bunch, step_extra, 0)

    def outer_extras(base):
        return [base + nf * w + lax.rem(nf - c, nf) for w in range(lanes)]

    outer_base = jnp.where(inner, near, own)
    near_images(qc, outer_extras(outer_base))
    first_copies(qc, outer_extras(outer_base))

    for copy in late:
        copy.wait()
    for copy in gives():
        copy.wait()
    for x in range(nf * sc):
        tiles_row[:, x * bs : (x + 1) * bs] = ta_all[x * bs : (x + 1) * bs, :]

    width = nf * kb
    spot = lax.broadcasted_iota(jnp.int32, (width, width), 1)
    origin = jnp.zeros((width, width), jnp.int32)
    for start, rows in chunks:
        inside = spot - start * nf * sc
        source = inside // rows * bs + start + lax.rem(inside, rows)
        origin = jnp.where(inside >= 0, source, origin)
    turn = jnp.where(
        lax.broadcasted_iota(jnp.int32, (width, width), 0) == origin, 1.0, 0.0
    ).astype(jnp.bfloat16)
    tiles_turned[...] = jnp.dot(
        tiles_row[...], turn, preferred_element_type=jnp.float32
    ).astype(jnp.bfloat16)

    def scale_columns(q):
        j = column_of(me, c, q)

        def one(i, carry):
            denominator = column(adiag, i) + bdiag[pl.ds(j, 1), :] - energy[0]
            value = alive(i, j) / denominator
            if q < qc:
                scale[0][i, :, q * bs : (q + 1) * bs] = value
            else:
                scale[1][i] = value
            return carry

        lax.fori_loop(0, nab, one, 0)

    for q in range(qc):
        scale_columns(q)

    @pl.when(more)
    def _():
        scale_columns(qc)

    def far_images(x, targets, qs):
        rows = chunks[x][1]
        places = [target(v) for v in targets]
        for k in range(nf):
            picked = []
            for d, f in places:
                for q in qs:
                    j = column_of(d, f, q)
                    picked.append(
                        jnp.concatenate(
                            [far[x][pb[k, s, j]].reshape(2 * rows, bs) for s in range(sc)],
                            axis=1,
                        )
                    )
            image = jnp.dot(
                jnp.concatenate(picked, axis=0),
                tb_all[k * kb : (k + 1) * kb, :],
                preferred_element_type=jnp.float32,
            ).astype(jnp.bfloat16)
            at = 0
            for v in targets:
                for q in qs:
                    for z in range(2):
                        send_far[x][(v - near) * slots + q, z * nf + k] = image[
                            at : at + rows
                        ]
                        at += rows

    def far_copy(x, v, q, stay=False):
        src = send_far[x].at[(v - near) * slots + q]
        dst = recv_far[x][q].at[pl.ds((lane * row_blocks + c) * 2 * nf, 2 * nf)]
        if stay:
            return pltpu.make_async_copy(src, dst, far_recv.at[x, q])
        d, f = target(v)
        return pltpu.make_async_remote_copy(
            src_ref=src,
            dst_ref=dst,
            send_sem=far_sem.at[x],
            recv_sem=far_recv.at[x, q],
            device_id={"fac": f, "str": d},
            device_id_type=MESH,
        )

    def far_step(x):
        def step(g, carry):
            base = near + g * bunch
            far_images(x, bunch_of(base), tuple(range(qc)))
            for q in range(qc):

                @pl.when(base == own)
                def _(q=q):
                    far_copy(x, own, q, stay=True).start()

                @pl.when(base != own)
                def _(q=q):
                    far_copy(x, base, q).start()

                for u in range(1, bunch):
                    far_copy(x, base + u, q).start()
            return carry

        lax.fori_loop(0, 2 * per // bunch, step, 0)

    def far_single(x, q):
        def step(g, carry):
            base = near + g * per
            targets = [base + u for u in range(per)]
            far_images(x, targets, (q,))

            @pl.when(base == own)
            def _():
                far_copy(x, own, q, stay=True).start()

            @pl.when(base != own)
            def _():
                far_copy(x, base, q).start()

            for v in targets[1:]:
                far_copy(x, v, q).start()
            return carry

        lax.fori_loop(0, 2, step, 0)

    def far_extras(x):
        extras = outer_extras(near) + [own + u for u in range(per)]
        far_images(x, extras, (qc,))
        for v in extras:
            far_copy(x, v, qc, stay=isinstance(v, int) and v == own).start()

    last = len(chunks) - 1

    nothing = plane_blocks * 2 * nf
    for q in range(slots):
        recv_near[q][nothing] = jnp.zeros((bs, bs), jnp.bfloat16)
        for x, (_, rows) in enumerate(chunks):
            recv_far[x][q][nothing] = jnp.zeros((rows, bs), jnp.bfloat16)

    def number(i, carry):
        for k in range(nf):
            for s in range(sc):
                p = pa[k, s, i]
                level = lax.div(p, plane_blocks)
                place = (lax.rem(p, plane_blocks) * 2 + lax.rem(level, 2)) * nf + k
                here = lax.div(level, 2) == side
                near_index[k, s, i] = jnp.where(here, place, nothing)
                far_index[k, s, i] = jnp.where(here, nothing, place)
        return carry

    lax.fori_loop(0, nab, number, 0)

    def partial(x, i, cols):
        parts = []
        source, index = (recv_near, near_index) if x < 0 else (recv_far[x], far_index)
        for k in range(nf):
            for s in range(sc):
                at = index[k, s, i]
                parts.append(jnp.concatenate([source[q][at] for q in cols], axis=1))
        if x < 0:
            tiles = tiles_row[...]
        else:
            start, rows = chunks[x]
            tiles = tiles_turned[:, start * nf * sc : (start + rows) * nf * sc]
        return jnp.dot(
            tiles, jnp.concatenate(parts, axis=0), preferred_element_type=jnp.float32
        )

    pair = tuple(range(qc))

    def accumulate(x, cols):
        which = int(cols[0] == qc)
        full = cols if which else pair
        spots = slice((cols[0] - full[0]) * bs, (cols[-1] - full[0] + 1) * bs)

        def one(i, carry):
            value = partial(x, i, cols)
            if x != 0:
                value = value + total[which][i, :, spots]
            if x < last:
                total[which][i, :, spots] = value
            else:
                first[which][i, :, spots] = (value * scale[which][i, :, spots]).astype(
                    jnp.bfloat16
                )
            return carry

        lax.fori_loop(0, nab, one, 0, unroll=4)

    def landed(x, cols):
        for q in cols:
            source, sem = (recv_near, near_sem) if x < 0 else (recv_far[x], far_recv.at[x])
            some = source[q].at[pl.ds(0, nothing)]
            pltpu.make_async_copy(some, some, sem.at[q]).wait()

    schedule = [[(y - 2, w) for w in (0, 1)] for y in range(len(chunks))]
    schedule[:2] = [[], []]
    schedule[-3:] = [
        [(last - 4, 0), (-1, 0)],
        [(last - 3, 0), (last - 2, 0)],
        [(last - 1, 0)],
    ]
    later = (last - 4, -1, last - 3, last - 2, last - 1, last)

    for x in range(len(chunks)):

        @pl.when(inner)
        def _(x=x):
            pltpu.make_async_copy(far[x], far[x], raw_recv.at[x]).wait()

        raw_copy(x).wait_send()
        if x + WINDOW < len(chunks):
            raw_copy(x + WINDOW).start()

        @pl.when(inner)
        def _(x=x):
            if x < last:
                far_step(x)
            else:
                for q in reversed(range(qc)):
                    far_single(x, q)
            for y in [x] if x < last - 1 else [last - 1, last] if x == last else []:
                far_extras(y)

        for y, which in schedule[x]:
            if which == 0:
                landed(y, pair)
                accumulate(y, pair)
            else:

                @pl.when(more)
                def _(y=y):
                    landed(y, (qc,))
                    accumulate(y, (qc,))

    def second_copy(q, h, v, stay=False):
        src = send2[q].at[h, v]
        dst = recv2[h].at[column_of(me, c, q)]
        if stay:
            return pltpu.make_async_copy(src, dst, recv2_sem.at[h])
        d, f = target(v)
        return pltpu.make_async_remote_copy(
            src_ref=src,
            dst_ref=dst,
            send_sem=send2_sem.at[q, h],
            recv_sem=recv2_sem.at[h],
            device_id={"fac": f, "str": d},
            device_id_type=MESH,
        )

    def share_copy(e):
        f = lax.rem(c + e, nf)
        src = first[0].at[pl.ds(f * half_rows, half_rows)]
        dst = out1.at[:, :, pl.ds(pl.multiple_of(c * qc * bs, bs), qc * bs)]
        if e == 0:
            return pltpu.make_async_copy(src, dst, o1_send.at[e])
        return pltpu.make_async_remote_copy(
            src_ref=src,
            dst_ref=dst,
            send_sem=o1_send.at[e],
            recv_sem=o1_recv.at[e],
            device_id={"fac": f, "str": me},
            device_id_type=MESH,
        )

    def begin(q):
        return jnp.where(more, near, 0) if q == 0 else near if q == qc else 0

    def alpha_images(v, q):
        d, f = target(v)
        i = d * nf + f
        which, y = (1, 0) if q == qc else (0, q)
        for k in range(nf):
            picked = jnp.concatenate(
                [first[which][pa[k, s, i], :, y * bs : (y + 1) * bs] for s in range(sc)],
                axis=0,
            )
            image = jnp.dot(
                tiles_row[:, k * kb : (k + 1) * kb],
                picked,
                preferred_element_type=jnp.float32,
            ).astype(jnp.bfloat16)
            for h in range(HALVES):
                send2[q][h, v, k] = image[h * hb : (h + 1) * hb]

    def second_copies(q, h, base):
        @pl.when(base == own)
        def _():
            second_copy(q, h, own, stay=True).start()

        @pl.when(base != own)
        def _():
            second_copy(q, h, base).start()

        for u in range(1, bunch):
            second_copy(q, h, base + u).start()

    def images_out(q):
        def step_two(g, carry):
            base = g * bunch
            for u in range(bunch):
                alpha_images(base + u, q)
            second_copies(q, 0, base)
            return carry

        lax.fori_loop(begin(q) // bunch, everyone // bunch, step_two, 0)

    order = list(reversed(range(qc)))
    for q in order:
        landed(last, (q,))
        accumulate(last, (q,))
        images_out(q)
    for e in range(nf):
        share_copy(e).start()

    def send_rest(q, h):
        def rest(g, carry):
            second_copies(q, h, g * bunch)
            return carry

        lax.fori_loop(begin(q) // bunch, everyone // bunch, rest, 0)

    for q in order:
        send_rest(q, 1)

    @pl.when(more)
    def _():
        for y in later:
            landed(y, (qc,))
            accumulate(y, (qc,))
        images_out(qc)

    for h in range(1, HALVES):
        for q in order if h > 1 else []:
            send_rest(q, h)

        @pl.when(more)
        def _(h=h):
            send_rest(qc, h)

    mine = me * nf + c
    group = max(g for g in (1, 2, 4, 8, 16) if half_blocks % g == 0)
    pieces = half_blocks // group

    def scale_row(j, carry):
        denominator = column(adiag, mine) + bdiag[pl.ds(j, 1), :] - energy[0]
        scale_last[j] = alive(mine, j) / denominator
        return carry

    lax.fori_loop(0, nbb, scale_row, 0)

    def sigma_two(h, first_block):
        rows = []
        for g in range(group):
            parts = [
                recv2[h][pb[k, s, first_block + g], k] for k in range(nf) for s in range(sc)
            ]
            rows.append(jnp.concatenate(parts, axis=1))
        sigma = jnp.dot(
            jnp.concatenate(rows, axis=0), tb_all[...], preferred_element_type=jnp.float32
        )
        for g in range(group):
            j = first_block + g
            value = sigma[g * hb : (g + 1) * hb] * scale_last[j, h * hb : (h + 1) * hb]
            staged[h * hb : (h + 1) * hb, block(j)] = value.astype(jnp.bfloat16)

    def piece_copy(h, e, x):
        f = lax.rem(c + e, nf)
        src_start = pl.multiple_of((f * half_blocks + x * group) * bs, bs)
        dst_start = pl.multiple_of(x * group * bs, bs)
        src = staged.at[pl.ds(h * hb, hb), pl.ds(src_start, group * bs)]
        dst = out2.at[
            pl.ds(pl.multiple_of(c * bs + h * hb, hb), hb), pl.ds(dst_start, group * bs)
        ]
        if e == 0:
            return pltpu.make_async_copy(src, dst, o2_send.at[e])
        return pltpu.make_async_remote_copy(
            src_ref=src,
            dst_ref=dst,
            send_sem=o2_send.at[e],
            recv_sem=o2_recv.at[e],
            device_id={"fac": f, "str": me},
            device_id_type=MESH,
        )

    for h in range(HALVES):
        pltpu.make_async_copy(recv2[h], recv2[h], recv2_sem.at[h]).wait()
        for e in reversed(range(nf)):

            def finish(x, carry, e=e, h=h):
                sigma_two(h, lax.rem(c + e, nf) * half_blocks + x * group)
                piece_copy(h, e, x).start()
                return carry

            lax.fori_loop(0, pieces, finish, 0)

    def second_sent(q, h, count):
        sent = send2[q].at[h, pl.ds(0, count)]
        pltpu.make_async_copy(sent, sent, send2_sem.at[q, h]).wait()

    def near_sent(q, count):
        sent = send1[q].at[pl.ds(0, count)]
        pltpu.make_async_copy(sent, sent, send1_sem.at[q]).wait()

    for q in range(qc):
        near_sent(q, near_count)
    for e in range(nf):
        share_copy(e).wait()

    @pl.when(inner)
    def _():
        for x in range(len(chunks)):
            some = send_far[x].at[pl.ds(0, near_count * qc + per - 1 + lanes)]
            pltpu.make_async_copy(some, some, far_sem.at[x]).wait()

    @pl.when(more)
    def _():
        near_sent(qc, per + lanes - 1)
        for h in range(HALVES):
            for q in range(slots):
                second_sent(q, h, near_count if q in (0, qc) else everyone - 1)

    @pl.when(jnp.logical_not(more))
    def _():
        near_sent(qc, per + lanes)
        for h in range(HALVES):
            for q in range(qc):
                second_sent(q, h, everyone - 1)

    for e in range(nf):
        sent = staged.at[:, pl.ds(0, half_blocks * bs)]
        pltpu.make_async_copy(sent, sent, o2_send.at[e]).wait()
        if e > 0:
            pltpu.make_async_copy(sent, sent, o2_recv.at[e]).wait()


COPIES = 4


def hand_over(source1, source2, out1, out2, stage1, stage2, sems_in, sems_out):
    loads, stores = [], []
    for y, (source, stage, out) in enumerate(
        [(source1, stage1, out1), (source2, stage2, out2)]
    ):
        step = source.shape[0] // COPIES
        for x in range(COPIES):
            part = pl.ds(x * step, step)
            loads.append(
                pltpu.make_async_copy(source.at[part], stage.at[part], sems_in.at[y, x])
            )
            stores.append(
                pltpu.make_async_copy(stage.at[part], out.at[part], sems_out.at[y, x])
            )
    for load in loads:
        load.start()
    for load, store in zip(loads, stores):
        load.wait()
        store.start()
    for store in stores:
        store.wait()


def split_body(
    vector,
    alpha_tiles,
    alpha_pattern,
    beta_tiles,
    beta_pattern,
    alpha_sector,
    beta_sector,
    alpha_diag,
    beta_diag,
    energy,
):
    n = lax.axis_size("str")
    nf = lax.axis_size("fac")
    sc, bs = alpha_tiles.shape[1], alpha_tiles.shape[2]
    nab, nbb = alpha_sector.shape[0], beta_sector.shape[0]
    qc = nbb // (n * nf)
    slots = qc + 1
    rows = vector.shape[0]
    smem = pl.BlockSpec(memory_space=pltpu.SMEM)
    anywhere = pl.BlockSpec(memory_space=pl.ANY)
    hbm = pl.BlockSpec(memory_space=pltpu.HBM)
    bf16 = jnp.bfloat16
    everyone = n * nf
    row_blocks = nab // n
    near = everyone // 2
    hb = bs // HALVES
    chunks = row_chunks(bs)
    dma = pltpu.SemaphoreType.DMA
    first_update, second_update = pl.pallas_call(
        functools.partial(exchange_kernel, (n, nf, bs, sc, qc, nab, nbb)),
        out_shape=(
            jax.ShapeDtypeStruct((nab // nf, bs, nbb * bs // n), bf16),
            jax.ShapeDtypeStruct((rows, nbb * bs // nf), bf16),
        ),
        in_specs=[smem] + [hbm] * 9,
        out_specs=(anywhere, anywhere),
        scratch_shapes=[
            pltpu.VMEM((nbb, rows, bs), bf16),
            [pltpu.VMEM((nbb, 2, count, bs), bf16) for _, count in chunks],
            pltpu.VMEM((nf * sc * bs, bs), bf16),
            pltpu.VMEM((nf * sc * bs, bs), bf16),
            pltpu.VMEM((bs, nf * sc * bs), bf16),
            pltpu.VMEM((bs, nf * sc * bs), bf16),
            pltpu.SMEM((nf, sc, nab), jnp.int32),
            pltpu.SMEM((nf, sc, nbb), jnp.int32),
            pltpu.SMEM((nab,), jnp.int32),
            pltpu.SMEM((nbb,), jnp.int32),
            pltpu.SMEM((nf, sc, nab), jnp.int32),
            pltpu.SMEM((nf, sc, nab), jnp.int32),
            pltpu.VMEM((nab, bs), jnp.float32),
            pltpu.VMEM((nbb, bs), jnp.float32),
            [pltpu.VMEM((near, row_blocks, bs, bs), bf16) for _ in range(slots)],
            [pltpu.VMEM((near * slots, 2 * nf, count, bs), bf16) for _, count in chunks],
            [
                pltpu.VMEM((nab // PLANES * 2 * nf + 1, bs, bs), bf16)
                for _ in range(slots)
            ],
            [
                [
                    pltpu.VMEM((nab // PLANES * 2 * nf + 1, count, bs), bf16)
                    for _ in range(slots)
                ]
                for _, count in chunks
            ],
            [pltpu.VMEM((nab, bs, cols * bs), jnp.float32) for cols in (qc, 1)],
            [pltpu.VMEM((nab, bs, cols * bs), jnp.float32) for cols in (qc, 1)],
            pltpu.VMEM((nbb, bs, bs), jnp.float32),
            [pltpu.VMEM((nab, bs, cols * bs), bf16) for cols in (qc, 1)],
            [pltpu.VMEM((HALVES, everyone, nf, hb, bs), bf16) for _ in range(slots)],
            [pltpu.VMEM((nbb, nf, hb, bs), bf16) for _ in range(HALVES)],
            pltpu.VMEM((bs, nbb * bs), bf16),
            dma,
            dma((2,)),
            dma((6,)),
            dma((nf - 1, 4)),
            dma((nf - 1, 4)),
            dma((len(chunks),)),
            dma((len(chunks),)),
            dma((slots,)),
            dma((len(chunks),)),
            dma((slots,)),
            dma((len(chunks), slots)),
            dma((slots, HALVES)),
            dma((HALVES,)),
            dma((nf,)),
            dma((nf,)),
            dma((nf,)),
            dma((nf,)),
        ],
        compiler_params=pltpu.CompilerParams(
            collective_id=0, has_side_effects=True, vmem_limit_bytes=61 * 1024 * 1024
        ),
    )(
        energy,
        vector,
        alpha_tiles.reshape(sc * bs, bs),
        beta_tiles.reshape(sc * bs, bs),
        alpha_pattern[0].T,
        beta_pattern[0].T,
        alpha_sector,
        beta_sector,
        alpha_diag.reshape(nab, bs),
        beta_diag.reshape(nbb, bs),
    )
    first_update, second_update = pl.pallas_call(
        hand_over,
        out_shape=(
            jax.ShapeDtypeStruct(first_update.shape, bf16),
            jax.ShapeDtypeStruct(second_update.shape, bf16),
        ),
        in_specs=[hbm] * 2,
        out_specs=(hbm, hbm),
        scratch_shapes=[
            pltpu.VMEM(first_update.shape, bf16),
            pltpu.VMEM(second_update.shape, bf16),
            dma((2, COPIES)),
            dma((2, COPIES)),
        ],
        compiler_params=pltpu.CompilerParams(vmem_limit_bytes=61 * 1024 * 1024),
    )(first_update, second_update)
    return first_update.reshape(nab * bs // nf, nbb * bs // n), second_update


def fits_split(*args):
    vector, alpha_tiles, _, _, _, alpha_sector, beta_sector = args[:7]
    n, nf = lax.axis_size("str"), lax.axis_size("fac")
    bs = alpha_tiles.shape[2]
    nab, nbb = alpha_sector.shape[0], beta_sector.shape[0]
    return (
        n % PLANES == 0
        and nf > 1
        and alpha_tiles.shape[0] == 1
        and bs % 128 == 0
        and nab == n * nf
        and nbb == 2 * n * nf
    )


def either_body(*args):
    return split_body(*args) if fits_split(*args) else body(*args)


def solution(mesh):
    return jax.shard_map(
        either_body,
        mesh=mesh,
        in_specs=(
            P("str", None),
            P("fac", None, None, None),
            P("fac", None, None),
            P("fac", None, None, None),
            P("fac", None, None),
            P(),
            P(),
            P(),
            P(),
            P(),
        ),
        out_specs=(P("fac", "str"), P("str", "fac")),
        check_vma=False,
    )
```

```python
import functools

import jax
import jax.numpy as jnp
from jax import lax
from jax.experimental import pallas as pl
from jax.experimental.pallas import tpu as pltpu
from jax.sharding import PartitionSpec as P

MESH = pl.DeviceIdType.MESH


def beta_apply(matrix, tile_set, pattern):
    height, width = matrix.shape
    slot_count, block_size = tile_set.shape[:2]
    stacked = tile_set.reshape(slot_count * block_size, block_size)

    def one(j, result):
        picked = jnp.concatenate(
            [
                lax.dynamic_slice_in_dim(matrix, pattern[j, s] * block_size, block_size, 1)
                for s in range(slot_count)
            ],
            axis=1,
        )
        image = jnp.dot(picked, stacked, preferred_element_type=jnp.float32)
        return lax.dynamic_update_slice_in_dim(result, image, j * block_size, 1)

    return lax.fori_loop(
        0, width // block_size, one, jnp.zeros((height, width), jnp.float32)
    )


def alpha_apply(matrix, tile_set, pattern):
    height, width = matrix.shape
    slot_count, block_size = tile_set.shape[:2]
    stacked = tile_set.transpose(1, 0, 2).reshape(block_size, slot_count * block_size)

    def one(i, result):
        picked = jnp.concatenate(
            [
                lax.dynamic_slice_in_dim(matrix, pattern[i, s] * block_size, block_size, 0)
                for s in range(slot_count)
            ],
            axis=0,
        )
        image = jnp.dot(stacked, picked, preferred_element_type=jnp.float32)
        return lax.dynamic_update_slice_in_dim(result, image, i * block_size, 0)

    return lax.fori_loop(
        0, height // block_size, one, jnp.zeros((height, width), jnp.float32)
    )


def precondition(
    sigma_part,
    row_start,
    col_start,
    block_size,
    alpha_sector,
    beta_sector,
    alpha_diag,
    beta_diag,
    energy,
):
    row_count, col_count = sigma_part.shape
    row_blocks = row_count // block_size
    col_blocks = col_count // block_size
    alpha_labels = lax.dynamic_slice_in_dim(alpha_sector, row_start // block_size, row_blocks)
    beta_labels = lax.dynamic_slice_in_dim(beta_sector, col_start // block_size, col_blocks)
    live_mask = (alpha_labels[:, None, None, None] == beta_labels[None, None, :, None]).astype(
        jnp.float32
    )
    masked = (
        sigma_part.reshape(row_blocks, block_size, col_blocks, block_size) * live_mask
    ).reshape(row_count, col_count)
    alpha_part = lax.dynamic_slice_in_dim(alpha_diag, row_start, row_count)
    beta_part = lax.dynamic_slice_in_dim(beta_diag, col_start, col_count)
    denominator = alpha_part[:, None] + beta_part[None, :] - energy[0]
    return (masked / denominator).astype(jnp.bfloat16)


def body(
    vector,
    alpha_tiles,
    alpha_pattern,
    beta_tiles,
    beta_pattern,
    alpha_sector,
    beta_sector,
    alpha_diag,
    beta_diag,
    energy,
):
    string_index = lax.axis_index("str")
    group_index = lax.axis_index("fac")
    string_count = lax.axis_size("str")
    block_size = alpha_tiles.shape[2]
    row_count = vector.shape[0]
    col_count = vector.shape[1] // string_count
    factor = 0
    image = beta_apply(vector, beta_tiles[factor], beta_pattern[factor]).astype(jnp.bfloat16)
    moved_one = lax.all_to_all(image, "str", split_axis=1, concat_axis=0, tiled=True)
    partial_value = alpha_apply(moved_one, alpha_tiles[factor], alpha_pattern[factor])
    share_rows = lax.psum_scatter(partial_value, "fac", scatter_dimension=0, tiled=True)
    first_update = precondition(
        share_rows,
        group_index * share_rows.shape[0],
        string_index * col_count,
        block_size,
        alpha_sector,
        beta_sector,
        alpha_diag,
        beta_diag,
        energy,
    )
    whole_first = lax.all_gather(first_update, "fac", axis=0, tiled=True)
    factor = 0
    back_image = alpha_apply(whole_first, alpha_tiles[factor], alpha_pattern[factor]).astype(
        jnp.bfloat16
    )
    returned_one = lax.all_to_all(back_image, "str", split_axis=0, concat_axis=1, tiled=True)
    partial_back = beta_apply(returned_one, beta_tiles[factor], beta_pattern[factor])
    share_cols = lax.psum_scatter(partial_back, "fac", scatter_dimension=1, tiled=True)
    second_update = precondition(
        share_cols,
        string_index * row_count,
        group_index * share_cols.shape[1],
        block_size,
        alpha_sector,
        beta_sector,
        alpha_diag,
        beta_diag,
        energy,
    )
    return (first_update, second_update)


PLANES = 4
SHARES = (3, 2, 2, 1)
HALVES = len(SHARES)
WINDOW = 3


def row_chunks(bs, shares=(1, 1, 2, 1, 1, 1, 1)):
    unit = bs // sum(shares)
    starts = [unit * sum(shares[:x]) for x in range(len(shares))]
    return [(start, unit * share) for start, share in zip(starts, shares)]


def exchange_kernel(
    sizes,
    energy,
    vec,
    ta_in,
    tb_in,
    pa_in,
    pb_in,
    sa_in,
    sb_in,
    ad_in,
    bd_in,
    out1,
    out2,
    held,
    far,
    ta_all,
    tb_all,
    tiles_row,
    tiles_turned,
    pa,
    pb,
    sa,
    sb,
    near_index,
    far_index,
    adiag,
    bdiag,
    send1,
    send_far,
    recv_near,
    recv_far,
    total,
    scale,
    scale_last,
    first,
    send2,
    recv2,
    staged,
    held_sem,
    early_sem,
    late_sem,
    give_send,
    give_recv,
    raw_send,
    raw_recv,
    send1_sem,
    far_sem,
    near_sem,
    far_recv,
    send2_sem,
    recv2_sem,
    o1_send,
    o1_recv,
    o2_send,
    o2_recv,
):
    n, nf, bs, sc, qc, nab, nbb = sizes
    slots = qc + 1
    me = lax.axis_index("str")
    c = lax.axis_index("fac")
    everyone = n * nf
    lanes = n // PLANES
    per = lanes * nf
    row_blocks = nab // n
    plane_blocks = lanes * row_blocks
    half_rows = nab // nf
    half_blocks = nbb // nf
    kb = sc * bs
    parts = row_chunks(bs, SHARES)
    plane = me // lanes
    lane = lax.rem(me, lanes)
    side = plane // 2
    inner = lax.rem(plane, 2) != side
    more = jnp.logical_or(inner, c == 0)
    near = 2 * per
    near_count = 2 * per - 1
    bunch = 4 if per % 4 == 0 else 1
    own = 3 * per
    chunks = row_chunks(bs)

    def target(v):
        step = v // per
        u = lax.rem(v, per)
        high = lax.rem(side + 1 - step // 2, 2)
        low = lax.rem(lax.rem(plane, 2) + step + step // 2, 2)
        d = (2 * high + low) * lanes + lax.rem(lane + u // nf, lanes)
        return d, lax.rem(c + lax.rem(u, nf), nf)

    def partner(t):
        return t + t // own

    def column_of(d, f, q):
        if q < qc:
            return (d * nf + f) * qc + q
        mirror = (PLANES - 1 - d // lanes) * lanes + lax.rem(d, lanes)
        return (mirror * nf + f) * qc

    barrier = pltpu.get_barrier_semaphore()

    def block(index):
        return pl.ds(pl.multiple_of(index * bs, bs), bs)

    own_kb = pl.ds(pl.multiple_of(c * kb, kb), kb)
    early = [
        pltpu.make_async_copy(tb_in, tb_all.at[own_kb], early_sem.at[0]),
        pltpu.make_async_copy(pb_in, pb.at[c], early_sem.at[1]),
    ]
    late = [
        pltpu.make_async_copy(ta_in, ta_all.at[own_kb], late_sem.at[0]),
        pltpu.make_async_copy(ad_in, adiag, late_sem.at[1]),
        pltpu.make_async_copy(bd_in, bdiag, late_sem.at[2]),
        pltpu.make_async_copy(pa_in, pa.at[c], late_sem.at[3]),
        pltpu.make_async_copy(sa_in, sa, late_sem.at[4]),
        pltpu.make_async_copy(sb_in, sb, late_sem.at[5]),
    ]
    for copy in early:
        copy.start()

    def load(b, carry):
        pltpu.make_async_copy(vec.at[:, block(b)], held.at[b], held_sem).start()
        return carry

    lax.fori_loop(0, nbb, load, 0, unroll=8)

    def greet(t, carry):
        d, f = target(partner(t))
        pl.semaphore_signal(
            barrier, inc=1, device_id={"fac": f, "str": d}, device_id_type=MESH
        )
        return carry

    lax.fori_loop(0, everyone - 1, greet, 0)

    for copy in late:
        copy.start()

    def gives():
        for e in range(1, nf):
            f = lax.rem(c + e, nf)
            for x, (a, b) in enumerate(
                [
                    (tb_in, tb_all.at[own_kb]),
                    (ta_in, ta_all.at[own_kb]),
                    (pb_in, pb.at[c]),
                    (pa_in, pa.at[c]),
                ]
            ):
                yield pltpu.make_async_remote_copy(
                    src_ref=a,
                    dst_ref=b,
                    send_sem=give_send.at[e - 1, x],
                    recv_sem=give_recv.at[e - 1, x],
                    device_id={"fac": f, "str": me},
                    device_id_type=MESH,
                )

    def raw_copy(x):
        start, rows = chunks[x]
        return pltpu.make_async_remote_copy(
            src_ref=held.at[:, pl.ds(pl.multiple_of(c * bs + start, 16), rows)],
            dst_ref=far[x].at[:, lax.rem(plane, 2)],
            send_sem=raw_send.at[x],
            recv_sem=raw_recv.at[x],
            device_id={"fac": c, "str": (2 - side) * lanes + lane},
            device_id_type=MESH,
        )

    def column(ref, index):
        return jnp.transpose(jnp.broadcast_to(ref[pl.ds(index, 1), :], (bs, bs)))

    def alive(i, j):
        return jnp.where(sa[i] == sb[j], 1.0, 0.0).astype(jnp.float32)

    def near_images(q, targets):
        picked = []
        for v in targets:
            d, f = target(v)
            j = column_of(d, f, q)
            picked.append(jnp.concatenate([held[pb[c, s, j]] for s in range(sc)], axis=1))
        image = jnp.dot(
            jnp.concatenate(picked, axis=0),
            tb_all[own_kb, :],
            preferred_element_type=jnp.float32,
        ).astype(jnp.bfloat16)
        at = 0
        for v in targets:
            for x in range(row_blocks):
                send1[q][v - near, x] = image[at : at + bs]
                at += bs

    def first_copy(q, v, x, stay=False):
        src = send1[q].at[v - near, x]
        level = lax.rem(plane, 2) * nf + c
        dst = recv_near[q].at[(lane * row_blocks + x) * 2 * nf + level]
        if stay:
            return pltpu.make_async_copy(src, dst, near_sem.at[q])
        d, f = target(v)
        return pltpu.make_async_remote_copy(
            src_ref=src,
            dst_ref=dst,
            send_sem=send1_sem.at[q],
            recv_sem=near_sem.at[q],
            device_id={"fac": f, "str": d},
            device_id_type=MESH,
        )

    def bunch_of(base):
        return [base + u for u in range(bunch)]

    def first_copies(q, targets):
        for x in range(row_blocks):

            @pl.when(targets[0] == own)
            def _(x=x):
                first_copy(q, own, x, stay=True).start()

            @pl.when(targets[0] != own)
            def _(x=x):
                first_copy(q, targets[0], x).start()

            for v in targets[1:]:
                first_copy(q, v, x).start()

    pltpu.make_async_copy(held, held, held_sem).wait()
    for copy in early:
        copy.wait()
    pl.semaphore_wait(barrier, everyone - 1)
    raw_copy(0).start()
    for copy in gives():
        copy.start()

    for x in range(1, WINDOW):
        raw_copy(x).start()
    for q in range(qc):

        def step_one(g, carry, q=q):
            near_images(q, bunch_of(near + g * bunch))
            first_copies(q, bunch_of(near + g * bunch))
            return carry

        lax.fori_loop(0, 2 * per // bunch, step_one, 0)

    extra_base = jnp.where(inner, own, near)

    def step_extra(g, carry):
        near_images(qc, bunch_of(extra_base + g * bunch))
        first_copies(qc, bunch_of(extra_base + g * bunch))
        return carry

    lax.fori_loop(0, per // bunch, step_extra, 0)

    def outer_extras(base):
        return [base + nf * w + lax.rem(nf - c, nf) for w in range(lanes)]

    outer_base = jnp.where(inner, near, own)
    near_images(qc, outer_extras(outer_base))
    first_copies(qc, outer_extras(outer_base))

    for copy in late:
        copy.wait()
    for copy in gives():
        copy.wait()
    for x in range(nf * sc):
        tiles_row[:, x * bs : (x + 1) * bs] = ta_all[x * bs : (x + 1) * bs, :]

    width = nf * kb
    spot = lax.broadcasted_iota(jnp.int32, (width, width), 1)
    origin = jnp.zeros((width, width), jnp.int32)
    for start, rows in chunks:
        inside = spot - start * nf * sc
        source = inside // rows * bs + start + lax.rem(inside, rows)
        origin = jnp.where(inside >= 0, source, origin)
    turn = jnp.where(
        lax.broadcasted_iota(jnp.int32, (width, width), 0) == origin, 1.0, 0.0
    ).astype(jnp.bfloat16)
    tiles_turned[...] = jnp.dot(
        tiles_row[...], turn, preferred_element_type=jnp.float32
    ).astype(jnp.bfloat16)

    def scale_columns(q):
        j = column_of(me, c, q)

        def one(i, carry):
            denominator = column(adiag, i) + bdiag[pl.ds(j, 1), :] - energy[0]
            value = alive(i, j) / denominator
            if q < qc:
                scale[0][i, :, q * bs : (q + 1) * bs] = value
            else:
                scale[1][i] = value
            return carry

        lax.fori_loop(0, nab, one, 0)

    for q in range(qc):
        scale_columns(q)

    @pl.when(more)
    def _():
        scale_columns(qc)

    def far_images(x, targets, qs):
        rows = chunks[x][1]
        places = [target(v) for v in targets]
        for k in range(nf):
            picked = []
            for d, f in places:
                for q in qs:
                    j = column_of(d, f, q)
                    picked.append(
                        jnp.concatenate(
                            [far[x][pb[k, s, j]].reshape(2 * rows, bs) for s in range(sc)],
                            axis=1,
                        )
                    )
            image = jnp.dot(
                jnp.concatenate(picked, axis=0),
                tb_all[k * kb : (k + 1) * kb, :],
                preferred_element_type=jnp.float32,
            ).astype(jnp.bfloat16)
            at = 0
            for v in targets:
                for q in qs:
                    for z in range(2):
                        send_far[x][(v - near) * slots + q, z * nf + k] = image[
                            at : at + rows
                        ]
                        at += rows

    def far_copy(x, v, q, stay=False):
        src = send_far[x].at[(v - near) * slots + q]
        dst = recv_far[x][q].at[pl.ds((lane * row_blocks + c) * 2 * nf, 2 * nf)]
        if stay:
            return pltpu.make_async_copy(src, dst, far_recv.at[x, q])
        d, f = target(v)
        return pltpu.make_async_remote_copy(
            src_ref=src,
            dst_ref=dst,
            send_sem=far_sem.at[x],
            recv_sem=far_recv.at[x, q],
            device_id={"fac": f, "str": d},
            device_id_type=MESH,
        )

    def far_step(x):
        def step(g, carry):
            base = near + g * bunch
            far_images(x, bunch_of(base), tuple(range(qc)))
            for q in range(qc):

                @pl.when(base == own)
                def _(q=q):
                    far_copy(x, own, q, stay=True).start()

                @pl.when(base != own)
                def _(q=q):
                    far_copy(x, base, q).start()

                for u in range(1, bunch):
                    far_copy(x, base + u, q).start()
            return carry

        lax.fori_loop(0, 2 * per // bunch, step, 0)

    def far_single(x, q):
        def step(g, carry):
            base = near + g * per
            targets = [base + u for u in range(per)]
            far_images(x, targets, (q,))

            @pl.when(base == own)
            def _():
                far_copy(x, own, q, stay=True).start()

            @pl.when(base != own)
            def _():
                far_copy(x, base, q).start()

            for v in targets[1:]:
                far_copy(x, v, q).start()
            return carry

        lax.fori_loop(0, 2, step, 0)

    def far_extras(x):
        extras = outer_extras(near) + [own + u for u in range(per)]
        far_images(x, extras, (qc,))
        for v in extras:
            far_copy(x, v, qc, stay=isinstance(v, int) and v == own).start()

    last = len(chunks) - 1

    nothing = plane_blocks * 2 * nf
    for q in range(slots):
        recv_near[q][nothing] = jnp.zeros((bs, bs), jnp.bfloat16)
        for x, (_, rows) in enumerate(chunks):
            recv_far[x][q][nothing] = jnp.zeros((rows, bs), jnp.bfloat16)

    def number(i, carry):
        for k in range(nf):
            for s in range(sc):
                p = pa[k, s, i]
                level = lax.div(p, plane_blocks)
                place = (lax.rem(p, plane_blocks) * 2 + lax.rem(level, 2)) * nf + k
                here = lax.div(level, 2) == side
                near_index[k, s, i] = jnp.where(here, place, nothing)
                far_index[k, s, i] = jnp.where(here, nothing, place)
        return carry

    lax.fori_loop(0, nab, number, 0)

    def partial(x, i, cols):
        parts = []
        source, index = (recv_near, near_index) if x < 0 else (recv_far[x], far_index)
        for k in range(nf):
            for s in range(sc):
                at = index[k, s, i]
                parts.append(jnp.concatenate([source[q][at] for q in cols], axis=1))
        if x < 0:
            tiles = tiles_row[...]
        else:
            start, rows = chunks[x]
            tiles = tiles_turned[:, start * nf * sc : (start + rows) * nf * sc]
        return jnp.dot(
            tiles, jnp.concatenate(parts, axis=0), preferred_element_type=jnp.float32
        )

    pair = tuple(range(qc))

    def accumulate(x, cols):
        which = int(cols[0] == qc)
        full = cols if which else pair
        spots = slice((cols[0] - full[0]) * bs, (cols[-1] - full[0] + 1) * bs)

        def one(i, carry):
            value = partial(x, i, cols)
            if x != 0:
                value = value + total[which][i, :, spots]
            if x < last:
                total[which][i, :, spots] = value
            else:
                first[which][i, :, spots] = (value * scale[which][i, :, spots]).astype(
                    jnp.bfloat16
                )
            return carry

        lax.fori_loop(0, nab, one, 0, unroll=4)

    def landed(x, cols):
        for q in cols:
            source, sem = (recv_near, near_sem) if x < 0 else (recv_far[x], far_recv.at[x])
            some = source[q].at[pl.ds(0, nothing)]
            pltpu.make_async_copy(some, some, sem.at[q]).wait()

    schedule = [[(y - 2, w) for w in (0, 1)] for y in range(len(chunks))]
    schedule[:2] = [[], []]
    schedule[-3:] = [
        [(last - 4, 0), (-1, 0)],
        [(last - 3, 0), (last - 2, 0)],
        [(last - 1, 0)],
    ]
    later = (last - 4, -1, last - 3, last - 2, last - 1, last)

    for x in range(len(chunks)):

        @pl.when(inner)
        def _(x=x):
            pltpu.make_async_copy(far[x], far[x], raw_recv.at[x]).wait()

        raw_copy(x).wait_send()
        if x + WINDOW < len(chunks):
            raw_copy(x + WINDOW).start()

        @pl.when(inner)
        def _(x=x):
            if x < last:
                far_step(x)
            else:
                for q in reversed(range(qc)):
                    far_single(x, q)
            for y in [x] if x < last - 1 else [last - 1, last] if x == last else []:
                far_extras(y)

        for y, which in schedule[x]:
            if which == 0:
                landed(y, pair)
                accumulate(y, pair)
            else:

                @pl.when(more)
                def _(y=y):
                    landed(y, (qc,))
                    accumulate(y, (qc,))

    def second_copy(q, h, v, stay=False):
        src = send2[q][h].at[v]
        dst = recv2[h].at[column_of(me, c, q)]
        if stay:
            return pltpu.make_async_copy(src, dst, recv2_sem.at[h])
        d, f = target(v)
        return pltpu.make_async_remote_copy(
            src_ref=src,
            dst_ref=dst,
            send_sem=send2_sem.at[q, h],
            recv_sem=recv2_sem.at[h],
            device_id={"fac": f, "str": d},
            device_id_type=MESH,
        )

    def share_copy(e):
        f = lax.rem(c + e, nf)
        src = first[0].at[pl.ds(f * half_rows, half_rows)]
        dst = out1.at[:, :, pl.ds(pl.multiple_of(c * qc * bs, bs), qc * bs)]
        if e == 0:
            return pltpu.make_async_copy(src, dst, o1_send.at[e])
        return pltpu.make_async_remote_copy(
            src_ref=src,
            dst_ref=dst,
            send_sem=o1_send.at[e],
            recv_sem=o1_recv.at[e],
            device_id={"fac": f, "str": me},
            device_id_type=MESH,
        )

    def begin(q):
        return jnp.where(more, near, 0) if q == 0 else near if q == qc else 0

    def alpha_images(v, q):
        d, f = target(v)
        i = d * nf + f
        which, y = (1, 0) if q == qc else (0, q)
        for k in range(nf):
            picked = jnp.concatenate(
                [first[which][pa[k, s, i], :, y * bs : (y + 1) * bs] for s in range(sc)],
                axis=0,
            )
            image = jnp.dot(
                tiles_row[:, k * kb : (k + 1) * kb],
                picked,
                preferred_element_type=jnp.float32,
            ).astype(jnp.bfloat16)
            for h in range(HALVES):
                start, rows = parts[h]
                send2[q][h][v, k] = image[start : start + rows]

    def second_copies(q, h, base):
        @pl.when(base == own)
        def _():
            second_copy(q, h, own, stay=True).start()

        @pl.when(base != own)
        def _():
            second_copy(q, h, base).start()

        for u in range(1, bunch):
            second_copy(q, h, base + u).start()

    def images_out(q):
        def step_two(g, carry):
            base = g * bunch
            for u in range(bunch):
                alpha_images(base + u, q)
            second_copies(q, 0, base)
            return carry

        lax.fori_loop(begin(q) // bunch, everyone // bunch, step_two, 0)

    order = list(reversed(range(qc)))
    for q in order:
        landed(last, (q,))
        accumulate(last, (q,))
        images_out(q)
    for e in range(nf):
        share_copy(e).start()

    def send_rest(q, h):
        def rest(g, carry):
            second_copies(q, h, g * bunch)
            return carry

        lax.fori_loop(begin(q) // bunch, everyone // bunch, rest, 0)

    for q in order:
        send_rest(q, 1)

    @pl.when(more)
    def _():
        for y in later:
            landed(y, (qc,))
            accumulate(y, (qc,))
        images_out(qc)

    for h in range(1, HALVES):
        for q in order if h > 1 else []:
            send_rest(q, h)

        @pl.when(more)
        def _(h=h):
            send_rest(qc, h)

    mine = me * nf + c
    group = max(g for g in (1, 2, 4, 8, 16) if half_blocks % g == 0)
    pieces = half_blocks // group

    def scale_row(j, carry):
        denominator = column(adiag, mine) + bdiag[pl.ds(j, 1), :] - energy[0]
        scale_last[j] = alive(mine, j) / denominator
        return carry

    lax.fori_loop(0, nbb, scale_row, 0)

    def sigma_two(h, first_block):
        start, rows = parts[h]
        stack = []
        for g in range(group):
            picked = [
                recv2[h][pb[k, s, first_block + g], k] for k in range(nf) for s in range(sc)
            ]
            stack.append(jnp.concatenate(picked, axis=1))
        sigma = jnp.dot(
            jnp.concatenate(stack, axis=0), tb_all[...], preferred_element_type=jnp.float32
        )
        for g in range(group):
            j = first_block + g
            value = sigma[g * rows : (g + 1) * rows] * scale_last[j, start : start + rows]
            staged[start : start + rows, block(j)] = value.astype(jnp.bfloat16)

    def piece_copy(h, e, x):
        f = lax.rem(c + e, nf)
        src_start = pl.multiple_of((f * half_blocks + x * group) * bs, bs)
        dst_start = pl.multiple_of(x * group * bs, bs)
        start, rows = parts[h]
        src = staged.at[pl.ds(start, rows), pl.ds(src_start, group * bs)]
        dst = out2.at[
            pl.ds(pl.multiple_of(c * bs + start, 16), rows), pl.ds(dst_start, group * bs)
        ]
        if e == 0:
            return pltpu.make_async_copy(src, dst, o2_send.at[e])
        return pltpu.make_async_remote_copy(
            src_ref=src,
            dst_ref=dst,
            send_sem=o2_send.at[e],
            recv_sem=o2_recv.at[e],
            device_id={"fac": f, "str": me},
            device_id_type=MESH,
        )

    for h in range(HALVES):
        pltpu.make_async_copy(recv2[h], recv2[h], recv2_sem.at[h]).wait()
        for e in reversed(range(nf)):

            def finish(x, carry, e=e, h=h):
                sigma_two(h, lax.rem(c + e, nf) * half_blocks + x * group)
                piece_copy(h, e, x).start()
                return carry

            lax.fori_loop(0, pieces, finish, 0)

    def second_sent(q, h, count):
        sent = send2[q][h].at[pl.ds(0, count)]
        pltpu.make_async_copy(sent, sent, send2_sem.at[q, h]).wait()

    def near_sent(q, count):
        sent = send1[q].at[pl.ds(0, count)]
        pltpu.make_async_copy(sent, sent, send1_sem.at[q]).wait()

    for q in range(qc):
        near_sent(q, near_count)
    for e in range(nf):
        share_copy(e).wait()

    @pl.when(inner)
    def _():
        for x in range(len(chunks)):
            some = send_far[x].at[pl.ds(0, near_count * qc + per - 1 + lanes)]
            pltpu.make_async_copy(some, some, far_sem.at[x]).wait()

    @pl.when(more)
    def _():
        near_sent(qc, per + lanes - 1)
        for h in range(HALVES):
            for q in range(slots):
                second_sent(q, h, near_count if q in (0, qc) else everyone - 1)

    @pl.when(jnp.logical_not(more))
    def _():
        near_sent(qc, per + lanes)
        for h in range(HALVES):
            for q in range(qc):
                second_sent(q, h, everyone - 1)

    for e in range(nf):
        sent = staged.at[:, pl.ds(0, half_blocks * bs)]
        pltpu.make_async_copy(sent, sent, o2_send.at[e]).wait()
        if e > 0:
            pltpu.make_async_copy(sent, sent, o2_recv.at[e]).wait()


COPIES = 4


def hand_over(source1, source2, out1, out2, stage1, stage2, sems_in, sems_out):
    loads, stores = [], []
    for y, (source, stage, out) in enumerate(
        [(source1, stage1, out1), (source2, stage2, out2)]
    ):
        step = source.shape[0] // COPIES
        for x in range(COPIES):
            part = pl.ds(x * step, step)
            loads.append(
                pltpu.make_async_copy(source.at[part], stage.at[part], sems_in.at[y, x])
            )
            stores.append(
                pltpu.make_async_copy(stage.at[part], out.at[part], sems_out.at[y, x])
            )
    for load in loads:
        load.start()
    for load, store in zip(loads, stores):
        load.wait()
        store.start()
    for store in stores:
        store.wait()


def split_body(
    vector,
    alpha_tiles,
    alpha_pattern,
    beta_tiles,
    beta_pattern,
    alpha_sector,
    beta_sector,
    alpha_diag,
    beta_diag,
    energy,
):
    n = lax.axis_size("str")
    nf = lax.axis_size("fac")
    sc, bs = alpha_tiles.shape[1], alpha_tiles.shape[2]
    nab, nbb = alpha_sector.shape[0], beta_sector.shape[0]
    qc = nbb // (n * nf)
    slots = qc + 1
    rows = vector.shape[0]
    smem = pl.BlockSpec(memory_space=pltpu.SMEM)
    anywhere = pl.BlockSpec(memory_space=pl.ANY)
    hbm = pl.BlockSpec(memory_space=pltpu.HBM)
    bf16 = jnp.bfloat16
    everyone = n * nf
    row_blocks = nab // n
    near = everyone // 2
    parts = row_chunks(bs, SHARES)
    chunks = row_chunks(bs)
    dma = pltpu.SemaphoreType.DMA
    first_update, second_update = pl.pallas_call(
        functools.partial(exchange_kernel, (n, nf, bs, sc, qc, nab, nbb)),
        out_shape=(
            jax.ShapeDtypeStruct((nab // nf, bs, nbb * bs // n), bf16),
            jax.ShapeDtypeStruct((rows, nbb * bs // nf), bf16),
        ),
        in_specs=[smem] + [hbm] * 9,
        out_specs=(anywhere, anywhere),
        scratch_shapes=[
            pltpu.VMEM((nbb, rows, bs), bf16),
            [pltpu.VMEM((nbb, 2, count, bs), bf16) for _, count in chunks],
            pltpu.VMEM((nf * sc * bs, bs), bf16),
            pltpu.VMEM((nf * sc * bs, bs), bf16),
            pltpu.VMEM((bs, nf * sc * bs), bf16),
            pltpu.VMEM((bs, nf * sc * bs), bf16),
            pltpu.SMEM((nf, sc, nab), jnp.int32),
            pltpu.SMEM((nf, sc, nbb), jnp.int32),
            pltpu.SMEM((nab,), jnp.int32),
            pltpu.SMEM((nbb,), jnp.int32),
            pltpu.SMEM((nf, sc, nab), jnp.int32),
            pltpu.SMEM((nf, sc, nab), jnp.int32),
            pltpu.VMEM((nab, bs), jnp.float32),
            pltpu.VMEM((nbb, bs), jnp.float32),
            [pltpu.VMEM((near, row_blocks, bs, bs), bf16) for _ in range(slots)],
            [pltpu.VMEM((near * slots, 2 * nf, count, bs), bf16) for _, count in chunks],
            [
                pltpu.VMEM((nab // PLANES * 2 * nf + 1, bs, bs), bf16)
                for _ in range(slots)
            ],
            [
                [
                    pltpu.VMEM((nab // PLANES * 2 * nf + 1, count, bs), bf16)
                    for _ in range(slots)
                ]
                for _, count in chunks
            ],
            [pltpu.VMEM((nab, bs, cols * bs), jnp.float32) for cols in (qc, 1)],
            [pltpu.VMEM((nab, bs, cols * bs), jnp.float32) for cols in (qc, 1)],
            pltpu.VMEM((nbb, bs, bs), jnp.float32),
            [pltpu.VMEM((nab, bs, cols * bs), bf16) for cols in (qc, 1)],
            [
                [pltpu.VMEM((everyone, nf, count, bs), bf16) for _, count in parts]
                for _ in range(slots)
            ],
            [pltpu.VMEM((nbb, nf, count, bs), bf16) for _, count in parts],
            pltpu.VMEM((bs, nbb * bs), bf16),
            dma,
            dma((2,)),
            dma((6,)),
            dma((nf - 1, 4)),
            dma((nf - 1, 4)),
            dma((len(chunks),)),
            dma((len(chunks),)),
            dma((slots,)),
            dma((len(chunks),)),
            dma((slots,)),
            dma((len(chunks), slots)),
            dma((slots, HALVES)),
            dma((HALVES,)),
            dma((nf,)),
            dma((nf,)),
            dma((nf,)),
            dma((nf,)),
        ],
        compiler_params=pltpu.CompilerParams(
            collective_id=0, has_side_effects=True, vmem_limit_bytes=61 * 1024 * 1024
        ),
    )(
        energy,
        vector,
        alpha_tiles.reshape(sc * bs, bs),
        beta_tiles.reshape(sc * bs, bs),
        alpha_pattern[0].T,
        beta_pattern[0].T,
        alpha_sector,
        beta_sector,
        alpha_diag.reshape(nab, bs),
        beta_diag.reshape(nbb, bs),
    )
    first_update, second_update = pl.pallas_call(
        hand_over,
        out_shape=(
            jax.ShapeDtypeStruct(first_update.shape, bf16),
            jax.ShapeDtypeStruct(second_update.shape, bf16),
        ),
        in_specs=[hbm] * 2,
        out_specs=(hbm, hbm),
        scratch_shapes=[
            pltpu.VMEM(first_update.shape, bf16),
            pltpu.VMEM(second_update.shape, bf16),
            dma((2, COPIES)),
            dma((2, COPIES)),
        ],
        compiler_params=pltpu.CompilerParams(vmem_limit_bytes=61 * 1024 * 1024),
    )(first_update, second_update)
    return first_update.reshape(nab * bs // nf, nbb * bs // n), second_update


def fits_split(*args):
    vector, alpha_tiles, _, _, _, alpha_sector, beta_sector = args[:7]
    n, nf = lax.axis_size("str"), lax.axis_size("fac")
    bs = alpha_tiles.shape[2]
    nab, nbb = alpha_sector.shape[0], beta_sector.shape[0]
    return (
        n % PLANES == 0
        and nf > 1
        and alpha_tiles.shape[0] == 1
        and bs % 128 == 0
        and nab == n * nf
        and nbb == 2 * n * nf
    )


def either_body(*args):
    return split_body(*args) if fits_split(*args) else body(*args)


def solution(mesh):
    return jax.shard_map(
        either_body,
        mesh=mesh,
        in_specs=(
            P("str", None),
            P("fac", None, None, None),
            P("fac", None, None),
            P("fac", None, None, None),
            P("fac", None, None),
            P(),
            P(),
            P(),
            P(),
            P(),
        ),
        out_specs=(P("fac", "str"), P("str", "fac")),
        check_vma=False,
    )
```

```python
import functools

import jax
import jax.numpy as jnp
from jax import lax
from jax.experimental import pallas as pl
from jax.experimental.pallas import tpu as pltpu
from jax.sharding import PartitionSpec as P

MESH = pl.DeviceIdType.MESH


def beta_apply(matrix, tile_set, pattern):
    height, width = matrix.shape
    slot_count, block_size = tile_set.shape[:2]
    stacked = tile_set.reshape(slot_count * block_size, block_size)

    def one(j, result):
        picked = jnp.concatenate(
            [
                lax.dynamic_slice_in_dim(matrix, pattern[j, s] * block_size, block_size, 1)
                for s in range(slot_count)
            ],
            axis=1,
        )
        image = jnp.dot(picked, stacked, preferred_element_type=jnp.float32)
        return lax.dynamic_update_slice_in_dim(result, image, j * block_size, 1)

    return lax.fori_loop(
        0, width // block_size, one, jnp.zeros((height, width), jnp.float32)
    )


def alpha_apply(matrix, tile_set, pattern):
    height, width = matrix.shape
    slot_count, block_size = tile_set.shape[:2]
    stacked = tile_set.transpose(1, 0, 2).reshape(block_size, slot_count * block_size)

    def one(i, result):
        picked = jnp.concatenate(
            [
                lax.dynamic_slice_in_dim(matrix, pattern[i, s] * block_size, block_size, 0)
                for s in range(slot_count)
            ],
            axis=0,
        )
        image = jnp.dot(stacked, picked, preferred_element_type=jnp.float32)
        return lax.dynamic_update_slice_in_dim(result, image, i * block_size, 0)

    return lax.fori_loop(
        0, height // block_size, one, jnp.zeros((height, width), jnp.float32)
    )


def precondition(
    sigma_part,
    row_start,
    col_start,
    block_size,
    alpha_sector,
    beta_sector,
    alpha_diag,
    beta_diag,
    energy,
):
    row_count, col_count = sigma_part.shape
    row_blocks = row_count // block_size
    col_blocks = col_count // block_size
    alpha_labels = lax.dynamic_slice_in_dim(alpha_sector, row_start // block_size, row_blocks)
    beta_labels = lax.dynamic_slice_in_dim(beta_sector, col_start // block_size, col_blocks)
    live_mask = (alpha_labels[:, None, None, None] == beta_labels[None, None, :, None]).astype(
        jnp.float32
    )
    masked = (
        sigma_part.reshape(row_blocks, block_size, col_blocks, block_size) * live_mask
    ).reshape(row_count, col_count)
    alpha_part = lax.dynamic_slice_in_dim(alpha_diag, row_start, row_count)
    beta_part = lax.dynamic_slice_in_dim(beta_diag, col_start, col_count)
    denominator = alpha_part[:, None] + beta_part[None, :] - energy[0]
    return (masked / denominator).astype(jnp.bfloat16)


def body(
    vector,
    alpha_tiles,
    alpha_pattern,
    beta_tiles,
    beta_pattern,
    alpha_sector,
    beta_sector,
    alpha_diag,
    beta_diag,
    energy,
):
    string_index = lax.axis_index("str")
    group_index = lax.axis_index("fac")
    string_count = lax.axis_size("str")
    block_size = alpha_tiles.shape[2]
    row_count = vector.shape[0]
    col_count = vector.shape[1] // string_count
    factor = 0
    image = beta_apply(vector, beta_tiles[factor], beta_pattern[factor]).astype(jnp.bfloat16)
    moved_one = lax.all_to_all(image, "str", split_axis=1, concat_axis=0, tiled=True)
    partial_value = alpha_apply(moved_one, alpha_tiles[factor], alpha_pattern[factor])
    share_rows = lax.psum_scatter(partial_value, "fac", scatter_dimension=0, tiled=True)
    first_update = precondition(
        share_rows,
        group_index * share_rows.shape[0],
        string_index * col_count,
        block_size,
        alpha_sector,
        beta_sector,
        alpha_diag,
        beta_diag,
        energy,
    )
    whole_first = lax.all_gather(first_update, "fac", axis=0, tiled=True)
    factor = 0
    back_image = alpha_apply(whole_first, alpha_tiles[factor], alpha_pattern[factor]).astype(
        jnp.bfloat16
    )
    returned_one = lax.all_to_all(back_image, "str", split_axis=0, concat_axis=1, tiled=True)
    partial_back = beta_apply(returned_one, beta_tiles[factor], beta_pattern[factor])
    share_cols = lax.psum_scatter(partial_back, "fac", scatter_dimension=1, tiled=True)
    second_update = precondition(
        share_cols,
        string_index * row_count,
        group_index * share_cols.shape[1],
        block_size,
        alpha_sector,
        beta_sector,
        alpha_diag,
        beta_diag,
        energy,
    )
    return (first_update, second_update)


PLANES = 4
HALVES = 4
WINDOW = 4


def row_chunks(bs):
    shares = (1, 1, 2, 1, 1, 1, 1)
    unit = bs // sum(shares)
    starts = [unit * sum(shares[:x]) for x in range(len(shares))]
    return [(start, unit * share) for start, share in zip(starts, shares)]


def exchange_kernel(
    sizes,
    energy,
    vec,
    ta_in,
    tb_in,
    pa_in,
    pb_in,
    sa_in,
    sb_in,
    ad_in,
    bd_in,
    out1,
    out2,
    held,
    far,
    ta_all,
    tb_all,
    tiles_row,
    tiles_turned,
    pa,
    pb,
    sa,
    sb,
    near_index,
    far_index,
    adiag,
    bdiag,
    send1,
    send_far,
    recv_near,
    recv_far,
    total,
    scale,
    scale_last,
    first,
    send2,
    recv2,
    staged,
    held_sem,
    early_sem,
    late_sem,
    give_send,
    give_recv,
    raw_send,
    raw_recv,
    send1_sem,
    far_sem,
    near_sem,
    far_recv,
    send2_sem,
    recv2_sem,
    o1_send,
    o1_recv,
    o2_send,
    o2_recv,
):
    n, nf, bs, sc, qc, nab, nbb = sizes
    slots = qc + 1
    me = lax.axis_index("str")
    c = lax.axis_index("fac")
    everyone = n * nf
    lanes = n // PLANES
    per = lanes * nf
    row_blocks = nab // n
    plane_blocks = lanes * row_blocks
    half_rows = nab // nf
    half_blocks = nbb // nf
    kb = sc * bs
    hb = bs // HALVES
    plane = me // lanes
    lane = lax.rem(me, lanes)
    side = plane // 2
    inner = lax.rem(plane, 2) != side
    more = jnp.logical_or(inner, c == 0)
    near = 2 * per
    near_count = 2 * per - 1
    bunch = 4 if per % 4 == 0 else 1
    own = 3 * per
    chunks = row_chunks(bs)

    def target(v):
        step = v // per
        u = lax.rem(v, per)
        high = lax.rem(side + 1 - step // 2, 2)
        low = lax.rem(lax.rem(plane, 2) + step + step // 2, 2)
        d = (2 * high + low) * lanes + lax.rem(lane + u // nf, lanes)
        return d, lax.rem(c + lax.rem(u, nf), nf)

    def partner(t):
        return t + t // own

    def column_of(d, f, q):
        if q < qc:
            return (d * nf + f) * qc + q
        mirror = (PLANES - 1 - d // lanes) * lanes + lax.rem(d, lanes)
        return (mirror * nf + f) * qc

    barrier = pltpu.get_barrier_semaphore()

    def block(index):
        return pl.ds(pl.multiple_of(index * bs, bs), bs)

    own_kb = pl.ds(pl.multiple_of(c * kb, kb), kb)
    early = [
        pltpu.make_async_copy(tb_in, tb_all.at[own_kb], early_sem.at[0]),
        pltpu.make_async_copy(pb_in, pb.at[c], early_sem.at[1]),
    ]
    late = [
        pltpu.make_async_copy(ta_in, ta_all.at[own_kb], late_sem.at[0]),
        pltpu.make_async_copy(ad_in, adiag, late_sem.at[1]),
        pltpu.make_async_copy(bd_in, bdiag, late_sem.at[2]),
        pltpu.make_async_copy(pa_in, pa.at[c], late_sem.at[3]),
        pltpu.make_async_copy(sa_in, sa, late_sem.at[4]),
        pltpu.make_async_copy(sb_in, sb, late_sem.at[5]),
    ]
    for copy in early:
        copy.start()

    def load(b, carry):
        pltpu.make_async_copy(vec.at[:, block(b)], held.at[b], held_sem).start()
        return carry

    lax.fori_loop(0, nbb, load, 0, unroll=8)

    def greet(t, carry):
        d, f = target(partner(t))
        pl.semaphore_signal(
            barrier, inc=1, device_id={"fac": f, "str": d}, device_id_type=MESH
        )
        return carry

    lax.fori_loop(0, everyone - 1, greet, 0)

    for copy in late:
        copy.start()

    def gives():
        for e in range(1, nf):
            f = lax.rem(c + e, nf)
            for x, (a, b) in enumerate(
                [
                    (tb_in, tb_all.at[own_kb]),
                    (ta_in, ta_all.at[own_kb]),
                    (pb_in, pb.at[c]),
                    (pa_in, pa.at[c]),
                ]
            ):
                yield pltpu.make_async_remote_copy(
                    src_ref=a,
                    dst_ref=b,
                    send_sem=give_send.at[e - 1, x],
                    recv_sem=give_recv.at[e - 1, x],
                    device_id={"fac": f, "str": me},
                    device_id_type=MESH,
                )

    def raw_copy(x):
        start, rows = chunks[x]
        return pltpu.make_async_remote_copy(
            src_ref=held.at[:, pl.ds(pl.multiple_of(c * bs + start, 16), rows)],
            dst_ref=far[x].at[:, lax.rem(plane, 2)],
            send_sem=raw_send.at[x],
            recv_sem=raw_recv.at[x],
            device_id={"fac": c, "str": (2 - side) * lanes + lane},
            device_id_type=MESH,
        )

    def column(ref, index):
        return jnp.transpose(jnp.broadcast_to(ref[pl.ds(index, 1), :], (bs, bs)))

    def alive(i, j):
        return jnp.where(sa[i] == sb[j], 1.0, 0.0).astype(jnp.float32)

    def near_images(q, targets):
        picked = []
        for v in targets:
            d, f = target(v)
            j = column_of(d, f, q)
            picked.append(jnp.concatenate([held[pb[c, s, j]] for s in range(sc)], axis=1))
        image = jnp.dot(
            jnp.concatenate(picked, axis=0),
            tb_all[own_kb, :],
            preferred_element_type=jnp.float32,
        ).astype(jnp.bfloat16)
        at = 0
        for v in targets:
            for x in range(row_blocks):
                send1[q][v - near, x] = image[at : at + bs]
                at += bs

    def first_copy(q, v, x, stay=False):
        src = send1[q].at[v - near, x]
        level = lax.rem(plane, 2) * nf + c
        dst = recv_near[q].at[(lane * row_blocks + x) * 2 * nf + level]
        if stay:
            return pltpu.make_async_copy(src, dst, near_sem.at[q])
        d, f = target(v)
        return pltpu.make_async_remote_copy(
            src_ref=src,
            dst_ref=dst,
            send_sem=send1_sem.at[q],
            recv_sem=near_sem.at[q],
            device_id={"fac": f, "str": d},
            device_id_type=MESH,
        )

    def bunch_of(base):
        return [base + u for u in range(bunch)]

    def first_copies(q, targets):
        for x in range(row_blocks):

            @pl.when(targets[0] == own)
            def _(x=x):
                first_copy(q, own, x, stay=True).start()

            @pl.when(targets[0] != own)
            def _(x=x):
                first_copy(q, targets[0], x).start()

            for v in targets[1:]:
                first_copy(q, v, x).start()

    pltpu.make_async_copy(held, held, held_sem).wait()
    for copy in early:
        copy.wait()
    pl.semaphore_wait(barrier, everyone - 1)
    raw_copy(0).start()
    for copy in gives():
        copy.start()

    for x in range(1, WINDOW):
        raw_copy(x).start()
    for q in range(qc):

        def step_one(g, carry, q=q):
            near_images(q, bunch_of(near + g * bunch))
            first_copies(q, bunch_of(near + g * bunch))
            return carry

        lax.fori_loop(0, 2 * per // bunch, step_one, 0)

    extra_base = jnp.where(inner, own, near)

    def step_extra(g, carry):
        near_images(qc, bunch_of(extra_base + g * bunch))
        first_copies(qc, bunch_of(extra_base + g * bunch))
        return carry

    lax.fori_loop(0, per // bunch, step_extra, 0)

    def outer_extras(base):
        return [base + nf * w + lax.rem(nf - c, nf) for w in range(lanes)]

    outer_base = jnp.where(inner, near, own)
    near_images(qc, outer_extras(outer_base))
    first_copies(qc, outer_extras(outer_base))

    for copy in late:
        copy.wait()
    for copy in gives():
        copy.wait()
    for x in range(nf * sc):
        tiles_row[:, x * bs : (x + 1) * bs] = ta_all[x * bs : (x + 1) * bs, :]

    width = nf * kb
    spot = lax.broadcasted_iota(jnp.int32, (width, width), 1)
    origin = jnp.zeros((width, width), jnp.int32)
    for start, rows in chunks:
        inside = spot - start * nf * sc
        source = inside // rows * bs + start + lax.rem(inside, rows)
        origin = jnp.where(inside >= 0, source, origin)
    turn = jnp.where(
        lax.broadcasted_iota(jnp.int32, (width, width), 0) == origin, 1.0, 0.0
    ).astype(jnp.bfloat16)
    tiles_turned[...] = jnp.dot(
        tiles_row[...], turn, preferred_element_type=jnp.float32
    ).astype(jnp.bfloat16)

    def scale_columns(q):
        j = column_of(me, c, q)

        def one(i, carry):
            denominator = column(adiag, i) + bdiag[pl.ds(j, 1), :] - energy[0]
            value = alive(i, j) / denominator
            if q < qc:
                scale[0][i, :, q * bs : (q + 1) * bs] = value
            else:
                scale[1][i] = value
            return carry

        lax.fori_loop(0, nab, one, 0)

    for q in range(qc):
        scale_columns(q)

    @pl.when(more)
    def _():
        scale_columns(qc)

    def far_images(x, targets, qs):
        rows = chunks[x][1]
        places = [target(v) for v in targets]
        for k in range(nf):
            picked = []
            for d, f in places:
                for q in qs:
                    j = column_of(d, f, q)
                    picked.append(
                        jnp.concatenate(
                            [far[x][pb[k, s, j]].reshape(2 * rows, bs) for s in range(sc)],
                            axis=1,
                        )
                    )
            image = jnp.dot(
                jnp.concatenate(picked, axis=0),
                tb_all[k * kb : (k + 1) * kb, :],
                preferred_element_type=jnp.float32,
            ).astype(jnp.bfloat16)
            at = 0
            for v in targets:
                for q in qs:
                    for z in range(2):
                        send_far[x][(v - near) * slots + q, z * nf + k] = image[
                            at : at + rows
                        ]
                        at += rows

    def far_copy(x, v, q, stay=False):
        src = send_far[x].at[(v - near) * slots + q]
        dst = recv_far[x][q].at[pl.ds((lane * row_blocks + c) * 2 * nf, 2 * nf)]
        if stay:
            return pltpu.make_async_copy(src, dst, far_recv.at[x, q])
        d, f = target(v)
        return pltpu.make_async_remote_copy(
            src_ref=src,
            dst_ref=dst,
            send_sem=far_sem.at[x],
            recv_sem=far_recv.at[x, q],
            device_id={"fac": f, "str": d},
            device_id_type=MESH,
        )

    def far_step(x):
        def step(g, carry):
            base = near + g * bunch
            far_images(x, bunch_of(base), tuple(range(qc)))
            for q in range(qc):

                @pl.when(base == own)
                def _(q=q):
                    far_copy(x, own, q, stay=True).start()

                @pl.when(base != own)
                def _(q=q):
                    far_copy(x, base, q).start()

                for u in range(1, bunch):
                    far_copy(x, base + u, q).start()
            return carry

        lax.fori_loop(0, 2 * per // bunch, step, 0)

    def far_single(x, q):
        def step(g, carry):
            base = near + g * per
            targets = [base + u for u in range(per)]
            far_images(x, targets, (q,))

            @pl.when(base == own)
            def _():
                far_copy(x, own, q, stay=True).start()

            @pl.when(base != own)
            def _():
                far_copy(x, base, q).start()

            for v in targets[1:]:
                far_copy(x, v, q).start()
            return carry

        lax.fori_loop(0, 2, step, 0)

    def far_extras(x):
        extras = outer_extras(near) + [own + u for u in range(per)]
        far_images(x, extras, (qc,))
        for v in extras:
            far_copy(x, v, qc, stay=isinstance(v, int) and v == own).start()

    last = len(chunks) - 1

    nothing = plane_blocks * 2 * nf
    for q in range(slots):
        recv_near[q][nothing] = jnp.zeros((bs, bs), jnp.bfloat16)
        for x, (_, rows) in enumerate(chunks):
            recv_far[x][q][nothing] = jnp.zeros((rows, bs), jnp.bfloat16)

    def number(i, carry):
        for k in range(nf):
            for s in range(sc):
                p = pa[k, s, i]
                level = lax.div(p, plane_blocks)
                place = (lax.rem(p, plane_blocks) * 2 + lax.rem(level, 2)) * nf + k
                here = lax.div(level, 2) == side
                near_index[k, s, i] = jnp.where(here, place, nothing)
                far_index[k, s, i] = jnp.where(here, nothing, place)
        return carry

    lax.fori_loop(0, nab, number, 0)

    def partial(x, i, cols):
        parts = []
        source, index = (recv_near, near_index) if x < 0 else (recv_far[x], far_index)
        for k in range(nf):
            for s in range(sc):
                at = index[k, s, i]
                parts.append(jnp.concatenate([source[q][at] for q in cols], axis=1))
        if x < 0:
            tiles = tiles_row[...]
        else:
            start, rows = chunks[x]
            tiles = tiles_turned[:, start * nf * sc : (start + rows) * nf * sc]
        return jnp.dot(
            tiles, jnp.concatenate(parts, axis=0), preferred_element_type=jnp.float32
        )

    pair = tuple(range(qc))

    def accumulate(x, cols):
        which = int(cols[0] == qc)
        full = cols if which else pair
        spots = slice((cols[0] - full[0]) * bs, (cols[-1] - full[0] + 1) * bs)

        def one(i, carry):
            value = partial(x, i, cols)
            if x != 0:
                value = value + total[which][i, :, spots]
            if x < last:
                total[which][i, :, spots] = value
            else:
                first[which][i, :, spots] = (value * scale[which][i, :, spots]).astype(
                    jnp.bfloat16
                )
            return carry

        lax.fori_loop(0, nab, one, 0, unroll=4)

    def landed(x, cols):
        for q in cols:
            source, sem = (recv_near, near_sem) if x < 0 else (recv_far[x], far_recv.at[x])
            some = source[q].at[pl.ds(0, nothing)]
            pltpu.make_async_copy(some, some, sem.at[q]).wait()

    schedule = [[(y - 2, w) for w in (0, 1)] for y in range(len(chunks))]
    schedule[:2] = [[], []]
    schedule[-3:] = [
        [(last - 4, 0), (-1, 0)],
        [(last - 3, 0), (last - 2, 0)],
        [(last - 1, 0)],
    ]
    later = (last - 4, -1, last - 3, last - 2, last - 1, last)

    for x in range(len(chunks)):

        @pl.when(inner)
        def _(x=x):
            pltpu.make_async_copy(far[x], far[x], raw_recv.at[x]).wait()

        raw_copy(x).wait_send()
        if x + WINDOW < len(chunks):
            raw_copy(x + WINDOW).start()

        @pl.when(inner)
        def _(x=x):
            if x < last:
                far_step(x)
            else:
                for q in reversed(range(qc)):
                    far_single(x, q)
            for y in [x] if x < last - 1 else [last - 1, last] if x == last else []:
                far_extras(y)

        for y, which in schedule[x]:
            if which == 0:
                landed(y, pair)
                accumulate(y, pair)
            else:

                @pl.when(more)
                def _(y=y):
                    landed(y, (qc,))
                    accumulate(y, (qc,))

    def second_copy(q, h, v, stay=False):
        src = send2[q].at[h, v]
        dst = recv2[h].at[column_of(me, c, q)]
        if stay:
            return pltpu.make_async_copy(src, dst, recv2_sem.at[h])
        d, f = target(v)
        return pltpu.make_async_remote_copy(
            src_ref=src,
            dst_ref=dst,
            send_sem=send2_sem.at[q, h],
            recv_sem=recv2_sem.at[h],
            device_id={"fac": f, "str": d},
            device_id_type=MESH,
        )

    def share_copy(e):
        f = lax.rem(c + e, nf)
        src = first[0].at[pl.ds(f * half_rows, half_rows)]
        dst = out1.at[:, :, pl.ds(pl.multiple_of(c * qc * bs, bs), qc * bs)]
        if e == 0:
            return pltpu.make_async_copy(src, dst, o1_send.at[e])
        return pltpu.make_async_remote_copy(
            src_ref=src,
            dst_ref=dst,
            send_sem=o1_send.at[e],
            recv_sem=o1_recv.at[e],
            device_id={"fac": f, "str": me},
            device_id_type=MESH,
        )

    def begin(q):
        return jnp.where(more, near, 0) if q == 0 else near if q == qc else 0

    def alpha_images(v, q):
        d, f = target(v)
        i = d * nf + f
        which, y = (1, 0) if q == qc else (0, q)
        for k in range(nf):
            picked = jnp.concatenate(
                [first[which][pa[k, s, i], :, y * bs : (y + 1) * bs] for s in range(sc)],
                axis=0,
            )
            image = jnp.dot(
                tiles_row[:, k * kb : (k + 1) * kb],
                picked,
                preferred_element_type=jnp.float32,
            ).astype(jnp.bfloat16)
            for h in range(HALVES):
                send2[q][h, v, k] = image[h * hb : (h + 1) * hb]

    def second_copies(q, h, base):
        @pl.when(base == own)
        def _():
            second_copy(q, h, own, stay=True).start()

        @pl.when(base != own)
        def _():
            second_copy(q, h, base).start()

        for u in range(1, bunch):
            second_copy(q, h, base + u).start()

    def images_out(q):
        def step_two(g, carry):
            base = g * bunch
            for u in range(bunch):
                alpha_images(base + u, q)
            second_copies(q, 0, base)
            return carry

        lax.fori_loop(begin(q) // bunch, everyone // bunch, step_two, 0)

    order = list(reversed(range(qc)))
    for q in order:
        landed(last, (q,))
        accumulate(last, (q,))
        images_out(q)
    for e in range(nf):
        share_copy(e).start()

    def send_rest(q, h):
        def rest(g, carry):
            second_copies(q, h, g * bunch)
            return carry

        lax.fori_loop(begin(q) // bunch, everyone // bunch, rest, 0)

    for q in order:
        send_rest(q, 1)

    @pl.when(more)
    def _():
        for y in later:
            landed(y, (qc,))
            accumulate(y, (qc,))
        images_out(qc)

    for h in range(1, HALVES):
        for q in order if h > 1 else []:
            send_rest(q, h)

        @pl.when(more)
        def _(h=h):
            send_rest(qc, h)

    mine = me * nf + c
    group = max(g for g in (1, 2, 4, 8, 16) if half_blocks % g == 0)
    pieces = half_blocks // group

    def scale_row(j, carry):
        denominator = column(adiag, mine) + bdiag[pl.ds(j, 1), :] - energy[0]
        scale_last[j] = alive(mine, j) / denominator
        return carry

    lax.fori_loop(0, nbb, scale_row, 0)

    def sigma_two(h, first_block):
        rows = []
        for g in range(group):
            parts = [
                recv2[h][pb[k, s, first_block + g], k] for k in range(nf) for s in range(sc)
            ]
            rows.append(jnp.concatenate(parts, axis=1))
        sigma = jnp.dot(
            jnp.concatenate(rows, axis=0), tb_all[...], preferred_element_type=jnp.float32
        )
        for g in range(group):
            j = first_block + g
            value = sigma[g * hb : (g + 1) * hb] * scale_last[j, h * hb : (h + 1) * hb]
            staged[h * hb : (h + 1) * hb, block(j)] = value.astype(jnp.bfloat16)

    def piece_copy(h, e, x):
        f = lax.rem(c + e, nf)
        src_start = pl.multiple_of((f * half_blocks + x * group) * bs, bs)
        dst_start = pl.multiple_of(x * group * bs, bs)
        src = staged.at[pl.ds(h * hb, hb), pl.ds(src_start, group * bs)]
        dst = out2.at[
            pl.ds(pl.multiple_of(c * bs + h * hb, hb), hb), pl.ds(dst_start, group * bs)
        ]
        if e == 0:
            return pltpu.make_async_copy(src, dst, o2_send.at[e])
        return pltpu.make_async_remote_copy(
            src_ref=src,
            dst_ref=dst,
            send_sem=o2_send.at[e],
            recv_sem=o2_recv.at[e],
            device_id={"fac": f, "str": me},
            device_id_type=MESH,
        )

    for h in range(HALVES):
        pltpu.make_async_copy(recv2[h], recv2[h], recv2_sem.at[h]).wait()
        for e in reversed(range(nf)):

            def finish(x, carry, e=e, h=h):
                sigma_two(h, lax.rem(c + e, nf) * half_blocks + x * group)
                piece_copy(h, e, x).start()
                return carry

            lax.fori_loop(0, pieces, finish, 0)

    def second_sent(q, h, count):
        sent = send2[q].at[h, pl.ds(0, count)]
        pltpu.make_async_copy(sent, sent, send2_sem.at[q, h]).wait()

    def near_sent(q, count):
        sent = send1[q].at[pl.ds(0, count)]
        pltpu.make_async_copy(sent, sent, send1_sem.at[q]).wait()

    for q in range(qc):
        near_sent(q, near_count)
    for e in range(nf):
        share_copy(e).wait()

    @pl.when(inner)
    def _():
        for x in range(len(chunks)):
            some = send_far[x].at[pl.ds(0, near_count * qc + per - 1 + lanes)]
            pltpu.make_async_copy(some, some, far_sem.at[x]).wait()

    @pl.when(more)
    def _():
        near_sent(qc, per + lanes - 1)
        for h in range(HALVES):
            for q in range(slots):
                second_sent(q, h, near_count if q in (0, qc) else everyone - 1)

    @pl.when(jnp.logical_not(more))
    def _():
        near_sent(qc, per + lanes)
        for h in range(HALVES):
            for q in range(qc):
                second_sent(q, h, everyone - 1)

    for e in range(nf):
        sent = staged.at[:, pl.ds(0, half_blocks * bs)]
        pltpu.make_async_copy(sent, sent, o2_send.at[e]).wait()
        if e > 0:
            pltpu.make_async_copy(sent, sent, o2_recv.at[e]).wait()


COPIES = 4


def hand_over(source1, source2, out1, out2, stage1, stage2, sems_in, sems_out):
    loads, stores = [], []
    for y, (source, stage, out) in enumerate(
        [(source1, stage1, out1), (source2, stage2, out2)]
    ):
        step = source.shape[0] // COPIES
        for x in range(COPIES):
            part = pl.ds(x * step, step)
            loads.append(
                pltpu.make_async_copy(source.at[part], stage.at[part], sems_in.at[y, x])
            )
            stores.append(
                pltpu.make_async_copy(stage.at[part], out.at[part], sems_out.at[y, x])
            )
    for load in loads:
        load.start()
    for load, store in zip(loads, stores):
        load.wait()
        store.start()
    for store in stores:
        store.wait()


def split_body(
    vector,
    alpha_tiles,
    alpha_pattern,
    beta_tiles,
    beta_pattern,
    alpha_sector,
    beta_sector,
    alpha_diag,
    beta_diag,
    energy,
):
    n = lax.axis_size("str")
    nf = lax.axis_size("fac")
    sc, bs = alpha_tiles.shape[1], alpha_tiles.shape[2]
    nab, nbb = alpha_sector.shape[0], beta_sector.shape[0]
    qc = nbb // (n * nf)
    slots = qc + 1
    rows = vector.shape[0]
    smem = pl.BlockSpec(memory_space=pltpu.SMEM)
    anywhere = pl.BlockSpec(memory_space=pl.ANY)
    hbm = pl.BlockSpec(memory_space=pltpu.HBM)
    bf16 = jnp.bfloat16
    everyone = n * nf
    row_blocks = nab // n
    near = everyone // 2
    hb = bs // HALVES
    chunks = row_chunks(bs)
    dma = pltpu.SemaphoreType.DMA
    first_update, second_update = pl.pallas_call(
        functools.partial(exchange_kernel, (n, nf, bs, sc, qc, nab, nbb)),
        out_shape=(
            jax.ShapeDtypeStruct((nab // nf, bs, nbb * bs // n), bf16),
            jax.ShapeDtypeStruct((rows, nbb * bs // nf), bf16),
        ),
        in_specs=[smem] + [hbm] * 9,
        out_specs=(anywhere, anywhere),
        scratch_shapes=[
            pltpu.VMEM((nbb, rows, bs), bf16),
            [pltpu.VMEM((nbb, 2, count, bs), bf16) for _, count in chunks],
            pltpu.VMEM((nf * sc * bs, bs), bf16),
            pltpu.VMEM((nf * sc * bs, bs), bf16),
            pltpu.VMEM((bs, nf * sc * bs), bf16),
            pltpu.VMEM((bs, nf * sc * bs), bf16),
            pltpu.SMEM((nf, sc, nab), jnp.int32),
            pltpu.SMEM((nf, sc, nbb), jnp.int32),
            pltpu.SMEM((nab,), jnp.int32),
            pltpu.SMEM((nbb,), jnp.int32),
            pltpu.SMEM((nf, sc, nab), jnp.int32),
            pltpu.SMEM((nf, sc, nab), jnp.int32),
            pltpu.VMEM((nab, bs), jnp.float32),
            pltpu.VMEM((nbb, bs), jnp.float32),
            [pltpu.VMEM((near, row_blocks, bs, bs), bf16) for _ in range(slots)],
            [pltpu.VMEM((near * slots, 2 * nf, count, bs), bf16) for _, count in chunks],
            [
                pltpu.VMEM((nab // PLANES * 2 * nf + 1, bs, bs), bf16)
                for _ in range(slots)
            ],
            [
                [
                    pltpu.VMEM((nab // PLANES * 2 * nf + 1, count, bs), bf16)
                    for _ in range(slots)
                ]
                for _, count in chunks
            ],
            [pltpu.VMEM((nab, bs, cols * bs), jnp.float32) for cols in (qc, 1)],
            [pltpu.VMEM((nab, bs, cols * bs), jnp.float32) for cols in (qc, 1)],
            pltpu.VMEM((nbb, bs, bs), jnp.float32),
            [pltpu.VMEM((nab, bs, cols * bs), bf16) for cols in (qc, 1)],
            [pltpu.VMEM((HALVES, everyone, nf, hb, bs), bf16) for _ in range(slots)],
            [pltpu.VMEM((nbb, nf, hb, bs), bf16) for _ in range(HALVES)],
            pltpu.VMEM((bs, nbb * bs), bf16),
            dma,
            dma((2,)),
            dma((6,)),
            dma((nf - 1, 4)),
            dma((nf - 1, 4)),
            dma((len(chunks),)),
            dma((len(chunks),)),
            dma((slots,)),
            dma((len(chunks),)),
            dma((slots,)),
            dma((len(chunks), slots)),
            dma((slots, HALVES)),
            dma((HALVES,)),
            dma((nf,)),
            dma((nf,)),
            dma((nf,)),
            dma((nf,)),
        ],
        compiler_params=pltpu.CompilerParams(
            collective_id=0, has_side_effects=True, vmem_limit_bytes=61 * 1024 * 1024
        ),
    )(
        energy,
        vector,
        alpha_tiles.reshape(sc * bs, bs),
        beta_tiles.reshape(sc * bs, bs),
        alpha_pattern[0].T,
        beta_pattern[0].T,
        alpha_sector,
        beta_sector,
        alpha_diag.reshape(nab, bs),
        beta_diag.reshape(nbb, bs),
    )
    first_update, second_update = pl.pallas_call(
        hand_over,
        out_shape=(
            jax.ShapeDtypeStruct(first_update.shape, bf16),
            jax.ShapeDtypeStruct(second_update.shape, bf16),
        ),
        in_specs=[hbm] * 2,
        out_specs=(hbm, hbm),
        scratch_shapes=[
            pltpu.VMEM(first_update.shape, bf16),
            pltpu.VMEM(second_update.shape, bf16),
            dma((2, COPIES)),
            dma((2, COPIES)),
        ],
        compiler_params=pltpu.CompilerParams(vmem_limit_bytes=61 * 1024 * 1024),
    )(first_update, second_update)
    return first_update.reshape(nab * bs // nf, nbb * bs // n), second_update


def fits_split(*args):
    vector, alpha_tiles, _, _, _, alpha_sector, beta_sector = args[:7]
    n, nf = lax.axis_size("str"), lax.axis_size("fac")
    bs = alpha_tiles.shape[2]
    nab, nbb = alpha_sector.shape[0], beta_sector.shape[0]
    return (
        n % PLANES == 0
        and nf > 1
        and alpha_tiles.shape[0] == 1
        and bs % 128 == 0
        and nab == n * nf
        and nbb == 2 * n * nf
    )


def either_body(*args):
    return split_body(*args) if fits_split(*args) else body(*args)


def solution(mesh):
    return jax.shard_map(
        either_body,
        mesh=mesh,
        in_specs=(
            P("str", None),
            P("fac", None, None, None),
            P("fac", None, None),
            P("fac", None, None, None),
            P("fac", None, None),
            P(),
            P(),
            P(),
            P(),
            P(),
        ),
        out_specs=(P("fac", "str"), P("str", "fac")),
        check_vma=False,
    )
```
